256 devices in a mesh: grp: 16 (over z, core), ep: 16 (over y, x).
Axes of the slice: x: 4, y: 4, z: 8, core: 2. Of those that a mesh axis runs over, the one named last changes fastest.
Arguments:
- queries: bfloat16 [1024, 64, 576], P(('grp', 'ep')), may hold values from -75 to 75
- cache: bfloat16 [1024, 256, 576], P(('grp', 'ep')), may hold values from -6 to 6
- lengths: int32 [1024], P(('grp', 'ep')), may hold values from 2 to 256, as said below
- live_rows: int32 [256], P(('grp', 'ep')), may hold values from 1 to 4, as said below
- tokens: bfloat16 [4096, 3584], P(('grp', 'ep')), may hold values from -6 to 6
- ids: int32 [4096, 8], P(('grp', 'ep')), may hold values from 0 to 127, all different within a row; in each aligned block of 16 rows (0 to 15, 16 to 31, ...) at most 2 rows name the same one
- gates: float32 [4096, 8], P(('grp', 'ep')), may hold values from 0.1 to 1
- w_gate: bfloat16 [256, 3584, 512], P(('grp', 'ep')), may hold values from -0.09375 to 0.09375
- w_up: bfloat16 [256, 3584, 512], P(('grp', 'ep')), may hold values from -0.09375 to 0.09375
- w_down: bfloat16 [256, 512, 3584], P(('grp', 'ep')), may hold values from -0.1875 to 0.1875
Outputs:
- context: bfloat16 [1024, 64, 512], P(('grp', 'ep'))
- mixed: bfloat16 [4096, 3584], P(('grp', 'ep'))
The draws below stay inside these ranges and needn't reach their ends.
Inputs may be any that keep to these rules, and one draw needn't show every extreme that they name: `ids`: each row names 8 different experts; among the rows of one device no expert is named more than 2 times. `lengths`: the first request slot of every device holds 256 positions. `live_rows`: a device's live request slots are its first ones; on a quarter of the grp indices every device holds 2 or fewer, elsewhere exactly 4.
All inputs are finite; a program needn't handle non-finite values.
Results may differ from the reference program's by a relative error of at most 0.012.
Values may be sent and summed in bfloat16 or wider, within the bound.
A program may use at most 128 MiB of HBM per device.

```python
import math
import jax
import jax.numpy as jnp
import numpy as np
from jax import lax

D = 3584
HID = 1024
HALF = 512
TOPK = 8
EXPERTS = 128
H = 64
LAT = 512
ROPE = 64
CACHE = 256
RA = 4
ROWS = 16
CAP = 2
REQS = 1024
TOKENS = 4096
N_GRP = 16
N_EP = 16


def draw_queries(key, part):
    base = jnp.clip(jax.random.normal(jax.random.fold_in(key, 1), (REQS, H, LAT + ROPE), jnp.float32), -6.0, 6.0)
    return base.astype(jnp.bfloat16)


def draw_cache(key, part):
    base = jnp.clip(jax.random.normal(jax.random.fold_in(key, 2), (REQS, CACHE, LAT + ROPE), jnp.float32), -6.0, 6.0)
    return base.astype(jnp.bfloat16)


def draw_lengths(key, part):
    drawn = jax.random.randint(jax.random.fold_in(key, 3), (REQS,), 2, CACHE + 1)
    request = jnp.arange(REQS)
    return jnp.where(request % RA == 0, CACHE, drawn).astype(jnp.int32)


def draw_live_rows(key, part):
    device_count = N_GRP * N_EP
    group = jnp.arange(device_count) // N_EP
    order = jax.random.permutation(jax.random.fold_in(key, 4), N_GRP)
    capped = order[group] < N_GRP // 4
    lowered = jax.random.randint(jax.random.fold_in(key, 5), (device_count,), 1, RA // 2 + 1)
    return jnp.where(capped, lowered, RA).astype(jnp.int32)


def level_of(rng, dims, cuts, smallest, largest):
    gain = 1.0
    for axis_at, blocks in cuts:
        steps = jax.random.uniform(jax.random.fold_in(jax.random.fold_in(rng, 6), axis_at), (blocks,), jnp.float32, smallest / len(cuts), largest / len(cuts))
        gain = gain * jnp.repeat(jnp.exp(steps), dims[axis_at] // blocks).reshape((-1,) + (1,) * (len(dims) - 1 - axis_at))
    return gain


def deal_out(rng, own, number, rows, count, top, bound, skew):
    sequence = jax.random.permutation(rng, count)
    crowded, common = shares(count, rows * top, bound, skew, True), shares(count, rows * top, bound, skew, False)
    places = jnp.arange(count)

    def named(sizes, turn):
        used = int((sizes > 0).sum())
        fixed = max(1, used // 4)
        passed = fixed + (places - fixed + turn * (used - fixed)) % max(1, count - fixed)
        return jnp.zeros((count,), jnp.int32).at[sequence[jnp.where(places < fixed, places, passed)]].set(jnp.asarray(sizes, jnp.int32))

    sizes = jnp.where(number % 4 == 0, named(crowded, number // 4), named(common, number - number // 4 - 1))
    mixed = jax.random.permutation(jax.random.fold_in(own, 3), count)
    donor, sink = mixed[0:count // 2 * 2:2], mixed[1:count // 2 * 2:2]
    slack = jnp.minimum(sizes[donor] - 1, bound - sizes[sink]) // 2
    slack = jnp.where((donor == sequence[0]) | (sink == sequence[0]) | (sizes[sink] == 0), 0, jnp.maximum(slack, 0))
    passed = jax.random.randint(jax.random.fold_in(own, 4), (count // 2,), 0, 1 << 20) % (slack + 1)
    sizes = sizes.at[donor].add(-passed).at[sink].add(passed)
    items = jnp.searchsorted(jnp.cumsum(sizes), jnp.arange(rows * top), side="right").astype(jnp.int32)
    grid = items.reshape(top, rows).T
    grid = grid[jax.random.permutation(jax.random.fold_in(own, 1), rows)]
    turn = jax.random.randint(jax.random.fold_in(own, 2), (rows, 1), 0, top)
    return jnp.take_along_axis(grid, (jnp.arange(top)[None, :] + turn) % top, axis=1)


def shares(amount, total, most, lean, full):
    portions = [(1 << 20) // math.isqrt(rank ** lean) + 1 for rank in range(1, amount + 1)]
    largest = most if full else min(most, max(-(-total // amount), total * portions[0] // sum(portions)))
    least = 1 if total - largest >= amount - 1 else 0
    counts, surplus = [largest] + [least] * (amount - 1), total - largest - least * (amount - 1)
    while surplus > 0:
        candidates = [i for i in range(1, amount) if counts[i] < largest] or [i for i in range(1, amount) if counts[i] < most]
        whole, budget = sum([portions[i] for i in candidates]), surplus
        for i in candidates:
            extra = min(most - counts[i], max(1, budget * portions[i] // whole), surplus)
            counts[i] = counts[i] + extra
            surplus = surplus - extra
    return np.array(counts)


def bell_draw(key, dims, scale, reach, shards=(), kind=jnp.bfloat16):
    level = level_of(key, dims, shards, -0.22, 0.18) if shards else 1.0
    result = jax.random.normal(key, dims, jnp.float32) * scale * level
    return jnp.minimum(jnp.maximum(result, -reach), reach).astype(kind)


def setup_inputs(seed: int = 0) -> dict:
    keys = jax.random.split(jax.random.key(seed), 11)
    queries = draw_queries(jax.random.fold_in(keys[10], 71), 0)
    cache = draw_cache(jax.random.fold_in(keys[10], 71), 0)
    lengths = draw_lengths(jax.random.fold_in(keys[10], 71), 0)
    live_rows = draw_live_rows(jax.random.fold_in(keys[10], 71), 0)
    tokens = bell_draw(keys[4], (TOKENS, D), 1.0, 6.0, ((0, 256),))
    ids_keys = jax.random.split(jax.random.fold_in(keys[5], 1), TOKENS // ROWS)
    ids_turns = jax.random.permutation(jax.random.fold_in(keys[5], 3), TOKENS // ROWS)
    ids = jax.vmap(lambda own, number: deal_out(jax.random.fold_in(keys[5], 2), own, number, ROWS, EXPERTS, TOPK, CAP, 2))(ids_keys, ids_turns).reshape((TOKENS, TOPK))
    gates = jnp.clip(0.1 + 0.9 * jax.random.uniform(keys[6], (TOKENS, TOPK), jnp.float32) ** level_of(keys[6], (TOKENS, TOPK), ((0, 256),), -0.2, 0.2), 0.1, 1.0)
    w_gate = bell_draw(keys[7], (2 * EXPERTS, D, HALF), D ** -0.5, 0.09375, ((0, 256),))
    w_up = bell_draw(keys[8], (2 * EXPERTS, D, HALF), D ** -0.5, 0.09375, ((0, 256),))
    w_down = bell_draw(keys[9], (2 * EXPERTS, HALF, D), HID ** -0.5, 0.1875, ((0, 256),))
    return {"queries": queries, "cache": cache, "lengths": lengths, "live_rows": live_rows, "tokens": tokens, "ids": ids, "gates": gates, "w_gate": w_gate, "w_up": w_up, "w_down": w_down}


score_scale = 192.0 ** -0.5
neg_large = -1.0e30


def attend(queries, cache, lengths, live_mask):
    scores = jnp.einsum('rhc,rlc->rhl', queries.astype(jnp.float32), cache.astype(jnp.float32)) * score_scale
    positions = lax.broadcasted_iota(jnp.int32, scores.shape, 2)
    inside = positions < lengths[:, None, None]
    masked = jnp.where(inside, scores, neg_large)
    highest = jnp.max(masked, axis=2, keepdims=True)
    powers = jnp.where(inside, jnp.exp(masked - highest), 0.0)
    totals = jnp.sum(powers, axis=2, keepdims=True)
    weights = (powers / totals).astype(jnp.bfloat16)
    context = jnp.einsum('rhl,rlc->rhc', weights.astype(jnp.float32), cache[:, :, :LAT].astype(jnp.float32)).astype(jnp.bfloat16)
    return jnp.where(live_mask[:, None, None], context, jnp.zeros_like(context))


def reference(queries, cache, lengths, live_rows, tokens, ids, gates, w_gate, w_up, w_down):
    request_index = jnp.arange(REQS, dtype=jnp.int32)
    live_mask = (request_index % RA) < live_rows[request_index // RA]
    context = attend(queries, cache, lengths, live_mask)

    device_count = N_GRP * N_EP
    expert_count = EXPERTS
    chosen_ids = ids.reshape(device_count, ROWS * TOPK)
    onehot = (chosen_ids[:, :, None] == jnp.arange(expert_count, dtype=jnp.int32)[None, None, :]).astype(jnp.int32)
    earlier = jnp.cumsum(onehot, axis=1) - onehot
    slot_only = jnp.sum(earlier * onehot, axis=2)
    device_index = jnp.arange(device_count, dtype=jnp.int32)[:, None]
    slot_index = device_index * CAP + slot_only
    source_row = device_index * ROWS + (jnp.arange(ROWS * TOPK, dtype=jnp.int32) // TOPK)[None, :]
    table = jnp.full((expert_count, device_count * CAP), TOKENS, jnp.int32)
    table = table.at[chosen_ids, slot_index].set(source_row)
    padded = jnp.concatenate([tokens, jnp.zeros((1, D), tokens.dtype)], axis=0)
    gate_pairs = w_gate.reshape(expert_count, 2, D, HALF)
    up_pairs = w_up.reshape(expert_count, 2, D, HALF)
    down_pairs = w_down.reshape(expert_count, 2, HALF, D)

    def serve(item):
        table_row, gate_half, up_half, down_half = item
        gathered = padded[table_row]
        summed = jnp.zeros((gathered.shape[0], D), jnp.float32)
        for which_half in range(2):
            gate_part = jnp.dot(gathered, gate_half[which_half], preferred_element_type=jnp.float32)
            up_part = jnp.dot(gathered, up_half[which_half], preferred_element_type=jnp.float32)
            hidden = (jax.nn.silu(gate_part) * up_part).astype(jnp.bfloat16)
            summed = summed + jnp.dot(hidden, down_half[which_half], preferred_element_type=jnp.float32)
        return summed.astype(jnp.bfloat16)

    answers = lax.map(serve, (table, gate_pairs, up_pairs, down_pairs))
    picked = answers[chosen_ids, slot_index].reshape(TOKENS, TOPK, D)
    summed = jnp.zeros((TOKENS, D), jnp.float32)
    for which_pick in range(TOPK):
        summed = summed + gates[:, which_pick:which_pick + 1] * picked[:, which_pick, :].astype(jnp.float32)
    mixed = summed.astype(jnp.bfloat16)
    return (context, mixed)
```

```python
import jax
import jax.numpy as jnp
from jax import lax
from jax.sharding import PartitionSpec as P

TOPK = 8
LAT = 512
CAP = 2


score_scale = 192.0 ** (-0.5)
neg_large = -1e30


def attend(queries, cache, lengths, live_count):
    scores = (
        jnp.einsum("rhc,rlc->rhl", queries, cache, preferred_element_type=jnp.float32) * score_scale
    )
    positions = lax.broadcasted_iota(jnp.int32, scores.shape, 2)
    inside = positions < lengths[:, None, None]
    masked = jnp.where(inside, scores, neg_large)
    highest = jnp.max(masked, axis=2, keepdims=True)
    powers = jnp.where(inside, jnp.exp(masked - highest), 0.0)
    totals = jnp.sum(powers, axis=2, keepdims=True)
    weights = (powers / totals).astype(jnp.bfloat16)
    context = jnp.einsum(
        "rhl,rlc->rhc", weights, cache[:, :, :LAT], preferred_element_type=jnp.float32
    ).astype(jnp.bfloat16)
    request_slot = lax.broadcasted_iota(jnp.int32, context.shape, 0)
    return jnp.where(request_slot < live_count, context, jnp.zeros_like(context))


def expert_partial(flat_rows, w_gate, w_up, w_down):
    gate_part = jnp.dot(flat_rows, w_gate[0], preferred_element_type=jnp.float32)
    up_part = jnp.dot(flat_rows, w_up[0], preferred_element_type=jnp.float32)
    hidden = (jax.nn.silu(gate_part) * up_part).astype(jnp.bfloat16)
    return jnp.dot(hidden, w_down[0], preferred_element_type=jnp.float32)


def per_device(queries, cache, lengths, live_rows, tokens, ids, gates, w_gate, w_up, w_down):
    context = attend(queries, cache, lengths, live_rows[0])
    group_count = lax.axis_size("grp")
    peer_count = lax.axis_size("ep")
    pair_count = peer_count // 2
    row_count = tokens.shape[0]
    feature = tokens.shape[1]
    expert_slots = group_count * CAP
    slot_count = pair_count * expert_slots
    column_rows = group_count * row_count

    all_tokens = lax.all_gather(tokens, "grp", axis=0, tiled=True)
    all_ids = lax.all_gather(ids, "grp", axis=0, tiled=True)
    all_gates = lax.all_gather(gates, "grp", axis=0, tiled=True)

    my_group = lax.axis_index("grp")
    local = all_ids - pair_count * my_group
    experts = jnp.arange(pair_count, dtype=jnp.int32)
    pick_hot = (local[:, :, None] == experts[None, None, :]).astype(jnp.int32)
    token_hot = jnp.sum(pick_hot, axis=1)
    gate_of = jnp.sum(all_gates[:, :, None] * pick_hot.astype(jnp.float32), axis=1)
    blocks = token_hot.reshape(group_count, row_count, pair_count)
    earlier = (jnp.cumsum(blocks, axis=1) - blocks).reshape(column_rows, pair_count)
    source = jnp.arange(column_rows, dtype=jnp.int32)[:, None] // row_count
    slot_id = experts[None, :] * expert_slots + source * CAP + earlier
    slot_id = jnp.where(token_hot > 0, slot_id, slot_count)
    slots = jnp.arange(slot_count, dtype=jnp.int32)
    match = slot_id[:, :, None] == slots[None, None, :]
    dispatch = jnp.any(match, axis=1).T.astype(jnp.bfloat16)
    combine = jnp.sum(jnp.where(match, gate_of[:, :, None], 0.0), axis=1)

    outgoing = jnp.dot(dispatch, all_tokens, preferred_element_type=jnp.float32).astype(
        jnp.bfloat16
    )
    doubled = jnp.repeat(outgoing.reshape(pair_count, expert_slots, feature), 2, axis=0)
    arriving = lax.all_to_all(doubled, "ep", split_axis=0, concat_axis=0, tiled=True)
    partials = expert_partial(
        arriving.reshape(peer_count * expert_slots, feature), w_gate, w_up, w_down
    ).astype(jnp.bfloat16)
    returned = lax.all_to_all(
        partials.reshape(peer_count, expert_slots, feature),
        "ep",
        split_axis=0,
        concat_axis=0,
        tiled=True,
    )
    expert_out = (
        returned.reshape(pair_count, 2, expert_slots, feature)
        .astype(jnp.float32)
        .sum(axis=1)
        .astype(jnp.bfloat16)
        .reshape(slot_count, feature)
    )
    column_mixed = jnp.dot(
        combine,
        expert_out.astype(jnp.float32),
        precision=lax.Precision.HIGHEST,
        preferred_element_type=jnp.float32,
    )
    mixed = lax.psum_scatter(column_mixed, "grp", scatter_dimension=0, tiled=True)
    return (context, mixed.astype(jnp.bfloat16))


def solution(mesh):
    in_specs = (
        P(("grp", "ep"), None, None),
        P(("grp", "ep"), None, None),
        P(("grp", "ep")),
        P(("grp", "ep")),
        P(("grp", "ep"), None),
        P(("grp", "ep"), None),
        P(("grp", "ep"), None),
        P(("grp", "ep"), None, None),
        P(("grp", "ep"), None, None),
        P(("grp", "ep"), None, None),
    )
    out_specs = (P(("grp", "ep"), None, None), P(("grp", "ep"), None))
    return jax.shard_map(
        per_device, mesh=mesh, in_specs=in_specs, out_specs=out_specs, check_vma=False
    )
```

```python
import jax
import jax.numpy as jnp
from jax import lax
from jax.sharding import PartitionSpec as P

TOPK = 8
LAT = 512
CAP = 2


score_scale = 192.0 ** (-0.5)
neg_large = -1e30


def attend(queries, cache, lengths, live_count):
    scores = (
        jnp.einsum("rhc,rlc->rhl", queries, cache, preferred_element_type=jnp.float32) * score_scale
    )
    positions = lax.broadcasted_iota(jnp.int32, scores.shape, 2)
    inside = positions < lengths[:, None, None]
    masked = jnp.where(inside, scores, neg_large)
    highest = jnp.max(masked, axis=2, keepdims=True)
    powers = jnp.where(inside, jnp.exp(masked - highest), 0.0)
    totals = jnp.sum(powers, axis=2, keepdims=True)
    weights = (powers / totals).astype(jnp.bfloat16)
    context = jnp.einsum(
        "rhl,rlc->rhc", weights, cache[:, :, :LAT], preferred_element_type=jnp.float32
    ).astype(jnp.bfloat16)
    request_slot = lax.broadcasted_iota(jnp.int32, context.shape, 0)
    return jnp.where(request_slot < live_count, context, jnp.zeros_like(context))


def expert_partial(flat_rows, w_gate, w_up, w_down):
    gate_part = jnp.dot(flat_rows, w_gate[0], preferred_element_type=jnp.float32)
    up_part = jnp.dot(flat_rows, w_up[0], preferred_element_type=jnp.float32)
    hidden = (jax.nn.silu(gate_part) * up_part).astype(jnp.bfloat16)
    return jnp.dot(hidden, w_down[0], preferred_element_type=jnp.float32)


def per_device(queries, cache, lengths, live_rows, tokens, ids, gates, w_gate, w_up, w_down):
    context = attend(queries, cache, lengths, live_rows[0])
    group_count = lax.axis_size("grp")
    peer_count = lax.axis_size("ep")
    pair_count = peer_count // 2
    row_count = tokens.shape[0]
    feature = tokens.shape[1]
    expert_slots = group_count * CAP
    slot_count = pair_count * expert_slots
    column_rows = group_count * row_count

    gate_high = gates.astype(jnp.bfloat16)
    gate_low = (gates - gate_high.astype(jnp.float32)).astype(jnp.bfloat16)
    meta = jnp.concatenate([ids.astype(jnp.bfloat16), gate_high, gate_low], axis=1)
    meta = jnp.pad(meta, ((0, 0), (0, 128 - meta.shape[1])))
    packed = lax.all_gather(
        jnp.concatenate([tokens, meta], axis=1), "grp", axis=0, tiled=True
    )
    all_tokens = packed[:, :feature]
    all_ids = packed[:, feature : feature + TOPK].astype(jnp.int32)
    all_gates = packed[:, feature + TOPK : feature + 2 * TOPK].astype(jnp.float32) + packed[
        :, feature + 2 * TOPK : feature + 3 * TOPK
    ].astype(jnp.float32)

    my_group = lax.axis_index("grp")
    local = all_ids - pair_count * my_group
    experts = jnp.arange(pair_count, dtype=jnp.int32)
    pick_hot = (local[:, :, None] == experts[None, None, :]).astype(jnp.int32)
    token_hot = jnp.sum(pick_hot, axis=1)
    gate_of = jnp.sum(all_gates[:, :, None] * pick_hot.astype(jnp.float32), axis=1)
    blocks = token_hot.reshape(group_count, row_count, pair_count)
    earlier = (jnp.cumsum(blocks, axis=1) - blocks).reshape(column_rows, pair_count)
    source = jnp.arange(column_rows, dtype=jnp.int32)[:, None] // row_count
    slot_id = experts[None, :] * expert_slots + source * CAP + earlier
    slot_id = jnp.where(token_hot > 0, slot_id, slot_count)
    slots = jnp.arange(slot_count, dtype=jnp.int32)
    match = slot_id[:, :, None] == slots[None, None, :]
    dispatch = jnp.any(match, axis=1).T.astype(jnp.bfloat16)
    combine = jnp.sum(jnp.where(match, gate_of[:, :, None], 0.0), axis=1)

    outgoing = jnp.dot(dispatch, all_tokens, preferred_element_type=jnp.float32).astype(
        jnp.bfloat16
    )
    doubled = jnp.repeat(outgoing.reshape(pair_count, expert_slots, feature), 2, axis=0)
    arriving = lax.all_to_all(doubled, "ep", split_axis=0, concat_axis=0, tiled=True)
    partials = expert_partial(
        arriving.reshape(peer_count * expert_slots, feature), w_gate, w_up, w_down
    ).astype(jnp.bfloat16)
    returned = lax.all_to_all(
        partials.reshape(peer_count, expert_slots, feature),
        "ep",
        split_axis=0,
        concat_axis=0,
        tiled=True,
    )
    expert_out = (
        returned.reshape(pair_count, 2, expert_slots, feature)
        .astype(jnp.float32)
        .sum(axis=1)
        .astype(jnp.bfloat16)
        .reshape(slot_count, feature)
    )
    column_mixed = jnp.dot(
        combine,
        expert_out.astype(jnp.float32),
        precision=lax.Precision.HIGHEST,
        preferred_element_type=jnp.float32,
    )
    mixed = lax.psum_scatter(
        column_mixed.astype(jnp.bfloat16), "grp", scatter_dimension=0, tiled=True
    )
    return (context, mixed)


def solution(mesh):
    in_specs = (
        P(("grp", "ep"), None, None),
        P(("grp", "ep"), None, None),
        P(("grp", "ep")),
        P(("grp", "ep")),
        P(("grp", "ep"), None),
        P(("grp", "ep"), None),
        P(("grp", "ep"), None),
        P(("grp", "ep"), None, None),
        P(("grp", "ep"), None, None),
        P(("grp", "ep"), None, None),
    )
    out_specs = (P(("grp", "ep"), None, None), P(("grp", "ep"), None))
    return jax.shard_map(
        per_device, mesh=mesh, in_specs=in_specs, out_specs=out_specs, check_vma=False
    )
```

```python
import functools

import jax
import jax.numpy as jnp
from jax import lax
from jax.experimental import pallas as pl
from jax.experimental.pallas import tpu as pltpu
from jax.sharding import PartitionSpec as P

MESH = pl.DeviceIdType.MESH
TOPK = 8
LAT = 512
CAP = 2


score_scale = 192.0 ** (-0.5)
neg_large = -1e30


def attend(queries, cache, lengths, live_count):
    scores = (
        jnp.einsum("rhc,rlc->rhl", queries, cache, preferred_element_type=jnp.float32) * score_scale
    )
    positions = lax.broadcasted_iota(jnp.int32, scores.shape, 2)
    inside = positions < lengths[:, None, None]
    masked = jnp.where(inside, scores, neg_large)
    highest = jnp.max(masked, axis=2, keepdims=True)
    powers = jnp.where(inside, jnp.exp(masked - highest), 0.0)
    totals = jnp.sum(powers, axis=2, keepdims=True)
    weights = (powers / totals).astype(jnp.bfloat16)
    context = jnp.einsum(
        "rhl,rlc->rhc", weights, cache[:, :, :LAT], preferred_element_type=jnp.float32
    ).astype(jnp.bfloat16)
    request_slot = lax.broadcasted_iota(jnp.int32, context.shape, 0)
    return jnp.where(request_slot < live_count, context, jnp.zeros_like(context))


def gather_kernel(chips, x_ref, out_ref, send_sem, recv_sem):
    group = lax.axis_index("grp")
    peer_col = lax.axis_index("ep")
    z = group // 2
    core = group % 2
    right = lax.rem(z + 1, chips) * 2 + core
    left = lax.rem(z + chips - 1, chips) * 2 + core
    partner = z * 2 + (1 - core)

    barrier = pltpu.get_barrier_semaphore()
    for peer in (left, right, partner):
        pl.semaphore_signal(barrier, inc=1, device_id=(peer, peer_col), device_id_type=MESH)
    pl.semaphore_wait(barrier, 3)

    started = []

    def send(src, origin, peer):
        copy = pltpu.make_async_remote_copy(
            src_ref=src,
            dst_ref=out_ref.at[origin],
            send_sem=send_sem.at[len(started)],
            recv_sem=recv_sem.at[origin],
            device_id=(peer, peer_col),
            device_id_type=MESH,
        )
        copy.start()
        started.append(copy)

    def arrive(origin, peer):
        pltpu.make_async_remote_copy(
            src_ref=out_ref.at[origin],
            dst_ref=out_ref.at[origin],
            send_sem=send_sem.at[0],
            recv_sem=recv_sem.at[origin],
            device_id=(peer, peer_col),
            device_id_type=MESH,
        ).wait_recv()

    send(x_ref, group, right)
    send(x_ref, group, left)
    send(x_ref, group, partner)
    out_ref[group] = x_ref[...]
    forward_hops = chips // 2
    backward_hops = (chips - 1) // 2
    for step in range(1, forward_hops + 1):
        origin = lax.rem(z + chips - step, chips) * 2 + core
        arrive(origin, left)
        if step < forward_hops:
            send(out_ref.at[origin], origin, right)
        send(out_ref.at[origin], origin, partner)
        if step <= backward_hops:
            origin = lax.rem(z + step, chips) * 2 + core
            arrive(origin, right)
            if step < backward_hops:
                send(out_ref.at[origin], origin, left)
            send(out_ref.at[origin], origin, partner)
    for other in range(chips):
        arrive(other * 2 + (1 - core), partner)
    for copy in started:
        copy.wait_send()


def send_count(chips):
    forward_hops = chips // 2
    backward_hops = (chips - 1) // 2
    return 3 + 2 * forward_hops - 1 + 2 * backward_hops - 1


def ring_gather(block, group_count):
    chips = group_count // 2
    return pl.pallas_call(
        functools.partial(gather_kernel, chips),
        out_shape=jax.ShapeDtypeStruct((group_count,) + block.shape, block.dtype),
        in_specs=[pl.BlockSpec(memory_space=pltpu.VMEM)],
        out_specs=pl.BlockSpec(memory_space=pltpu.VMEM),
        scratch_shapes=[
            pltpu.SemaphoreType.DMA((send_count(chips),)),
            pltpu.SemaphoreType.DMA((group_count,)),
        ],
        compiler_params=pltpu.CompilerParams(collective_id=0, has_side_effects=True),
    )(block)


def expert_partial(flat_rows, w_gate, w_up, w_down):
    gate_part = jnp.dot(flat_rows, w_gate[0], preferred_element_type=jnp.float32)
    up_part = jnp.dot(flat_rows, w_up[0], preferred_element_type=jnp.float32)
    hidden = (jax.nn.silu(gate_part) * up_part).astype(jnp.bfloat16)
    return jnp.dot(hidden, w_down[0], preferred_element_type=jnp.float32)


def per_device(queries, cache, lengths, live_rows, tokens, ids, gates, w_gate, w_up, w_down):
    context = attend(queries, cache, lengths, live_rows[0])
    group_count = lax.axis_size("grp")
    peer_count = lax.axis_size("ep")
    pair_count = peer_count // 2
    row_count = tokens.shape[0]
    feature = tokens.shape[1]
    expert_slots = group_count * CAP
    slot_count = pair_count * expert_slots
    column_rows = group_count * row_count

    gate_high = gates.astype(jnp.bfloat16)
    gate_low = (gates - gate_high.astype(jnp.float32)).astype(jnp.bfloat16)
    meta = jnp.concatenate([ids.astype(jnp.bfloat16), gate_high, gate_low], axis=1)
    meta = jnp.pad(meta, ((0, 0), (0, 128 - meta.shape[1])))
    packed = ring_gather(jnp.concatenate([tokens, meta], axis=1), group_count).reshape(
        column_rows, feature + meta.shape[1]
    )
    all_tokens = packed[:, :feature]
    all_ids = packed[:, feature : feature + TOPK].astype(jnp.int32)
    all_gates = packed[:, feature + TOPK : feature + 2 * TOPK].astype(jnp.float32) + packed[
        :, feature + 2 * TOPK : feature + 3 * TOPK
    ].astype(jnp.float32)

    my_group = lax.axis_index("grp")
    local = all_ids - pair_count * my_group
    experts = jnp.arange(pair_count, dtype=jnp.int32)
    pick_hot = (local[:, :, None] == experts[None, None, :]).astype(jnp.int32)
    token_hot = jnp.sum(pick_hot, axis=1)
    gate_of = jnp.sum(all_gates[:, :, None] * pick_hot.astype(jnp.float32), axis=1)
    blocks = token_hot.reshape(group_count, row_count, pair_count)
    earlier = (jnp.cumsum(blocks, axis=1) - blocks).reshape(column_rows, pair_count)
    source = jnp.arange(column_rows, dtype=jnp.int32)[:, None] // row_count
    slot_id = experts[None, :] * expert_slots + source * CAP + earlier
    slot_id = jnp.where(token_hot > 0, slot_id, slot_count)
    slots = jnp.arange(slot_count, dtype=jnp.int32)
    match = slot_id[:, :, None] == slots[None, None, :]
    dispatch = jnp.any(match, axis=1).T.astype(jnp.bfloat16)
    combine = jnp.sum(jnp.where(match, gate_of[:, :, None], 0.0), axis=1)

    outgoing = jnp.dot(dispatch, all_tokens, preferred_element_type=jnp.float32).astype(
        jnp.bfloat16
    )
    doubled = jnp.repeat(outgoing.reshape(pair_count, expert_slots, feature), 2, axis=0)
    arriving = lax.all_to_all(doubled, "ep", split_axis=0, concat_axis=0, tiled=True)
    partials = expert_partial(
        arriving.reshape(peer_count * expert_slots, feature), w_gate, w_up, w_down
    ).astype(jnp.bfloat16)
    returned = lax.all_to_all(
        partials.reshape(peer_count, expert_slots, feature),
        "ep",
        split_axis=0,
        concat_axis=0,
        tiled=True,
    )
    expert_out = (
        returned.reshape(pair_count, 2, expert_slots, feature)
        .astype(jnp.float32)
        .sum(axis=1)
        .astype(jnp.bfloat16)
        .reshape(slot_count, feature)
    )
    column_mixed = jnp.dot(
        combine,
        expert_out.astype(jnp.float32),
        precision=lax.Precision.HIGHEST,
        preferred_element_type=jnp.float32,
    )
    mixed = lax.psum_scatter(
        column_mixed.astype(jnp.bfloat16), "grp", scatter_dimension=0, tiled=True
    )
    return (context, mixed)


def solution(mesh):
    in_specs = (
        P(("grp", "ep"), None, None),
        P(("grp", "ep"), None, None),
        P(("grp", "ep")),
        P(("grp", "ep")),
        P(("grp", "ep"), None),
        P(("grp", "ep"), None),
        P(("grp", "ep"), None),
        P(("grp", "ep"), None, None),
        P(("grp", "ep"), None, None),
        P(("grp", "ep"), None, None),
    )
    out_specs = (P(("grp", "ep"), None, None), P(("grp", "ep"), None))
    return jax.shard_map(
        per_device, mesh=mesh, in_specs=in_specs, out_specs=out_specs, check_vma=False
    )
```

```python
import functools

import jax
import jax.numpy as jnp
from jax import lax
from jax.experimental import pallas as pl
from jax.experimental.pallas import tpu as pltpu
from jax.sharding import PartitionSpec as P

MESH = pl.DeviceIdType.MESH
TOPK = 8
LAT = 512
CAP = 2


score_scale = 192.0 ** (-0.5)
neg_large = -1e30


def attend(queries, cache, lengths, live_count):
    scores = (
        jnp.einsum("rhc,rlc->rhl", queries, cache, preferred_element_type=jnp.float32) * score_scale
    )
    positions = lax.broadcasted_iota(jnp.int32, scores.shape, 2)
    inside = positions < lengths[:, None, None]
    masked = jnp.where(inside, scores, neg_large)
    highest = jnp.max(masked, axis=2, keepdims=True)
    powers = jnp.where(inside, jnp.exp(masked - highest), 0.0)
    totals = jnp.sum(powers, axis=2, keepdims=True)
    weights = (powers / totals).astype(jnp.bfloat16)
    context = jnp.einsum(
        "rhl,rlc->rhc", weights, cache[:, :, :LAT], preferred_element_type=jnp.float32
    ).astype(jnp.bfloat16)
    request_slot = lax.broadcasted_iota(jnp.int32, context.shape, 0)
    return jnp.where(request_slot < live_count, context, jnp.zeros_like(context))


def gather_kernel(chips, x_ref, out_ref, send_sem, recv_sem):
    group = lax.axis_index("grp")
    peer_col = lax.axis_index("ep")
    z = group // 2
    core = group % 2
    right = lax.rem(z + 1, chips) * 2 + core
    left = lax.rem(z + chips - 1, chips) * 2 + core
    partner = z * 2 + (1 - core)

    barrier = pltpu.get_barrier_semaphore()
    for peer in (left, right, partner):
        pl.semaphore_signal(barrier, inc=1, device_id=(peer, peer_col), device_id_type=MESH)
    pl.semaphore_wait(barrier, 3)

    started = []

    def send(src, origin, peer):
        copy = pltpu.make_async_remote_copy(
            src_ref=src,
            dst_ref=out_ref.at[origin],
            send_sem=send_sem.at[len(started)],
            recv_sem=recv_sem.at[origin],
            device_id=(peer, peer_col),
            device_id_type=MESH,
        )
        copy.start()
        started.append(copy)

    def arrive(origin, peer):
        pltpu.make_async_remote_copy(
            src_ref=out_ref.at[origin],
            dst_ref=out_ref.at[origin],
            send_sem=send_sem.at[0],
            recv_sem=recv_sem.at[origin],
            device_id=(peer, peer_col),
            device_id_type=MESH,
        ).wait_recv()

    send(x_ref, group, right)
    send(x_ref, group, left)
    send(x_ref, group, partner)
    out_ref[group] = x_ref[...]
    forward_hops = chips // 2
    backward_hops = (chips - 1) // 2
    for step in range(1, forward_hops + 1):
        origin = lax.rem(z + chips - step, chips) * 2 + core
        arrive(origin, left)
        if step < forward_hops:
            send(out_ref.at[origin], origin, right)
        send(out_ref.at[origin], origin, partner)
        if step <= backward_hops:
            origin = lax.rem(z + step, chips) * 2 + core
            arrive(origin, right)
            if step < backward_hops:
                send(out_ref.at[origin], origin, left)
            send(out_ref.at[origin], origin, partner)
    for other in range(chips):
        arrive(other * 2 + (1 - core), partner)
    for copy in started:
        copy.wait_send()


def send_count(chips):
    forward_hops = chips // 2
    backward_hops = (chips - 1) // 2
    return 3 + 2 * forward_hops - 1 + 2 * backward_hops - 1


def ring_gather(block, group_count):
    chips = group_count // 2
    return pl.pallas_call(
        functools.partial(gather_kernel, chips),
        out_shape=jax.ShapeDtypeStruct((group_count,) + block.shape, block.dtype),
        in_specs=[pl.BlockSpec(memory_space=pltpu.VMEM)],
        out_specs=pl.BlockSpec(memory_space=pltpu.VMEM),
        scratch_shapes=[
            pltpu.SemaphoreType.DMA((send_count(chips),)),
            pltpu.SemaphoreType.DMA((group_count,)),
        ],
        compiler_params=pltpu.CompilerParams(collective_id=0, has_side_effects=True),
    )(block)


def scatter_kernel(
    chips, parts_ref, out_ref, early, forward_in, backward_in, forward_out, backward_out,
    send_sem, recv_sem,
):
    group = lax.axis_index("grp")
    peer_col = lax.axis_index("ep")
    z = group // 2
    core = group % 2
    right = lax.rem(z + 1, chips) * 2 + core
    left = lax.rem(z + chips - 1, chips) * 2 + core
    partner = z * 2 + (1 - core)
    forward_hops = chips // 2
    backward_hops = (chips - 1) // 2

    barrier = pltpu.get_barrier_semaphore()
    for peer in (left, right, partner):
        pl.semaphore_signal(barrier, inc=1, device_id=(peer, peer_col), device_id_type=MESH)
    pl.semaphore_wait(barrier, 3)

    started = []

    def copy_of(src, dst, peer, slot, number):
        return pltpu.make_async_remote_copy(
            src_ref=src,
            dst_ref=dst,
            send_sem=send_sem.at[number],
            recv_sem=recv_sem.at[slot],
            device_id=(peer, peer_col),
            device_id_type=MESH,
        )

    def send(src, dst, peer, slot):
        copy = copy_of(src, dst, peer, slot, len(started))
        copy.start()
        started.append(copy)

    def arrive(dst, peer, slot):
        copy_of(dst, dst, peer, slot, 0).wait_recv()

    for other in range(chips):
        send(parts_ref.at[other * 2 + (1 - core)], early.at[other], partner, other)
    for other in range(chips):
        arrive(early.at[other], partner, other)

    def chip_part(chip):
        return parts_ref[chip * 2 + core].astype(jnp.float32) + early[chip].astype(jnp.float32)

    for step in range(forward_hops):
        chip = lax.rem(z + forward_hops - step, chips)
        value = chip_part(chip)
        if step > 0:
            arrive(forward_in.at[step - 1], left, chips + step - 1)
            value = value + forward_in[step - 1].astype(jnp.float32)
        forward_out[step] = value.astype(forward_out.dtype)
        send(forward_out.at[step], forward_in.at[step], right, chips + step)
        if step < backward_hops:
            chip = lax.rem(z + chips - backward_hops + step, chips)
            value = chip_part(chip)
            if step > 0:
                arrive(backward_in.at[step - 1], right, chips + forward_hops + step - 1)
                value = value + backward_in[step - 1].astype(jnp.float32)
            backward_out[step] = value.astype(backward_out.dtype)
            send(backward_out.at[step], backward_in.at[step], left, chips + forward_hops + step)
    arrive(forward_in.at[forward_hops - 1], left, chips + forward_hops - 1)
    total = chip_part(z) + forward_in[forward_hops - 1].astype(jnp.float32)
    if backward_hops > 0:
        arrive(backward_in.at[backward_hops - 1], right, chips + forward_hops + backward_hops - 1)
        total = total + backward_in[backward_hops - 1].astype(jnp.float32)
    out_ref[...] = total.astype(out_ref.dtype)
    for copy in started:
        copy.wait_send()


def ring_scatter(parts, group_count):
    chips = group_count // 2
    forward_hops = chips // 2
    backward_hops = (chips - 1) // 2
    block = parts.shape[1:]
    slots = chips + forward_hops + backward_hops
    return pl.pallas_call(
        functools.partial(scatter_kernel, chips),
        out_shape=jax.ShapeDtypeStruct(block, parts.dtype),
        in_specs=[pl.BlockSpec(memory_space=pltpu.VMEM)],
        out_specs=pl.BlockSpec(memory_space=pltpu.VMEM),
        scratch_shapes=[
            pltpu.VMEM((chips,) + block, parts.dtype),
            pltpu.VMEM((forward_hops,) + block, parts.dtype),
            pltpu.VMEM((max(backward_hops, 1),) + block, parts.dtype),
            pltpu.VMEM((forward_hops,) + block, parts.dtype),
            pltpu.VMEM((max(backward_hops, 1),) + block, parts.dtype),
            pltpu.SemaphoreType.DMA((slots,)),
            pltpu.SemaphoreType.DMA((slots,)),
        ],
        compiler_params=pltpu.CompilerParams(collective_id=1, has_side_effects=True),
    )(parts)


def expert_partial(flat_rows, w_gate, w_up, w_down):
    gate_part = jnp.dot(flat_rows, w_gate[0], preferred_element_type=jnp.float32)
    up_part = jnp.dot(flat_rows, w_up[0], preferred_element_type=jnp.float32)
    hidden = (jax.nn.silu(gate_part) * up_part).astype(jnp.bfloat16)
    return jnp.dot(hidden, w_down[0], preferred_element_type=jnp.float32)


def per_device(queries, cache, lengths, live_rows, tokens, ids, gates, w_gate, w_up, w_down):
    context = attend(queries, cache, lengths, live_rows[0])
    group_count = lax.axis_size("grp")
    peer_count = lax.axis_size("ep")
    pair_count = peer_count // 2
    row_count = tokens.shape[0]
    feature = tokens.shape[1]
    expert_slots = group_count * CAP
    slot_count = pair_count * expert_slots
    column_rows = group_count * row_count

    gate_high = gates.astype(jnp.bfloat16)
    gate_low = (gates - gate_high.astype(jnp.float32)).astype(jnp.bfloat16)
    meta = jnp.concatenate([ids.astype(jnp.bfloat16), gate_high, gate_low], axis=1)
    meta = jnp.pad(meta, ((0, 0), (0, 128 - meta.shape[1])))
    packed = ring_gather(jnp.concatenate([tokens, meta], axis=1), group_count).reshape(
        column_rows, feature + meta.shape[1]
    )
    all_tokens = packed[:, :feature]
    all_ids = packed[:, feature : feature + TOPK].astype(jnp.int32)
    all_gates = packed[:, feature + TOPK : feature + 2 * TOPK].astype(jnp.float32) + packed[
        :, feature + 2 * TOPK : feature + 3 * TOPK
    ].astype(jnp.float32)

    my_group = lax.axis_index("grp")
    local = all_ids - pair_count * my_group
    experts = jnp.arange(pair_count, dtype=jnp.int32)
    pick_hot = (local[:, :, None] == experts[None, None, :]).astype(jnp.int32)
    token_hot = jnp.sum(pick_hot, axis=1)
    gate_of = jnp.sum(all_gates[:, :, None] * pick_hot.astype(jnp.float32), axis=1)
    blocks = token_hot.reshape(group_count, row_count, pair_count)
    earlier = (jnp.cumsum(blocks, axis=1) - blocks).reshape(column_rows, pair_count)
    source = jnp.arange(column_rows, dtype=jnp.int32)[:, None] // row_count
    slot_id = experts[None, :] * expert_slots + source * CAP + earlier
    slot_id = jnp.where(token_hot > 0, slot_id, slot_count)
    slots = jnp.arange(slot_count, dtype=jnp.int32)
    match = slot_id[:, :, None] == slots[None, None, :]
    dispatch = jnp.any(match, axis=1).T.astype(jnp.bfloat16)
    combine = jnp.sum(jnp.where(match, gate_of[:, :, None], 0.0), axis=1)

    outgoing = jnp.dot(dispatch, all_tokens, preferred_element_type=jnp.float32).astype(
        jnp.bfloat16
    )
    doubled = jnp.repeat(outgoing.reshape(pair_count, expert_slots, feature), 2, axis=0)
    arriving = lax.all_to_all(doubled, "ep", split_axis=0, concat_axis=0, tiled=True)
    partials = expert_partial(
        arriving.reshape(peer_count * expert_slots, feature), w_gate, w_up, w_down
    ).astype(jnp.bfloat16)
    returned = lax.all_to_all(
        partials.reshape(peer_count, expert_slots, feature),
        "ep",
        split_axis=0,
        concat_axis=0,
        tiled=True,
    )
    expert_out = (
        returned.reshape(pair_count, 2, expert_slots, feature)
        .astype(jnp.float32)
        .sum(axis=1)
        .astype(jnp.bfloat16)
        .reshape(slot_count, feature)
    )
    column_mixed = jnp.dot(
        combine,
        expert_out.astype(jnp.float32),
        precision=lax.Precision.HIGHEST,
        preferred_element_type=jnp.float32,
    )
    mixed = ring_scatter(
        column_mixed.astype(jnp.bfloat16).reshape(group_count, row_count, feature), group_count
    )
    return (context, mixed)


def solution(mesh):
    in_specs = (
        P(("grp", "ep"), None, None),
        P(("grp", "ep"), None, None),
        P(("grp", "ep")),
        P(("grp", "ep")),
        P(("grp", "ep"), None),
        P(("grp", "ep"), None),
        P(("grp", "ep"), None),
        P(("grp", "ep"), None, None),
        P(("grp", "ep"), None, None),
        P(("grp", "ep"), None, None),
    )
    out_specs = (P(("grp", "ep"), None, None), P(("grp", "ep"), None))
    return jax.shard_map(
        per_device, mesh=mesh, in_specs=in_specs, out_specs=out_specs, check_vma=False
    )
```

```python
import functools

import jax
import jax.numpy as jnp
from jax import lax
from jax.experimental import pallas as pl
from jax.experimental.pallas import tpu as pltpu
from jax.sharding import PartitionSpec as P

MESH = pl.DeviceIdType.MESH
TOPK = 8
LAT = 512
CAP = 2


score_scale = 192.0 ** (-0.5)
neg_large = -1e30


def attend(queries, cache, lengths, live_count):
    scores = (
        jnp.einsum("rhc,rlc->rhl", queries, cache, preferred_element_type=jnp.float32) * score_scale
    )
    positions = lax.broadcasted_iota(jnp.int32, scores.shape, 2)
    inside = positions < lengths[:, None, None]
    masked = jnp.where(inside, scores, neg_large)
    highest = jnp.max(masked, axis=2, keepdims=True)
    powers = jnp.where(inside, jnp.exp(masked - highest), 0.0)
    totals = jnp.sum(powers, axis=2, keepdims=True)
    weights = (powers / totals).astype(jnp.bfloat16)
    context = jnp.einsum(
        "rhl,rlc->rhc", weights, cache[:, :, :LAT], preferred_element_type=jnp.float32
    ).astype(jnp.bfloat16)
    request_slot = lax.broadcasted_iota(jnp.int32, context.shape, 0)
    return jnp.where(request_slot < live_count, context, jnp.zeros_like(context))


def gather_kernel(chips, x_ref, out_ref, send_sem, recv_sem):
    group = lax.axis_index("grp")
    peer_col = lax.axis_index("ep")
    z = group // 2
    core = group % 2
    right = lax.rem(z + 1, chips) * 2 + core
    left = lax.rem(z + chips - 1, chips) * 2 + core
    partner = z * 2 + (1 - core)

    barrier = pltpu.get_barrier_semaphore()
    for peer in (left, right, partner):
        pl.semaphore_signal(barrier, inc=1, device_id=(peer, peer_col), device_id_type=MESH)
    pl.semaphore_wait(barrier, 3)

    started = []

    def send(src, origin, peer):
        copy = pltpu.make_async_remote_copy(
            src_ref=src,
            dst_ref=out_ref.at[origin],
            send_sem=send_sem.at[len(started)],
            recv_sem=recv_sem.at[origin],
            device_id=(peer, peer_col),
            device_id_type=MESH,
        )
        copy.start()
        started.append(copy)

    def arrive(origin, peer):
        pltpu.make_async_remote_copy(
            src_ref=out_ref.at[origin],
            dst_ref=out_ref.at[origin],
            send_sem=send_sem.at[0],
            recv_sem=recv_sem.at[origin],
            device_id=(peer, peer_col),
            device_id_type=MESH,
        ).wait_recv()

    send(x_ref, group, right)
    send(x_ref, group, left)
    send(x_ref, group, partner)
    out_ref[group] = x_ref[...]
    forward_hops = chips // 2
    backward_hops = (chips - 1) // 2
    for step in range(1, forward_hops + 1):
        origin = lax.rem(z + chips - step, chips) * 2 + core
        arrive(origin, left)
        if step < forward_hops:
            send(out_ref.at[origin], origin, right)
        send(out_ref.at[origin], origin, partner)
        if step <= backward_hops:
            origin = lax.rem(z + step, chips) * 2 + core
            arrive(origin, right)
            if step < backward_hops:
                send(out_ref.at[origin], origin, left)
            send(out_ref.at[origin], origin, partner)
    for other in range(chips):
        arrive(other * 2 + (1 - core), partner)
    for copy in started:
        copy.wait_send()


def send_count(chips):
    forward_hops = chips // 2
    backward_hops = (chips - 1) // 2
    return 3 + 2 * forward_hops - 1 + 2 * backward_hops - 1


def ring_gather(block, group_count):
    chips = group_count // 2
    return pl.pallas_call(
        functools.partial(gather_kernel, chips),
        out_shape=jax.ShapeDtypeStruct((group_count,) + block.shape, block.dtype),
        in_specs=[pl.BlockSpec(memory_space=pltpu.VMEM)],
        out_specs=pl.BlockSpec(memory_space=pltpu.VMEM),
        scratch_shapes=[
            pltpu.SemaphoreType.DMA((send_count(chips),)),
            pltpu.SemaphoreType.DMA((group_count,)),
        ],
        compiler_params=pltpu.CompilerParams(collective_id=0, has_side_effects=True),
    )(block)


def scatter_kernel(
    chips, parts_ref, out_ref, early, forward_in, backward_in, forward_out, backward_out,
    send_sem, recv_sem,
):
    group = lax.axis_index("grp")
    peer_col = lax.axis_index("ep")
    z = group // 2
    core = group % 2
    right = lax.rem(z + 1, chips) * 2 + core
    left = lax.rem(z + chips - 1, chips) * 2 + core
    partner = z * 2 + (1 - core)
    forward_hops = chips // 2
    backward_hops = (chips - 1) // 2

    barrier = pltpu.get_barrier_semaphore()
    for peer in (left, right, partner):
        pl.semaphore_signal(barrier, inc=1, device_id=(peer, peer_col), device_id_type=MESH)
    pl.semaphore_wait(barrier, 3)

    started = []

    def copy_of(src, dst, peer, slot, number):
        return pltpu.make_async_remote_copy(
            src_ref=src,
            dst_ref=dst,
            send_sem=send_sem.at[number],
            recv_sem=recv_sem.at[slot],
            device_id=(peer, peer_col),
            device_id_type=MESH,
        )

    def send(src, dst, peer, slot):
        copy = copy_of(src, dst, peer, slot, len(started))
        copy.start()
        started.append(copy)

    def arrive(dst, peer, slot):
        copy_of(dst, dst, peer, slot, 0).wait_recv()

    for other in range(chips):
        send(parts_ref.at[other * 2 + (1 - core)], early.at[other], partner, other)
    for other in range(chips):
        arrive(early.at[other], partner, other)

    def chip_part(chip):
        return parts_ref[chip * 2 + core].astype(jnp.float32) + early[chip].astype(jnp.float32)

    for step in range(forward_hops):
        chip = lax.rem(z + forward_hops - step, chips)
        value = chip_part(chip)
        if step > 0:
            arrive(forward_in.at[step - 1], left, chips + step - 1)
            value = value + forward_in[step - 1].astype(jnp.float32)
        forward_out[step] = value.astype(forward_out.dtype)
        send(forward_out.at[step], forward_in.at[step], right, chips + step)
        if step < backward_hops:
            chip = lax.rem(z + chips - backward_hops + step, chips)
            value = chip_part(chip)
            if step > 0:
                arrive(backward_in.at[step - 1], right, chips + forward_hops + step - 1)
                value = value + backward_in[step - 1].astype(jnp.float32)
            backward_out[step] = value.astype(backward_out.dtype)
            send(backward_out.at[step], backward_in.at[step], left, chips + forward_hops + step)
    arrive(forward_in.at[forward_hops - 1], left, chips + forward_hops - 1)
    total = chip_part(z) + forward_in[forward_hops - 1].astype(jnp.float32)
    if backward_hops > 0:
        arrive(backward_in.at[backward_hops - 1], right, chips + forward_hops + backward_hops - 1)
        total = total + backward_in[backward_hops - 1].astype(jnp.float32)
    out_ref[...] = total.astype(out_ref.dtype)
    for copy in started:
        copy.wait_send()


def ring_scatter(parts, group_count):
    chips = group_count // 2
    forward_hops = chips // 2
    backward_hops = (chips - 1) // 2
    block = parts.shape[1:]
    slots = chips + forward_hops + backward_hops
    return pl.pallas_call(
        functools.partial(scatter_kernel, chips),
        out_shape=jax.ShapeDtypeStruct(block, parts.dtype),
        in_specs=[pl.BlockSpec(memory_space=pltpu.VMEM)],
        out_specs=pl.BlockSpec(memory_space=pltpu.VMEM),
        scratch_shapes=[
            pltpu.VMEM((chips,) + block, parts.dtype),
            pltpu.VMEM((forward_hops,) + block, parts.dtype),
            pltpu.VMEM((max(backward_hops, 1),) + block, parts.dtype),
            pltpu.VMEM((forward_hops,) + block, parts.dtype),
            pltpu.VMEM((max(backward_hops, 1),) + block, parts.dtype),
            pltpu.SemaphoreType.DMA((slots,)),
            pltpu.SemaphoreType.DMA((slots,)),
        ],
        compiler_params=pltpu.CompilerParams(collective_id=1, has_side_effects=True),
    )(parts)


def exchange_kernel(peer_count, from_pair, src_ref, out_ref, send_sem, recv_sem):
    group = lax.axis_index("grp")
    me = lax.axis_index("ep")

    def source_of(dest):
        return dest // 2 if from_pair else dest

    barrier = pltpu.get_barrier_semaphore()
    for shift in range(1, peer_count):
        pl.semaphore_signal(
            barrier,
            inc=1,
            device_id=(group, lax.rem(me + shift, peer_count)),
            device_id_type=MESH,
        )
    pl.semaphore_wait(barrier, peer_count - 1)

    started = []
    for shift in range(1, peer_count):
        dest = lax.rem(me + shift, peer_count)
        copy = pltpu.make_async_remote_copy(
            src_ref=src_ref.at[source_of(dest)],
            dst_ref=out_ref.at[me],
            send_sem=send_sem.at[shift - 1],
            recv_sem=recv_sem.at[me],
            device_id=(group, dest),
            device_id_type=MESH,
        )
        copy.start()
        started.append(copy)
    out_ref[me] = src_ref[source_of(me)]
    for shift in range(1, peer_count):
        origin = lax.rem(me + peer_count - shift, peer_count)
        pltpu.make_async_remote_copy(
            src_ref=out_ref.at[origin],
            dst_ref=out_ref.at[origin],
            send_sem=send_sem.at[0],
            recv_sem=recv_sem.at[origin],
            device_id=(group, origin),
            device_id_type=MESH,
        ).wait_recv()
    for copy in started:
        copy.wait_send()


def exchange(blocks, peer_count, from_pair, collective_id):
    block = blocks.shape[1:]
    return pl.pallas_call(
        functools.partial(exchange_kernel, peer_count, from_pair),
        out_shape=jax.ShapeDtypeStruct((peer_count,) + block, blocks.dtype),
        in_specs=[pl.BlockSpec(memory_space=pltpu.VMEM)],
        out_specs=pl.BlockSpec(memory_space=pltpu.VMEM),
        scratch_shapes=[
            pltpu.SemaphoreType.DMA((peer_count - 1,)),
            pltpu.SemaphoreType.DMA((peer_count,)),
        ],
        compiler_params=pltpu.CompilerParams(
            collective_id=collective_id, has_side_effects=True
        ),
    )(blocks)


def expert_partial(flat_rows, w_gate, w_up, w_down):
    gate_part = jnp.dot(flat_rows, w_gate[0], preferred_element_type=jnp.float32)
    up_part = jnp.dot(flat_rows, w_up[0], preferred_element_type=jnp.float32)
    hidden = (jax.nn.silu(gate_part) * up_part).astype(jnp.bfloat16)
    return jnp.dot(hidden, w_down[0], preferred_element_type=jnp.float32)


def per_device(queries, cache, lengths, live_rows, tokens, ids, gates, w_gate, w_up, w_down):
    context = attend(queries, cache, lengths, live_rows[0])
    group_count = lax.axis_size("grp")
    peer_count = lax.axis_size("ep")
    pair_count = peer_count // 2
    row_count = tokens.shape[0]
    feature = tokens.shape[1]
    expert_slots = group_count * CAP
    slot_count = pair_count * expert_slots
    column_rows = group_count * row_count

    gate_high = gates.astype(jnp.bfloat16)
    gate_low = (gates - gate_high.astype(jnp.float32)).astype(jnp.bfloat16)
    meta = jnp.concatenate([ids.astype(jnp.bfloat16), gate_high, gate_low], axis=1)
    meta = jnp.pad(meta, ((0, 0), (0, 128 - meta.shape[1])))
    packed = ring_gather(jnp.concatenate([tokens, meta], axis=1), group_count).reshape(
        column_rows, feature + meta.shape[1]
    )
    all_tokens = packed[:, :feature]
    all_ids = packed[:, feature : feature + TOPK].astype(jnp.int32)
    all_gates = packed[:, feature + TOPK : feature + 2 * TOPK].astype(jnp.float32) + packed[
        :, feature + 2 * TOPK : feature + 3 * TOPK
    ].astype(jnp.float32)

    my_group = lax.axis_index("grp")
    local = all_ids - pair_count * my_group
    experts = jnp.arange(pair_count, dtype=jnp.int32)
    pick_hot = (local[:, :, None] == experts[None, None, :]).astype(jnp.int32)
    token_hot = jnp.sum(pick_hot, axis=1)
    gate_of = jnp.sum(all_gates[:, :, None] * pick_hot.astype(jnp.float32), axis=1)
    blocks = token_hot.reshape(group_count, row_count, pair_count)
    earlier = (jnp.cumsum(blocks, axis=1) - blocks).reshape(column_rows, pair_count)
    source = jnp.arange(column_rows, dtype=jnp.int32)[:, None] // row_count
    slot_id = experts[None, :] * expert_slots + source * CAP + earlier
    slot_id = jnp.where(token_hot > 0, slot_id, slot_count)
    slots = jnp.arange(slot_count, dtype=jnp.int32)
    match = slot_id[:, :, None] == slots[None, None, :]
    dispatch = jnp.any(match, axis=1).T.astype(jnp.bfloat16)
    combine = jnp.sum(jnp.where(match, gate_of[:, :, None], 0.0), axis=1)

    outgoing = jnp.dot(dispatch, all_tokens, preferred_element_type=jnp.float32).astype(
        jnp.bfloat16
    )
    arriving = exchange(
        outgoing.reshape(pair_count, expert_slots, feature), peer_count, True, 2
    )
    partials = expert_partial(
        arriving.reshape(peer_count * expert_slots, feature), w_gate, w_up, w_down
    ).astype(jnp.bfloat16)
    returned = exchange(
        partials.reshape(peer_count, expert_slots, feature), peer_count, False, 3
    )
    expert_out = (
        returned.reshape(pair_count, 2, expert_slots, feature)
        .astype(jnp.float32)
        .sum(axis=1)
        .astype(jnp.bfloat16)
        .reshape(slot_count, feature)
    )
    column_mixed = jnp.dot(
        combine,
        expert_out.astype(jnp.float32),
        precision=lax.Precision.HIGHEST,
        preferred_element_type=jnp.float32,
    )
    mixed = ring_scatter(
        column_mixed.astype(jnp.bfloat16).reshape(group_count, row_count, feature), group_count
    )
    return (context, mixed)


def solution(mesh):
    in_specs = (
        P(("grp", "ep"), None, None),
        P(("grp", "ep"), None, None),
        P(("grp", "ep")),
        P(("grp", "ep")),
        P(("grp", "ep"), None),
        P(("grp", "ep"), None),
        P(("grp", "ep"), None),
        P(("grp", "ep"), None, None),
        P(("grp", "ep"), None, None),
        P(("grp", "ep"), None, None),
    )
    out_specs = (P(("grp", "ep"), None, None), P(("grp", "ep"), None))
    return jax.shard_map(
        per_device, mesh=mesh, in_specs=in_specs, out_specs=out_specs, check_vma=False
    )
```

```python
import functools

import jax
import jax.numpy as jnp
from jax import lax
from jax.experimental import pallas as pl
from jax.experimental.pallas import tpu as pltpu
from jax.sharding import PartitionSpec as P

MESH = pl.DeviceIdType.MESH
TOPK = 8
LAT = 512
CAP = 2


score_scale = 192.0 ** (-0.5)
neg_large = -1e30


def attend(queries, cache, lengths, live_count):
    scores = (
        jnp.einsum("rhc,rlc->rhl", queries, cache, preferred_element_type=jnp.float32) * score_scale
    )
    positions = lax.broadcasted_iota(jnp.int32, scores.shape, 2)
    inside = positions < lengths[:, None, None]
    masked = jnp.where(inside, scores, neg_large)
    highest = jnp.max(masked, axis=2, keepdims=True)
    powers = jnp.where(inside, jnp.exp(masked - highest), 0.0)
    totals = jnp.sum(powers, axis=2, keepdims=True)
    weights = (powers / totals).astype(jnp.bfloat16)
    context = jnp.einsum(
        "rhl,rlc->rhc", weights, cache[:, :, :LAT], preferred_element_type=jnp.float32
    ).astype(jnp.bfloat16)
    request_slot = lax.broadcasted_iota(jnp.int32, context.shape, 0)
    return jnp.where(request_slot < live_count, context, jnp.zeros_like(context))


def gather_kernel(chips, x_ref, out_ref, send_sem, recv_sem):
    group = lax.axis_index("grp")
    peer_col = lax.axis_index("ep")
    z = group // 2
    core = group % 2
    right = lax.rem(z + 1, chips) * 2 + core
    left = lax.rem(z + chips - 1, chips) * 2 + core
    partner = z * 2 + (1 - core)

    barrier = pltpu.get_barrier_semaphore()
    for peer in (left, right, partner):
        pl.semaphore_signal(barrier, inc=1, device_id=(peer, peer_col), device_id_type=MESH)
    pl.semaphore_wait(barrier, 3)

    started = []

    def send(src, origin, peer):
        copy = pltpu.make_async_remote_copy(
            src_ref=src,
            dst_ref=out_ref.at[origin],
            send_sem=send_sem.at[len(started)],
            recv_sem=recv_sem.at[origin],
            device_id=(peer, peer_col),
            device_id_type=MESH,
        )
        copy.start()
        started.append(copy)

    def arrive(origin, peer):
        pltpu.make_async_remote_copy(
            src_ref=out_ref.at[origin],
            dst_ref=out_ref.at[origin],
            send_sem=send_sem.at[0],
            recv_sem=recv_sem.at[origin],
            device_id=(peer, peer_col),
            device_id_type=MESH,
        ).wait_recv()

    send(x_ref, group, right)
    send(x_ref, group, left)
    send(x_ref, group, partner)
    out_ref[group] = x_ref[...]
    forward_hops = chips // 2
    backward_hops = (chips - 1) // 2
    for step in range(1, forward_hops + 1):
        origin = lax.rem(z + chips - step, chips) * 2 + core
        arrive(origin, left)
        if step < forward_hops:
            send(out_ref.at[origin], origin, right)
        send(out_ref.at[origin], origin, partner)
        if step <= backward_hops:
            origin = lax.rem(z + step, chips) * 2 + core
            arrive(origin, right)
            if step < backward_hops:
                send(out_ref.at[origin], origin, left)
            send(out_ref.at[origin], origin, partner)
    for other in range(chips):
        arrive(other * 2 + (1 - core), partner)
    for copy in started:
        copy.wait_send()


def send_count(chips):
    forward_hops = chips // 2
    backward_hops = (chips - 1) // 2
    return 3 + 2 * forward_hops - 1 + 2 * backward_hops - 1


def ring_gather(block, group_count):
    chips = group_count // 2
    return pl.pallas_call(
        functools.partial(gather_kernel, chips),
        out_shape=jax.ShapeDtypeStruct((group_count,) + block.shape, block.dtype),
        in_specs=[pl.BlockSpec(memory_space=pltpu.VMEM)],
        out_specs=pl.BlockSpec(memory_space=pltpu.VMEM),
        scratch_shapes=[
            pltpu.SemaphoreType.DMA((send_count(chips),)),
            pltpu.SemaphoreType.DMA((group_count,)),
        ],
        compiler_params=pltpu.CompilerParams(collective_id=0, has_side_effects=True),
    )(block)


def scatter_kernel(
    chips, parts_ref, out_ref, early, forward_in, backward_in, forward_out, backward_out,
    send_sem, recv_sem,
):
    group = lax.axis_index("grp")
    peer_col = lax.axis_index("ep")
    z = group // 2
    core = group % 2
    right = lax.rem(z + 1, chips) * 2 + core
    left = lax.rem(z + chips - 1, chips) * 2 + core
    partner = z * 2 + (1 - core)
    forward_hops = chips // 2
    backward_hops = (chips - 1) // 2

    barrier = pltpu.get_barrier_semaphore()
    for peer in (left, right, partner):
        pl.semaphore_signal(barrier, inc=1, device_id=(peer, peer_col), device_id_type=MESH)
    pl.semaphore_wait(barrier, 3)

    started = []

    def copy_of(src, dst, peer, slot, number):
        return pltpu.make_async_remote_copy(
            src_ref=src,
            dst_ref=dst,
            send_sem=send_sem.at[number],
            recv_sem=recv_sem.at[slot],
            device_id=(peer, peer_col),
            device_id_type=MESH,
        )

    def send(src, dst, peer, slot):
        copy = copy_of(src, dst, peer, slot, len(started))
        copy.start()
        started.append(copy)

    def arrive(dst, peer, slot):
        copy_of(dst, dst, peer, slot, 0).wait_recv()

    for other in range(chips):
        send(parts_ref.at[other * 2 + (1 - core)], early.at[other], partner, other)
    for other in range(chips):
        arrive(early.at[other], partner, other)

    def chip_part(chip):
        return parts_ref[chip * 2 + core].astype(jnp.float32) + early[chip].astype(jnp.float32)

    for step in range(forward_hops):
        chip = lax.rem(z + forward_hops - step, chips)
        value = chip_part(chip)
        if step > 0:
            arrive(forward_in.at[step - 1], left, chips + step - 1)
            value = value + forward_in[step - 1].astype(jnp.float32)
        forward_out[step] = value.astype(forward_out.dtype)
        send(forward_out.at[step], forward_in.at[step], right, chips + step)
        if step < backward_hops:
            chip = lax.rem(z + chips - backward_hops + step, chips)
            value = chip_part(chip)
            if step > 0:
                arrive(backward_in.at[step - 1], right, chips + forward_hops + step - 1)
                value = value + backward_in[step - 1].astype(jnp.float32)
            backward_out[step] = value.astype(backward_out.dtype)
            send(backward_out.at[step], backward_in.at[step], left, chips + forward_hops + step)
    arrive(forward_in.at[forward_hops - 1], left, chips + forward_hops - 1)
    total = chip_part(z) + forward_in[forward_hops - 1].astype(jnp.float32)
    if backward_hops > 0:
        arrive(backward_in.at[backward_hops - 1], right, chips + forward_hops + backward_hops - 1)
        total = total + backward_in[backward_hops - 1].astype(jnp.float32)
    out_ref[...] = total.astype(out_ref.dtype)
    for copy in started:
        copy.wait_send()


def ring_scatter(parts, group_count):
    chips = group_count // 2
    forward_hops = chips // 2
    backward_hops = (chips - 1) // 2
    block = parts.shape[1:]
    slots = chips + forward_hops + backward_hops
    return pl.pallas_call(
        functools.partial(scatter_kernel, chips),
        out_shape=jax.ShapeDtypeStruct(block, parts.dtype),
        in_specs=[pl.BlockSpec(memory_space=pltpu.VMEM)],
        out_specs=pl.BlockSpec(memory_space=pltpu.VMEM),
        scratch_shapes=[
            pltpu.VMEM((chips,) + block, parts.dtype),
            pltpu.VMEM((forward_hops,) + block, parts.dtype),
            pltpu.VMEM((max(backward_hops, 1),) + block, parts.dtype),
            pltpu.VMEM((forward_hops,) + block, parts.dtype),
            pltpu.VMEM((max(backward_hops, 1),) + block, parts.dtype),
            pltpu.SemaphoreType.DMA((slots,)),
            pltpu.SemaphoreType.DMA((slots,)),
        ],
        compiler_params=pltpu.CompilerParams(collective_id=1, has_side_effects=True),
    )(parts)


def expert_partial(flat_rows, w_gate, w_up, w_down):
    gate_part = jnp.dot(flat_rows, w_gate[0], preferred_element_type=jnp.float32)
    up_part = jnp.dot(flat_rows, w_up[0], preferred_element_type=jnp.float32)
    hidden = (jax.nn.silu(gate_part) * up_part).astype(jnp.bfloat16)
    return jnp.dot(hidden, w_down[0], preferred_element_type=jnp.float32)


def per_device(queries, cache, lengths, live_rows, tokens, ids, gates, w_gate, w_up, w_down):
    context = attend(queries, cache, lengths, live_rows[0])
    group_count = lax.axis_size("grp")
    peer_count = lax.axis_size("ep")
    pair_count = peer_count // 2
    row_count = tokens.shape[0]
    feature = tokens.shape[1]
    expert_slots = group_count * CAP
    slot_count = pair_count * expert_slots
    column_rows = group_count * row_count

    gate_high = gates.astype(jnp.bfloat16)
    gate_low = (gates - gate_high.astype(jnp.float32)).astype(jnp.bfloat16)
    meta = jnp.concatenate([ids.astype(jnp.bfloat16), gate_high, gate_low], axis=1)
    meta = jnp.pad(meta, ((0, 0), (0, 128 - meta.shape[1])))
    packed = ring_gather(jnp.concatenate([tokens, meta], axis=1), group_count).reshape(
        column_rows, feature + meta.shape[1]
    )
    all_tokens = packed[:, :feature]
    all_ids = packed[:, feature : feature + TOPK].astype(jnp.int32)
    all_gates = packed[:, feature + TOPK : feature + 2 * TOPK].astype(jnp.float32) + packed[
        :, feature + 2 * TOPK : feature + 3 * TOPK
    ].astype(jnp.float32)

    my_group = lax.axis_index("grp")
    local = all_ids - pair_count * my_group
    experts = jnp.arange(pair_count, dtype=jnp.int32)
    pick_hot = (local[:, :, None] == experts[None, None, :]).astype(jnp.int32)
    token_hot = jnp.sum(pick_hot, axis=1)
    gate_of = jnp.sum(all_gates[:, :, None] * pick_hot.astype(jnp.float32), axis=1)
    blocks = token_hot.reshape(group_count, row_count, pair_count)
    earlier = (jnp.cumsum(blocks, axis=1) - blocks).reshape(column_rows, pair_count)
    source = jnp.arange(column_rows, dtype=jnp.int32)[:, None] // row_count
    slot_id = experts[None, :] * expert_slots + source * CAP + earlier
    slot_id = jnp.where(token_hot > 0, slot_id, slot_count)
    slots = jnp.arange(slot_count, dtype=jnp.int32)
    match = slot_id[:, :, None] == slots[None, None, :]
    dispatch = jnp.any(match, axis=1).T.astype(jnp.bfloat16)
    combine = jnp.sum(jnp.where(match, gate_of[:, :, None], 0.0), axis=1)

    outgoing = jnp.dot(dispatch, all_tokens, preferred_element_type=jnp.float32).astype(
        jnp.bfloat16
    )
    staged = outgoing.reshape(pair_count, 2, expert_slots // 2, feature)
    answers = []
    for part in range(2):
        doubled = jnp.repeat(staged[:, part], 2, axis=0)
        arriving = lax.all_to_all(doubled, "ep", split_axis=0, concat_axis=0, tiled=True)
        partials = expert_partial(
            arriving.reshape(peer_count * expert_slots // 2, feature), w_gate, w_up, w_down
        ).astype(jnp.bfloat16)
        returned = lax.all_to_all(
            partials.reshape(peer_count, expert_slots // 2, feature),
            "ep",
            split_axis=0,
            concat_axis=0,
            tiled=True,
        )
        answers.append(
            returned.reshape(pair_count, 2, expert_slots // 2, feature)
            .astype(jnp.float32)
            .sum(axis=1)
            .astype(jnp.bfloat16)
        )
    expert_out = jnp.stack(answers, axis=1).reshape(slot_count, feature)
    column_mixed = jnp.dot(
        combine,
        expert_out.astype(jnp.float32),
        precision=lax.Precision.HIGHEST,
        preferred_element_type=jnp.float32,
    )
    mixed = ring_scatter(
        column_mixed.astype(jnp.bfloat16).reshape(group_count, row_count, feature), group_count
    )
    return (context, mixed)


def solution(mesh):
    in_specs = (
        P(("grp", "ep"), None, None),
        P(("grp", "ep"), None, None),
        P(("grp", "ep")),
        P(("grp", "ep")),
        P(("grp", "ep"), None),
        P(("grp", "ep"), None),
        P(("grp", "ep"), None),
        P(("grp", "ep"), None, None),
        P(("grp", "ep"), None, None),
        P(("grp", "ep"), None, None),
    )
    out_specs = (P(("grp", "ep"), None, None), P(("grp", "ep"), None))
    return jax.shard_map(
        per_device, mesh=mesh, in_specs=in_specs, out_specs=out_specs, check_vma=False
    )
```

```python
import functools

import jax
import jax.numpy as jnp
from jax import lax
from jax.experimental import pallas as pl
from jax.experimental.pallas import tpu as pltpu
from jax.sharding import PartitionSpec as P

MESH = pl.DeviceIdType.MESH
TOPK = 8
LAT = 512
CAP = 2


score_scale = 192.0 ** (-0.5)
neg_large = -1e30


def attend(queries, cache, lengths, live_count):
    scores = (
        jnp.einsum("rhc,rlc->rhl", queries, cache, preferred_element_type=jnp.float32) * score_scale
    )
    positions = lax.broadcasted_iota(jnp.int32, scores.shape, 2)
    inside = positions < lengths[:, None, None]
    masked = jnp.where(inside, scores, neg_large)
    highest = jnp.max(masked, axis=2, keepdims=True)
    powers = jnp.where(inside, jnp.exp(masked - highest), 0.0)
    totals = jnp.sum(powers, axis=2, keepdims=True)
    weights = (powers / totals).astype(jnp.bfloat16)
    context = jnp.einsum(
        "rhl,rlc->rhc", weights, cache[:, :, :LAT], preferred_element_type=jnp.float32
    ).astype(jnp.bfloat16)
    request_slot = lax.broadcasted_iota(jnp.int32, context.shape, 0)
    return jnp.where(request_slot < live_count, context, jnp.zeros_like(context))


def gather_kernel(chips, x_ref, out_ref, send_sem, recv_sem):
    group = lax.axis_index("grp")
    peer_col = lax.axis_index("ep")
    z = group // 2
    core = group % 2
    right = lax.rem(z + 1, chips) * 2 + core
    left = lax.rem(z + chips - 1, chips) * 2 + core
    partner = z * 2 + (1 - core)

    barrier = pltpu.get_barrier_semaphore()
    for peer in (left, right, partner):
        pl.semaphore_signal(barrier, inc=1, device_id=(peer, peer_col), device_id_type=MESH)
    pl.semaphore_wait(barrier, 3)

    started = []

    def send(src, origin, peer):
        copy = pltpu.make_async_remote_copy(
            src_ref=src,
            dst_ref=out_ref.at[origin],
            send_sem=send_sem.at[len(started)],
            recv_sem=recv_sem.at[origin],
            device_id=(peer, peer_col),
            device_id_type=MESH,
        )
        copy.start()
        started.append(copy)

    def arrive(origin, peer):
        pltpu.make_async_remote_copy(
            src_ref=out_ref.at[origin],
            dst_ref=out_ref.at[origin],
            send_sem=send_sem.at[0],
            recv_sem=recv_sem.at[origin],
            device_id=(peer, peer_col),
            device_id_type=MESH,
        ).wait_recv()

    send(x_ref, group, right)
    send(x_ref, group, left)
    send(x_ref, group, partner)
    out_ref[group] = x_ref[...]
    forward_hops = chips // 2
    backward_hops = (chips - 1) // 2
    for step in range(1, forward_hops + 1):
        origin = lax.rem(z + chips - step, chips) * 2 + core
        arrive(origin, left)
        if step < forward_hops:
            send(out_ref.at[origin], origin, right)
        send(out_ref.at[origin], origin, partner)
        if step <= backward_hops:
            origin = lax.rem(z + step, chips) * 2 + core
            arrive(origin, right)
            if step < backward_hops:
                send(out_ref.at[origin], origin, left)
            send(out_ref.at[origin], origin, partner)
    for other in range(chips):
        arrive(other * 2 + (1 - core), partner)
    for copy in started:
        copy.wait_send()


def send_count(chips):
    forward_hops = chips // 2
    backward_hops = (chips - 1) // 2
    return 3 + 2 * forward_hops - 1 + 2 * backward_hops - 1


def ring_gather(block, group_count):
    chips = group_count // 2
    return pl.pallas_call(
        functools.partial(gather_kernel, chips),
        out_shape=jax.ShapeDtypeStruct((group_count,) + block.shape, block.dtype),
        in_specs=[pl.BlockSpec(memory_space=pltpu.VMEM)],
        out_specs=pl.BlockSpec(memory_space=pltpu.VMEM),
        scratch_shapes=[
            pltpu.SemaphoreType.DMA((send_count(chips),)),
            pltpu.SemaphoreType.DMA((group_count,)),
        ],
        compiler_params=pltpu.CompilerParams(collective_id=0, has_side_effects=True),
    )(block)


def scatter_kernel(
    chips, parts_ref, out_ref, early, forward_in, backward_in, forward_out, backward_out,
    send_sem, recv_sem,
):
    group = lax.axis_index("grp")
    peer_col = lax.axis_index("ep")
    z = group // 2
    core = group % 2
    right = lax.rem(z + 1, chips) * 2 + core
    left = lax.rem(z + chips - 1, chips) * 2 + core
    partner = z * 2 + (1 - core)
    forward_hops = chips // 2
    backward_hops = (chips - 1) // 2

    barrier = pltpu.get_barrier_semaphore()
    for peer in (left, right, partner):
        pl.semaphore_signal(barrier, inc=1, device_id=(peer, peer_col), device_id_type=MESH)
    pl.semaphore_wait(barrier, 3)

    started = []

    def copy_of(src, dst, peer, slot, number):
        return pltpu.make_async_remote_copy(
            src_ref=src,
            dst_ref=dst,
            send_sem=send_sem.at[number],
            recv_sem=recv_sem.at[slot],
            device_id=(peer, peer_col),
            device_id_type=MESH,
        )

    def send(src, dst, peer, slot):
        copy = copy_of(src, dst, peer, slot, len(started))
        copy.start()
        started.append(copy)

    def arrive(dst, peer, slot):
        copy_of(dst, dst, peer, slot, 0).wait_recv()

    for other in range(chips):
        send(parts_ref.at[other * 2 + (1 - core)], early.at[other], partner, other)
    for other in range(chips):
        arrive(early.at[other], partner, other)

    def chip_part(chip):
        return parts_ref[chip * 2 + core].astype(jnp.float32) + early[chip].astype(jnp.float32)

    for step in range(forward_hops):
        chip = lax.rem(z + forward_hops - step, chips)
        value = chip_part(chip)
        if step > 0:
            arrive(forward_in.at[step - 1], left, chips + step - 1)
            value = value + forward_in[step - 1].astype(jnp.float32)
        forward_out[step] = value.astype(forward_out.dtype)
        send(forward_out.at[step], forward_in.at[step], right, chips + step)
        if step < backward_hops:
            chip = lax.rem(z + chips - backward_hops + step, chips)
            value = chip_part(chip)
            if step > 0:
                arrive(backward_in.at[step - 1], right, chips + forward_hops + step - 1)
                value = value + backward_in[step - 1].astype(jnp.float32)
            backward_out[step] = value.astype(backward_out.dtype)
            send(backward_out.at[step], backward_in.at[step], left, chips + forward_hops + step)
    arrive(forward_in.at[forward_hops - 1], left, chips + forward_hops - 1)
    total = chip_part(z) + forward_in[forward_hops - 1].astype(jnp.float32)
    if backward_hops > 0:
        arrive(backward_in.at[backward_hops - 1], right, chips + forward_hops + backward_hops - 1)
        total = total + backward_in[backward_hops - 1].astype(jnp.float32)
    out_ref[...] = total.astype(out_ref.dtype)
    for copy in started:
        copy.wait_send()


def ring_scatter(parts, group_count):
    chips = group_count // 2
    forward_hops = chips // 2
    backward_hops = (chips - 1) // 2
    block = parts.shape[1:]
    slots = chips + forward_hops + backward_hops
    return pl.pallas_call(
        functools.partial(scatter_kernel, chips),
        out_shape=jax.ShapeDtypeStruct(block, parts.dtype),
        in_specs=[pl.BlockSpec(memory_space=pltpu.VMEM)],
        out_specs=pl.BlockSpec(memory_space=pltpu.VMEM),
        scratch_shapes=[
            pltpu.VMEM((chips,) + block, parts.dtype),
            pltpu.VMEM((forward_hops,) + block, parts.dtype),
            pltpu.VMEM((max(backward_hops, 1),) + block, parts.dtype),
            pltpu.VMEM((forward_hops,) + block, parts.dtype),
            pltpu.VMEM((max(backward_hops, 1),) + block, parts.dtype),
            pltpu.SemaphoreType.DMA((slots,)),
            pltpu.SemaphoreType.DMA((slots,)),
        ],
        compiler_params=pltpu.CompilerParams(collective_id=1, has_side_effects=True),
    )(parts)


def expert_partial(flat_rows, w_gate, w_up, w_down):
    gate_part = jnp.dot(flat_rows, w_gate[0], preferred_element_type=jnp.float32)
    up_part = jnp.dot(flat_rows, w_up[0], preferred_element_type=jnp.float32)
    hidden = (jax.nn.silu(gate_part) * up_part).astype(jnp.bfloat16)
    return jnp.dot(hidden, w_down[0], preferred_element_type=jnp.float32)


def per_device(queries, cache, lengths, live_rows, tokens, ids, gates, w_gate, w_up, w_down):
    context = attend(queries, cache, lengths, live_rows[0])
    group_count = lax.axis_size("grp")
    peer_count = lax.axis_size("ep")
    pair_count = peer_count // 2
    row_count = tokens.shape[0]
    feature = tokens.shape[1]
    expert_slots = group_count * CAP
    slot_count = pair_count * expert_slots
    column_rows = group_count * row_count

    gate_high = gates.astype(jnp.bfloat16)
    gate_low = (gates - gate_high.astype(jnp.float32)).astype(jnp.bfloat16)
    meta = jnp.concatenate([ids.astype(jnp.bfloat16), gate_high, gate_low], axis=1)
    meta = jnp.pad(meta, ((0, 0), (0, 128 - meta.shape[1])))
    packed = ring_gather(jnp.concatenate([tokens, meta], axis=1), group_count).reshape(
        column_rows, feature + meta.shape[1]
    )
    all_tokens = packed[:, :feature]
    all_ids = packed[:, feature : feature + TOPK].astype(jnp.int32)
    all_gates = packed[:, feature + TOPK : feature + 2 * TOPK].astype(jnp.float32) + packed[
        :, feature + 2 * TOPK : feature + 3 * TOPK
    ].astype(jnp.float32)

    my_group = lax.axis_index("grp")
    local = all_ids - pair_count * my_group
    experts = jnp.arange(pair_count, dtype=jnp.int32)
    pick_hot = (local[:, :, None] == experts[None, None, :]).astype(jnp.int32)
    token_hot = jnp.sum(pick_hot, axis=1)
    gate_of = jnp.sum(all_gates[:, :, None] * pick_hot.astype(jnp.float32), axis=1)
    blocks = token_hot.reshape(group_count, row_count, pair_count)
    earlier = (jnp.cumsum(blocks, axis=1) - blocks).reshape(column_rows, pair_count)
    source = jnp.arange(column_rows, dtype=jnp.int32)[:, None] // row_count
    slot_id = experts[None, :] * expert_slots + source * CAP + earlier
    slot_id = jnp.where(token_hot > 0, slot_id, slot_count)
    slots = jnp.arange(slot_count, dtype=jnp.int32)
    match = slot_id[:, :, None] == slots[None, None, :]
    dispatch = jnp.any(match, axis=1).T.astype(jnp.bfloat16)
    combine = jnp.sum(jnp.where(match, gate_of[:, :, None], 0.0), axis=1)

    outgoing = jnp.dot(dispatch, all_tokens, preferred_element_type=jnp.float32).astype(
        jnp.bfloat16
    )
    doubled = jnp.repeat(outgoing.reshape(pair_count, expert_slots, feature), 2, axis=0)
    arriving = lax.all_to_all(doubled, "ep", split_axis=0, concat_axis=0, tiled=True)
    partials = expert_partial(
        arriving.reshape(peer_count * expert_slots, feature), w_gate, w_up, w_down
    ).astype(jnp.bfloat16)
    returned = lax.all_to_all(
        partials.reshape(peer_count, expert_slots, feature),
        "ep",
        split_axis=0,
        concat_axis=0,
        tiled=True,
    )
    by_half = jnp.broadcast_to(
        combine.reshape(column_rows, pair_count, 1, expert_slots),
        (column_rows, pair_count, 2, expert_slots),
    ).reshape(column_rows, peer_count * expert_slots)
    weight_high = by_half.astype(jnp.bfloat16)
    weight_low = (by_half - weight_high.astype(jnp.float32)).astype(jnp.bfloat16)
    halves = returned.reshape(peer_count * expert_slots, feature)
    column_mixed = jnp.dot(weight_high, halves, preferred_element_type=jnp.float32) + jnp.dot(
        weight_low, halves, preferred_element_type=jnp.float32
    )
    mixed = ring_scatter(
        column_mixed.astype(jnp.bfloat16).reshape(group_count, row_count, feature), group_count
    )
    return (context, mixed)


def solution(mesh):
    in_specs = (
        P(("grp", "ep"), None, None),
        P(("grp", "ep"), None, None),
        P(("grp", "ep")),
        P(("grp", "ep")),
        P(("grp", "ep"), None),
        P(("grp", "ep"), None),
        P(("grp", "ep"), None),
        P(("grp", "ep"), None, None),
        P(("grp", "ep"), None, None),
        P(("grp", "ep"), None, None),
    )
    out_specs = (P(("grp", "ep"), None, None), P(("grp", "ep"), None))
    return jax.shard_map(
        per_device, mesh=mesh, in_specs=in_specs, out_specs=out_specs, check_vma=False
    )
```

```python
import functools

import jax
import jax.numpy as jnp
from jax import lax
from jax.experimental import pallas as pl
from jax.experimental.pallas import tpu as pltpu
from jax.sharding import PartitionSpec as P

MESH = pl.DeviceIdType.MESH
TOPK = 8
LAT = 512
CAP = 2


score_scale = 192.0 ** (-0.5)
neg_large = -1e30


def attend(queries, cache, lengths, live_count):
    scores = (
        jnp.einsum("rhc,rlc->rhl", queries, cache, preferred_element_type=jnp.float32) * score_scale
    )
    positions = lax.broadcasted_iota(jnp.int32, scores.shape, 2)
    inside = positions < lengths[:, None, None]
    masked = jnp.where(inside, scores, neg_large)
    highest = jnp.max(masked, axis=2, keepdims=True)
    powers = jnp.where(inside, jnp.exp(masked - highest), 0.0)
    totals = jnp.sum(powers, axis=2, keepdims=True)
    weights = (powers / totals).astype(jnp.bfloat16)
    context = jnp.einsum(
        "rhl,rlc->rhc", weights, cache[:, :, :LAT], preferred_element_type=jnp.float32
    ).astype(jnp.bfloat16)
    request_slot = lax.broadcasted_iota(jnp.int32, context.shape, 0)
    return jnp.where(request_slot < live_count, context, jnp.zeros_like(context))


def gather_kernel(chips, widths, x_ref, out_ref, send_sem, recv_sem):
    group = lax.axis_index("grp")
    peer_col = lax.axis_index("ep")
    z = group // 2
    core = group % 2
    right = lax.rem(z + 1, chips) * 2 + core
    left = lax.rem(z + chips - 1, chips) * 2 + core
    partner = z * 2 + (1 - core)
    starts = [sum(widths[:piece]) for piece in range(len(widths))]

    barrier = pltpu.get_barrier_semaphore()
    for peer in (left, right, partner):
        pl.semaphore_signal(barrier, inc=1, device_id=(peer, peer_col), device_id_type=MESH)
    pl.semaphore_wait(barrier, 3)

    started = []

    def window(ref, origin, piece):
        columns = pl.ds(starts[piece], widths[piece])
        if origin is None:
            return ref.at[:, columns]
        return ref.at[origin, :, columns]

    def send(origin, piece, peer, from_input):
        copy = pltpu.make_async_remote_copy(
            src_ref=window(x_ref, None, piece) if from_input else window(out_ref, origin, piece),
            dst_ref=window(out_ref, origin, piece),
            send_sem=send_sem.at[len(started)],
            recv_sem=recv_sem.at[origin, piece],
            device_id=(peer, peer_col),
            device_id_type=MESH,
        )
        copy.start()
        started.append(copy)

    def arrive(origin, piece, peer):
        pltpu.make_async_remote_copy(
            src_ref=window(out_ref, origin, piece),
            dst_ref=window(out_ref, origin, piece),
            send_sem=send_sem.at[0],
            recv_sem=recv_sem.at[origin, piece],
            device_id=(peer, peer_col),
            device_id_type=MESH,
        ).wait_recv()

    for piece in range(len(widths)):
        send(group, piece, right, True)
        send(group, piece, left, True)
        send(group, piece, partner, True)
    out_ref[group] = x_ref[...]
    forward_hops = chips // 2
    backward_hops = (chips - 1) // 2
    for step in range(1, forward_hops + 1):
        origin = lax.rem(z + chips - step, chips) * 2 + core
        for piece in range(len(widths)):
            arrive(origin, piece, left)
            if step < forward_hops:
                send(origin, piece, right, False)
            send(origin, piece, partner, False)
        if step <= backward_hops:
            origin = lax.rem(z + step, chips) * 2 + core
            for piece in range(len(widths)):
                arrive(origin, piece, right)
                if step < backward_hops:
                    send(origin, piece, left, False)
                send(origin, piece, partner, False)
    for other in range(chips):
        for piece in range(len(widths)):
            arrive(other * 2 + (1 - core), piece, partner)
    for copy in started:
        copy.wait_send()


def send_count(chips):
    forward_hops = chips // 2
    backward_hops = (chips - 1) // 2
    return 3 + 2 * forward_hops - 1 + 2 * backward_hops - 1


def ring_gather(block, group_count):
    chips = group_count // 2
    lanes = block.shape[1] // 128
    widths = (lanes // 2 * 128, (lanes - lanes // 2) * 128)
    return pl.pallas_call(
        functools.partial(gather_kernel, chips, widths),
        out_shape=jax.ShapeDtypeStruct((group_count,) + block.shape, block.dtype),
        in_specs=[pl.BlockSpec(memory_space=pltpu.VMEM)],
        out_specs=pl.BlockSpec(memory_space=pltpu.VMEM),
        scratch_shapes=[
            pltpu.SemaphoreType.DMA((send_count(chips) * len(widths),)),
            pltpu.SemaphoreType.DMA((group_count, len(widths))),
        ],
        compiler_params=pltpu.CompilerParams(collective_id=0, has_side_effects=True),
    )(block)


def scatter_kernel(
    chips, parts_ref, out_ref, early, forward_in, backward_in, forward_out, backward_out,
    send_sem, recv_sem,
):
    group = lax.axis_index("grp")
    peer_col = lax.axis_index("ep")
    z = group // 2
    core = group % 2
    right = lax.rem(z + 1, chips) * 2 + core
    left = lax.rem(z + chips - 1, chips) * 2 + core
    partner = z * 2 + (1 - core)
    forward_hops = chips // 2
    backward_hops = (chips - 1) // 2

    barrier = pltpu.get_barrier_semaphore()
    for peer in (left, right, partner):
        pl.semaphore_signal(barrier, inc=1, device_id=(peer, peer_col), device_id_type=MESH)
    pl.semaphore_wait(barrier, 3)

    started = []

    def copy_of(src, dst, peer, slot, number):
        return pltpu.make_async_remote_copy(
            src_ref=src,
            dst_ref=dst,
            send_sem=send_sem.at[number],
            recv_sem=recv_sem.at[slot],
            device_id=(peer, peer_col),
            device_id_type=MESH,
        )

    def send(src, dst, peer, slot):
        copy = copy_of(src, dst, peer, slot, len(started))
        copy.start()
        started.append(copy)

    def arrive(dst, peer, slot):
        copy_of(dst, dst, peer, slot, 0).wait_recv()

    for other in range(chips):
        send(parts_ref.at[other * 2 + (1 - core)], early.at[other], partner, other)
    for other in range(chips):
        arrive(early.at[other], partner, other)

    def chip_part(chip):
        return parts_ref[chip * 2 + core].astype(jnp.float32) + early[chip].astype(jnp.float32)

    for step in range(forward_hops):
        chip = lax.rem(z + forward_hops - step, chips)
        value = chip_part(chip)
        if step > 0:
            arrive(forward_in.at[step - 1], left, chips + step - 1)
            value = value + forward_in[step - 1].astype(jnp.float32)
        forward_out[step] = value.astype(forward_out.dtype)
        send(forward_out.at[step], forward_in.at[step], right, chips + step)
        if step < backward_hops:
            chip = lax.rem(z + chips - backward_hops + step, chips)
            value = chip_part(chip)
            if step > 0:
                arrive(backward_in.at[step - 1], right, chips + forward_hops + step - 1)
                value = value + backward_in[step - 1].astype(jnp.float32)
            backward_out[step] = value.astype(backward_out.dtype)
            send(backward_out.at[step], backward_in.at[step], left, chips + forward_hops + step)
    arrive(forward_in.at[forward_hops - 1], left, chips + forward_hops - 1)
    total = chip_part(z) + forward_in[forward_hops - 1].astype(jnp.float32)
    if backward_hops > 0:
        arrive(backward_in.at[backward_hops - 1], right, chips + forward_hops + backward_hops - 1)
        total = total + backward_in[backward_hops - 1].astype(jnp.float32)
    out_ref[...] = total.astype(out_ref.dtype)
    for copy in started:
        copy.wait_send()


def ring_scatter(parts, group_count):
    chips = group_count // 2
    forward_hops = chips // 2
    backward_hops = (chips - 1) // 2
    block = parts.shape[1:]
    slots = chips + forward_hops + backward_hops
    return pl.pallas_call(
        functools.partial(scatter_kernel, chips),
        out_shape=jax.ShapeDtypeStruct(block, parts.dtype),
        in_specs=[pl.BlockSpec(memory_space=pltpu.VMEM)],
        out_specs=pl.BlockSpec(memory_space=pltpu.VMEM),
        scratch_shapes=[
            pltpu.VMEM((chips,) + block, parts.dtype),
            pltpu.VMEM((forward_hops,) + block, parts.dtype),
            pltpu.VMEM((max(backward_hops, 1),) + block, parts.dtype),
            pltpu.VMEM((forward_hops,) + block, parts.dtype),
            pltpu.VMEM((max(backward_hops, 1),) + block, parts.dtype),
            pltpu.SemaphoreType.DMA((slots,)),
            pltpu.SemaphoreType.DMA((slots,)),
        ],
        compiler_params=pltpu.CompilerParams(collective_id=1, has_side_effects=True),
    )(parts)


def expert_partial(flat_rows, w_gate, w_up, w_down):
    gate_part = jnp.dot(flat_rows, w_gate[0], preferred_element_type=jnp.float32)
    up_part = jnp.dot(flat_rows, w_up[0], preferred_element_type=jnp.float32)
    hidden = (jax.nn.silu(gate_part) * up_part).astype(jnp.bfloat16)
    return jnp.dot(hidden, w_down[0], preferred_element_type=jnp.float32)


def per_device(queries, cache, lengths, live_rows, tokens, ids, gates, w_gate, w_up, w_down):
    context = attend(queries, cache, lengths, live_rows[0])
    group_count = lax.axis_size("grp")
    peer_count = lax.axis_size("ep")
    pair_count = peer_count // 2
    row_count = tokens.shape[0]
    feature = tokens.shape[1]
    expert_slots = group_count * CAP
    slot_count = pair_count * expert_slots
    column_rows = group_count * row_count

    gate_high = gates.astype(jnp.bfloat16)
    gate_low = (gates - gate_high.astype(jnp.float32)).astype(jnp.bfloat16)
    meta = jnp.concatenate([ids.astype(jnp.bfloat16), gate_high, gate_low], axis=1)
    meta = jnp.pad(meta, ((0, 0), (0, 128 - meta.shape[1])))
    packed = ring_gather(jnp.concatenate([tokens, meta], axis=1), group_count).reshape(
        column_rows, feature + meta.shape[1]
    )
    all_tokens = packed[:, :feature]
    all_ids = packed[:, feature : feature + TOPK].astype(jnp.int32)
    all_gates = packed[:, feature + TOPK : feature + 2 * TOPK].astype(jnp.float32) + packed[
        :, feature + 2 * TOPK : feature + 3 * TOPK
    ].astype(jnp.float32)

    my_group = lax.axis_index("grp")
    local = all_ids - pair_count * my_group
    experts = jnp.arange(pair_count, dtype=jnp.int32)
    pick_hot = (local[:, :, None] == experts[None, None, :]).astype(jnp.int32)
    token_hot = jnp.sum(pick_hot, axis=1)
    gate_of = jnp.sum(all_gates[:, :, None] * pick_hot.astype(jnp.float32), axis=1)
    blocks = token_hot.reshape(group_count, row_count, pair_count)
    earlier = (jnp.cumsum(blocks, axis=1) - blocks).reshape(column_rows, pair_count)
    source = jnp.arange(column_rows, dtype=jnp.int32)[:, None] // row_count
    slot_id = experts[None, :] * expert_slots + source * CAP + earlier
    slot_id = jnp.where(token_hot > 0, slot_id, slot_count)
    slots = jnp.arange(slot_count, dtype=jnp.int32)
    match = slot_id[:, :, None] == slots[None, None, :]
    dispatch = jnp.any(match, axis=1).T.astype(jnp.bfloat16)
    combine = jnp.sum(jnp.where(match, gate_of[:, :, None], 0.0), axis=1)

    outgoing = jnp.dot(dispatch, all_tokens, preferred_element_type=jnp.float32).astype(
        jnp.bfloat16
    )
    doubled = jnp.repeat(outgoing.reshape(pair_count, expert_slots, feature), 2, axis=0)
    arriving = lax.all_to_all(doubled, "ep", split_axis=0, concat_axis=0, tiled=True)
    partials = expert_partial(
        arriving.reshape(peer_count * expert_slots, feature), w_gate, w_up, w_down
    ).astype(jnp.bfloat16)
    returned = lax.all_to_all(
        partials.reshape(peer_count, expert_slots, feature),
        "ep",
        split_axis=0,
        concat_axis=0,
        tiled=True,
    )
    expert_out = (
        returned.reshape(pair_count, 2, expert_slots, feature)
        .astype(jnp.float32)
        .sum(axis=1)
        .astype(jnp.bfloat16)
        .reshape(slot_count, feature)
    )
    column_mixed = jnp.dot(
        combine,
        expert_out.astype(jnp.float32),
        precision=lax.Precision.HIGHEST,
        preferred_element_type=jnp.float32,
    )
    mixed = ring_scatter(
        column_mixed.astype(jnp.bfloat16).reshape(group_count, row_count, feature), group_count
    )
    return (context, mixed)


def solution(mesh):
    in_specs = (
        P(("grp", "ep"), None, None),
        P(("grp", "ep"), None, None),
        P(("grp", "ep")),
        P(("grp", "ep")),
        P(("grp", "ep"), None),
        P(("grp", "ep"), None),
        P(("grp", "ep"), None),
        P(("grp", "ep"), None, None),
        P(("grp", "ep"), None, None),
        P(("grp", "ep"), None, None),
    )
    out_specs = (P(("grp", "ep"), None, None), P(("grp", "ep"), None))
    return jax.shard_map(
        per_device, mesh=mesh, in_specs=in_specs, out_specs=out_specs, check_vma=False
    )
```

```python
import functools

import jax
import jax.numpy as jnp
from jax import lax
from jax.experimental import pallas as pl
from jax.experimental.pallas import tpu as pltpu
from jax.sharding import PartitionSpec as P

MESH = pl.DeviceIdType.MESH
TOPK = 8
LAT = 512
CAP = 2


score_scale = 192.0 ** (-0.5)
neg_large = -1e30


def attend(queries, cache, lengths, live_count):
    scores = (
        jnp.einsum("rhc,rlc->rhl", queries, cache, preferred_element_type=jnp.float32) * score_scale
    )
    positions = lax.broadcasted_iota(jnp.int32, scores.shape, 2)
    inside = positions < lengths[:, None, None]
    masked = jnp.where(inside, scores, neg_large)
    highest = jnp.max(masked, axis=2, keepdims=True)
    powers = jnp.where(inside, jnp.exp(masked - highest), 0.0)
    totals = jnp.sum(powers, axis=2, keepdims=True)
    weights = (powers / totals).astype(jnp.bfloat16)
    context = jnp.einsum(
        "rhl,rlc->rhc", weights, cache[:, :, :LAT], preferred_element_type=jnp.float32
    ).astype(jnp.bfloat16)
    request_slot = lax.broadcasted_iota(jnp.int32, context.shape, 0)
    return jnp.where(request_slot < live_count, context, jnp.zeros_like(context))


def gather_kernel(chips, widths, x_ref, out_ref, send_sem, recv_sem):
    group = lax.axis_index("grp")
    peer_col = lax.axis_index("ep")
    z = group // 2
    core = group % 2
    right = lax.rem(z + 1, chips) * 2 + core
    left = lax.rem(z + chips - 1, chips) * 2 + core
    partner = z * 2 + (1 - core)
    starts = [sum(widths[:piece]) for piece in range(len(widths))]

    barrier = pltpu.get_barrier_semaphore()
    for peer in (left, right, partner):
        pl.semaphore_signal(barrier, inc=1, device_id=(peer, peer_col), device_id_type=MESH)
    pl.semaphore_wait(barrier, 3)

    started = []

    def window(ref, origin, piece):
        columns = pl.ds(starts[piece], widths[piece])
        if origin is None:
            return ref.at[:, columns]
        return ref.at[origin, :, columns]

    def send(origin, piece, peer, from_input):
        copy = pltpu.make_async_remote_copy(
            src_ref=window(x_ref, None, piece) if from_input else window(out_ref, origin, piece),
            dst_ref=window(out_ref, origin, piece),
            send_sem=send_sem.at[len(started)],
            recv_sem=recv_sem.at[origin, piece],
            device_id=(peer, peer_col),
            device_id_type=MESH,
        )
        copy.start()
        started.append(copy)

    def arrive(origin, piece, peer):
        pltpu.make_async_remote_copy(
            src_ref=window(out_ref, origin, piece),
            dst_ref=window(out_ref, origin, piece),
            send_sem=send_sem.at[0],
            recv_sem=recv_sem.at[origin, piece],
            device_id=(peer, peer_col),
            device_id_type=MESH,
        ).wait_recv()

    for piece in range(len(widths)):
        send(group, piece, right, True)
        send(group, piece, left, True)
        send(group, piece, partner, True)
    out_ref[group] = x_ref[...]
    forward_hops = chips // 2
    backward_hops = (chips - 1) // 2
    for step in range(1, forward_hops + 1):
        origin = lax.rem(z + chips - step, chips) * 2 + core
        for piece in range(len(widths)):
            arrive(origin, piece, left)
            if step < forward_hops:
                send(origin, piece, right, False)
            send(origin, piece, partner, False)
        if step <= backward_hops:
            origin = lax.rem(z + step, chips) * 2 + core
            for piece in range(len(widths)):
                arrive(origin, piece, right)
                if step < backward_hops:
                    send(origin, piece, left, False)
                send(origin, piece, partner, False)
    for other in range(chips):
        for piece in range(len(widths)):
            arrive(other * 2 + (1 - core), piece, partner)
    for copy in started:
        copy.wait_send()


def send_count(chips):
    forward_hops = chips // 2
    backward_hops = (chips - 1) // 2
    return 3 + 2 * forward_hops - 1 + 2 * backward_hops - 1


def ring_gather(block, group_count):
    chips = group_count // 2
    lanes = block.shape[1] // 128
    widths = (lanes // 2 * 128, (lanes - lanes // 2) * 128)
    return pl.pallas_call(
        functools.partial(gather_kernel, chips, widths),
        out_shape=jax.ShapeDtypeStruct((group_count,) + block.shape, block.dtype),
        in_specs=[pl.BlockSpec(memory_space=pltpu.VMEM)],
        out_specs=pl.BlockSpec(memory_space=pltpu.VMEM),
        scratch_shapes=[
            pltpu.SemaphoreType.DMA((send_count(chips) * len(widths),)),
            pltpu.SemaphoreType.DMA((group_count, len(widths))),
        ],
        compiler_params=pltpu.CompilerParams(collective_id=0, has_side_effects=True),
    )(block)


def scatter_kernel(
    chips, parts_ref, out_ref, early, forward_in, backward_in, forward_out, backward_out,
    send_sem, recv_sem,
):
    group = lax.axis_index("grp")
    peer_col = lax.axis_index("ep")
    z = group // 2
    core = group % 2
    right = lax.rem(z + 1, chips) * 2 + core
    left = lax.rem(z + chips - 1, chips) * 2 + core
    partner = z * 2 + (1 - core)
    forward_hops = chips // 2
    backward_hops = (chips - 1) // 2

    barrier = pltpu.get_barrier_semaphore()
    for peer in (left, right, partner):
        pl.semaphore_signal(barrier, inc=1, device_id=(peer, peer_col), device_id_type=MESH)
    pl.semaphore_wait(barrier, 3)

    started = []

    def copy_of(src, dst, peer, slot, number):
        return pltpu.make_async_remote_copy(
            src_ref=src,
            dst_ref=dst,
            send_sem=send_sem.at[number],
            recv_sem=recv_sem.at[slot],
            device_id=(peer, peer_col),
            device_id_type=MESH,
        )

    def send(src, dst, peer, slot):
        copy = copy_of(src, dst, peer, slot, len(started))
        copy.start()
        started.append(copy)

    def arrive(dst, peer, slot):
        copy_of(dst, dst, peer, slot, 0).wait_recv()

    for other in range(chips):
        send(parts_ref.at[other * 2 + (1 - core)], early.at[other], partner, other)
    for other in range(chips):
        arrive(early.at[other], partner, other)

    def chip_part(chip):
        return parts_ref[chip * 2 + core].astype(jnp.float32) + early[chip].astype(jnp.float32)

    for step in range(forward_hops):
        chip = lax.rem(z + forward_hops - step, chips)
        value = chip_part(chip)
        if step > 0:
            arrive(forward_in.at[step - 1], left, chips + step - 1)
            value = value + forward_in[step - 1].astype(jnp.float32)
        forward_out[step] = value.astype(forward_out.dtype)
        send(forward_out.at[step], forward_in.at[step], right, chips + step)
        if step < backward_hops:
            chip = lax.rem(z + chips - backward_hops + step, chips)
            value = chip_part(chip)
            if step > 0:
                arrive(backward_in.at[step - 1], right, chips + forward_hops + step - 1)
                value = value + backward_in[step - 1].astype(jnp.float32)
            backward_out[step] = value.astype(backward_out.dtype)
            send(backward_out.at[step], backward_in.at[step], left, chips + forward_hops + step)
    arrive(forward_in.at[forward_hops - 1], left, chips + forward_hops - 1)
    total = chip_part(z) + forward_in[forward_hops - 1].astype(jnp.float32)
    if backward_hops > 0:
        arrive(backward_in.at[backward_hops - 1], right, chips + forward_hops + backward_hops - 1)
        total = total + backward_in[backward_hops - 1].astype(jnp.float32)
    out_ref[...] = total.astype(out_ref.dtype)
    for copy in started:
        copy.wait_send()


def ring_scatter(parts, group_count):
    chips = group_count // 2
    forward_hops = chips // 2
    backward_hops = (chips - 1) // 2
    block = parts.shape[1:]
    slots = chips + forward_hops + backward_hops
    return pl.pallas_call(
        functools.partial(scatter_kernel, chips),
        out_shape=jax.ShapeDtypeStruct(block, parts.dtype),
        in_specs=[pl.BlockSpec(memory_space=pltpu.VMEM)],
        out_specs=pl.BlockSpec(memory_space=pltpu.VMEM),
        scratch_shapes=[
            pltpu.VMEM((chips,) + block, parts.dtype),
            pltpu.VMEM((forward_hops,) + block, parts.dtype),
            pltpu.VMEM((max(backward_hops, 1),) + block, parts.dtype),
            pltpu.VMEM((forward_hops,) + block, parts.dtype),
            pltpu.VMEM((max(backward_hops, 1),) + block, parts.dtype),
            pltpu.SemaphoreType.DMA((slots,)),
            pltpu.SemaphoreType.DMA((slots,)),
        ],
        compiler_params=pltpu.CompilerParams(collective_id=1, has_side_effects=True),
    )(parts)


def expert_partial(flat_rows, w_gate, w_up, w_down):
    gate_part = jnp.dot(flat_rows, w_gate[0], preferred_element_type=jnp.float32)
    up_part = jnp.dot(flat_rows, w_up[0], preferred_element_type=jnp.float32)
    hidden = lax.optimization_barrier((jax.nn.silu(gate_part) * up_part).astype(jnp.bfloat16))
    return jnp.dot(hidden, w_down[0], preferred_element_type=jnp.float32)


def per_device(queries, cache, lengths, live_rows, tokens, ids, gates, w_gate, w_up, w_down):
    context = attend(queries, cache, lengths, live_rows[0])
    group_count = lax.axis_size("grp")
    peer_count = lax.axis_size("ep")
    pair_count = peer_count // 2
    row_count = tokens.shape[0]
    feature = tokens.shape[1]
    expert_slots = group_count * CAP
    slot_count = pair_count * expert_slots
    column_rows = group_count * row_count

    gate_high = gates.astype(jnp.bfloat16)
    gate_low = (gates - gate_high.astype(jnp.float32)).astype(jnp.bfloat16)
    meta = jnp.concatenate([ids.astype(jnp.bfloat16), gate_high, gate_low], axis=1)
    meta = jnp.pad(meta, ((0, 0), (0, 128 - meta.shape[1])))
    packed = ring_gather(jnp.concatenate([tokens, meta], axis=1), group_count).reshape(
        column_rows, feature + meta.shape[1]
    )
    all_tokens = packed[:, :feature]
    all_ids = packed[:, feature : feature + TOPK].astype(jnp.int32)
    all_gates = packed[:, feature + TOPK : feature + 2 * TOPK].astype(jnp.float32) + packed[
        :, feature + 2 * TOPK : feature + 3 * TOPK
    ].astype(jnp.float32)

    my_group = lax.axis_index("grp")
    local = all_ids - pair_count * my_group
    experts = jnp.arange(pair_count, dtype=jnp.int32)
    pick_hot = (local[:, :, None] == experts[None, None, :]).astype(jnp.int32)
    token_hot = jnp.sum(pick_hot, axis=1)
    gate_of = jnp.sum(all_gates[:, :, None] * pick_hot.astype(jnp.float32), axis=1)
    blocks = token_hot.reshape(group_count, row_count, pair_count)
    earlier = (jnp.cumsum(blocks, axis=1) - blocks).reshape(column_rows, pair_count)
    source = jnp.arange(column_rows, dtype=jnp.int32)[:, None] // row_count
    slot_id = experts[None, :] * expert_slots + source * CAP + earlier
    slot_id = jnp.where(token_hot > 0, slot_id, slot_count)
    slots = jnp.arange(slot_count, dtype=jnp.int32)
    match = slot_id[:, :, None] == slots[None, None, :]
    dispatch = jnp.any(match, axis=1).T.astype(jnp.bfloat16)
    combine = jnp.sum(jnp.where(match, gate_of[:, :, None], 0.0), axis=1)

    outgoing = jnp.dot(dispatch, all_tokens, preferred_element_type=jnp.float32).astype(
        jnp.bfloat16
    )
    doubled = jnp.repeat(outgoing.reshape(pair_count, expert_slots, feature), 2, axis=0)
    arriving = lax.all_to_all(doubled, "ep", split_axis=0, concat_axis=0, tiled=True)
    partials = expert_partial(
        arriving.reshape(peer_count * expert_slots, feature), w_gate, w_up, w_down
    ).astype(jnp.bfloat16)
    returned = lax.all_to_all(
        partials.reshape(peer_count, expert_slots, feature),
        "ep",
        split_axis=0,
        concat_axis=0,
        tiled=True,
    )
    expert_out = (
        returned.reshape(pair_count, 2, expert_slots, feature)
        .astype(jnp.float32)
        .sum(axis=1)
        .astype(jnp.bfloat16)
        .reshape(slot_count, feature)
    )
    column_mixed = jnp.dot(
        combine,
        expert_out.astype(jnp.float32),
        precision=lax.Precision.HIGHEST,
        preferred_element_type=jnp.float32,
    )
    mixed = ring_scatter(
        column_mixed.astype(jnp.bfloat16).reshape(group_count, row_count, feature), group_count
    )
    return (context, mixed)


def solution(mesh):
    in_specs = (
        P(("grp", "ep"), None, None),
        P(("grp", "ep"), None, None),
        P(("grp", "ep")),
        P(("grp", "ep")),
        P(("grp", "ep"), None),
        P(("grp", "ep"), None),
        P(("grp", "ep"), None),
        P(("grp", "ep"), None, None),
        P(("grp", "ep"), None, None),
        P(("grp", "ep"), None, None),
    )
    out_specs = (P(("grp", "ep"), None, None), P(("grp", "ep"), None))
    return jax.shard_map(
        per_device, mesh=mesh, in_specs=in_specs, out_specs=out_specs, check_vma=False
    )
```

```python
import functools

import jax
import jax.numpy as jnp
from jax import lax
from jax.experimental import pallas as pl
from jax.experimental.pallas import tpu as pltpu
from jax.sharding import PartitionSpec as P

MESH = pl.DeviceIdType.MESH
TOPK = 8
LAT = 512
CAP = 2


score_scale = 192.0 ** (-0.5)
neg_large = -1e30


def attend(queries, cache, lengths, live_count):
    scores = (
        jnp.einsum("rhc,rlc->rhl", queries, cache, preferred_element_type=jnp.float32) * score_scale
    )
    positions = lax.broadcasted_iota(jnp.int32, scores.shape, 2)
    inside = positions < lengths[:, None, None]
    masked = jnp.where(inside, scores, neg_large)
    highest = jnp.max(masked, axis=2, keepdims=True)
    powers = jnp.where(inside, jnp.exp(masked - highest), 0.0)
    totals = jnp.sum(powers, axis=2, keepdims=True)
    weights = (powers / totals).astype(jnp.bfloat16)
    context = jnp.einsum(
        "rhl,rlc->rhc", weights, cache[:, :, :LAT], preferred_element_type=jnp.float32
    ).astype(jnp.bfloat16)
    request_slot = lax.broadcasted_iota(jnp.int32, context.shape, 0)
    return jnp.where(request_slot < live_count, context, jnp.zeros_like(context))


def gather_kernel(chips, widths, x_ref, out_ref, send_sem, recv_sem):
    group = lax.axis_index("grp")
    peer_col = lax.axis_index("ep")
    z = group // 2
    core = group % 2
    right = lax.rem(z + 1, chips) * 2 + core
    left = lax.rem(z + chips - 1, chips) * 2 + core
    partner = z * 2 + (1 - core)
    starts = [sum(widths[:piece]) for piece in range(len(widths))]

    barrier = pltpu.get_barrier_semaphore()
    for peer in (left, right, partner):
        pl.semaphore_signal(barrier, inc=1, device_id=(peer, peer_col), device_id_type=MESH)
    pl.semaphore_wait(barrier, 3)

    started = []

    def window(ref, origin, piece):
        columns = pl.ds(starts[piece], widths[piece])
        if origin is None:
            return ref.at[:, columns]
        return ref.at[origin, :, columns]

    def send(origin, piece, peer, from_input):
        copy = pltpu.make_async_remote_copy(
            src_ref=window(x_ref, None, piece) if from_input else window(out_ref, origin, piece),
            dst_ref=window(out_ref, origin, piece),
            send_sem=send_sem.at[len(started)],
            recv_sem=recv_sem.at[origin, piece],
            device_id=(peer, peer_col),
            device_id_type=MESH,
        )
        copy.start()
        started.append(copy)

    def arrive(origin, piece, peer):
        pltpu.make_async_remote_copy(
            src_ref=window(out_ref, origin, piece),
            dst_ref=window(out_ref, origin, piece),
            send_sem=send_sem.at[0],
            recv_sem=recv_sem.at[origin, piece],
            device_id=(peer, peer_col),
            device_id_type=MESH,
        ).wait_recv()

    for piece in range(len(widths)):
        send(group, piece, right, True)
        send(group, piece, left, True)
        send(group, piece, partner, True)
    out_ref[group] = x_ref[...]
    forward_hops = chips // 2
    backward_hops = (chips - 1) // 2
    for step in range(1, forward_hops + 1):
        origin = lax.rem(z + chips - step, chips) * 2 + core
        for piece in range(len(widths)):
            arrive(origin, piece, left)
            if step < forward_hops:
                send(origin, piece, right, False)
            send(origin, piece, partner, False)
        if step <= backward_hops:
            origin = lax.rem(z + step, chips) * 2 + core
            for piece in range(len(widths)):
                arrive(origin, piece, right)
                if step < backward_hops:
                    send(origin, piece, left, False)
                send(origin, piece, partner, False)
    for other in range(chips):
        for piece in range(len(widths)):
            arrive(other * 2 + (1 - core), piece, partner)
    for copy in started:
        copy.wait_send()


def send_count(chips):
    forward_hops = chips // 2
    backward_hops = (chips - 1) // 2
    return 3 + 2 * forward_hops - 1 + 2 * backward_hops - 1


def ring_gather(block, group_count):
    chips = group_count // 2
    lanes = block.shape[1] // 128
    widths = (lanes // 2 * 128, (lanes - lanes // 2) * 128)
    return pl.pallas_call(
        functools.partial(gather_kernel, chips, widths),
        out_shape=jax.ShapeDtypeStruct((group_count,) + block.shape, block.dtype),
        in_specs=[pl.BlockSpec(memory_space=pltpu.VMEM)],
        out_specs=pl.BlockSpec(memory_space=pltpu.VMEM),
        scratch_shapes=[
            pltpu.SemaphoreType.DMA((send_count(chips) * len(widths),)),
            pltpu.SemaphoreType.DMA((group_count, len(widths))),
        ],
        compiler_params=pltpu.CompilerParams(collective_id=0, has_side_effects=True),
    )(block)


def scatter_kernel(
    chips, widths, parts_ref, out_ref, early, forward_in, backward_in, forward_out, backward_out,
    send_sem, recv_sem,
):
    group = lax.axis_index("grp")
    peer_col = lax.axis_index("ep")
    z = group // 2
    core = group % 2
    right = lax.rem(z + 1, chips) * 2 + core
    left = lax.rem(z + chips - 1, chips) * 2 + core
    partner = z * 2 + (1 - core)
    forward_hops = chips // 2
    backward_hops = (chips - 1) // 2
    starts = [sum(widths[:piece]) for piece in range(len(widths))]
    pieces = range(len(widths))

    def cols(piece):
        return pl.ds(starts[piece], widths[piece])

    barrier = pltpu.get_barrier_semaphore()
    for peer in (left, right, partner):
        pl.semaphore_signal(barrier, inc=1, device_id=(peer, peer_col), device_id_type=MESH)
    pl.semaphore_wait(barrier, 3)

    started = []

    def copy_of(src, dst, peer, slot, piece, number):
        return pltpu.make_async_remote_copy(
            src_ref=src,
            dst_ref=dst,
            send_sem=send_sem.at[number],
            recv_sem=recv_sem.at[slot, piece],
            device_id=(peer, peer_col),
            device_id_type=MESH,
        )

    def send(src, dst, peer, slot, piece):
        copy = copy_of(src, dst, peer, slot, piece, len(started))
        copy.start()
        started.append(copy)

    def arrive(dst, peer, slot, piece):
        copy_of(dst, dst, peer, slot, piece, 0).wait_recv()

    for other in range(chips):
        for piece in pieces:
            send(
                parts_ref.at[other * 2 + (1 - core), :, cols(piece)],
                early.at[other, :, cols(piece)],
                partner,
                other,
                piece,
            )
    for other in range(chips):
        for piece in pieces:
            arrive(early.at[other, :, cols(piece)], partner, other, piece)

    def chip_part(chip, piece):
        return parts_ref[chip * 2 + core, :, cols(piece)].astype(jnp.float32) + early[
            chip, :, cols(piece)
        ].astype(jnp.float32)

    def hop(step, chip, inbox, outbox, source, dest, first_slot, piece):
        value = chip_part(chip, piece)
        if step > 0:
            arrive(inbox.at[step - 1, :, cols(piece)], source, first_slot + step - 1, piece)
            value = value + inbox[step - 1, :, cols(piece)].astype(jnp.float32)
        outbox[step, :, cols(piece)] = value.astype(outbox.dtype)
        send(outbox.at[step, :, cols(piece)], inbox.at[step, :, cols(piece)], dest, first_slot + step, piece)

    for step in range(forward_hops):
        chip = lax.rem(z + forward_hops - step, chips)
        for piece in pieces:
            hop(step, chip, forward_in, forward_out, left, right, chips, piece)
        if step < backward_hops:
            chip = lax.rem(z + chips - backward_hops + step, chips)
            for piece in pieces:
                hop(step, chip, backward_in, backward_out, right, left, chips + forward_hops, piece)
    for piece in pieces:
        arrive(forward_in.at[forward_hops - 1, :, cols(piece)], left, chips + forward_hops - 1, piece)
        total = chip_part(z, piece) + forward_in[forward_hops - 1, :, cols(piece)].astype(
            jnp.float32
        )
        if backward_hops > 0:
            last = chips + forward_hops + backward_hops - 1
            arrive(backward_in.at[backward_hops - 1, :, cols(piece)], right, last, piece)
            total = total + backward_in[backward_hops - 1, :, cols(piece)].astype(jnp.float32)
        out_ref[:, cols(piece)] = total.astype(out_ref.dtype)
    for copy in started:
        copy.wait_send()


def ring_scatter(parts, group_count):
    chips = group_count // 2
    forward_hops = chips // 2
    backward_hops = (chips - 1) // 2
    block = parts.shape[1:]
    lanes = block[1] // 128
    widths = (lanes // 2 * 128, (lanes - lanes // 2) * 128)
    slots = chips + forward_hops + backward_hops
    sends = (chips + forward_hops + backward_hops) * len(widths)
    return pl.pallas_call(
        functools.partial(scatter_kernel, chips, widths),
        out_shape=jax.ShapeDtypeStruct(block, parts.dtype),
        in_specs=[pl.BlockSpec(memory_space=pltpu.VMEM)],
        out_specs=pl.BlockSpec(memory_space=pltpu.VMEM),
        scratch_shapes=[
            pltpu.VMEM((chips,) + block, parts.dtype),
            pltpu.VMEM((forward_hops,) + block, parts.dtype),
            pltpu.VMEM((max(backward_hops, 1),) + block, parts.dtype),
            pltpu.VMEM((forward_hops,) + block, parts.dtype),
            pltpu.VMEM((max(backward_hops, 1),) + block, parts.dtype),
            pltpu.SemaphoreType.DMA((sends,)),
            pltpu.SemaphoreType.DMA((slots, len(widths))),
        ],
        compiler_params=pltpu.CompilerParams(collective_id=1, has_side_effects=True),
    )(parts)


def expert_partial(flat_rows, w_gate, w_up, w_down):
    gate_part = jnp.dot(flat_rows, w_gate[0], preferred_element_type=jnp.float32)
    up_part = jnp.dot(flat_rows, w_up[0], preferred_element_type=jnp.float32)
    hidden = lax.optimization_barrier((jax.nn.silu(gate_part) * up_part).astype(jnp.bfloat16))
    return jnp.dot(hidden, w_down[0], preferred_element_type=jnp.float32)


def per_device(queries, cache, lengths, live_rows, tokens, ids, gates, w_gate, w_up, w_down):
    context = attend(queries, cache, lengths, live_rows[0])
    group_count = lax.axis_size("grp")
    peer_count = lax.axis_size("ep")
    pair_count = peer_count // 2
    row_count = tokens.shape[0]
    feature = tokens.shape[1]
    expert_slots = group_count * CAP
    slot_count = pair_count * expert_slots
    column_rows = group_count * row_count

    gate_high = gates.astype(jnp.bfloat16)
    gate_low = (gates - gate_high.astype(jnp.float32)).astype(jnp.bfloat16)
    meta = jnp.concatenate([ids.astype(jnp.bfloat16), gate_high, gate_low], axis=1)
    meta = jnp.pad(meta, ((0, 0), (0, 128 - meta.shape[1])))
    packed = ring_gather(jnp.concatenate([tokens, meta], axis=1), group_count).reshape(
        column_rows, feature + meta.shape[1]
    )
    all_tokens = packed[:, :feature]
    all_ids = packed[:, feature : feature + TOPK].astype(jnp.int32)
    all_gates = packed[:, feature + TOPK : feature + 2 * TOPK].astype(jnp.float32) + packed[
        :, feature + 2 * TOPK : feature + 3 * TOPK
    ].astype(jnp.float32)

    my_group = lax.axis_index("grp")
    local = all_ids - pair_count * my_group
    experts = jnp.arange(pair_count, dtype=jnp.int32)
    pick_hot = (local[:, :, None] == experts[None, None, :]).astype(jnp.int32)
    token_hot = jnp.sum(pick_hot, axis=1)
    gate_of = jnp.sum(all_gates[:, :, None] * pick_hot.astype(jnp.float32), axis=1)
    blocks = token_hot.reshape(group_count, row_count, pair_count)
    earlier = (jnp.cumsum(blocks, axis=1) - blocks).reshape(column_rows, pair_count)
    source = jnp.arange(column_rows, dtype=jnp.int32)[:, None] // row_count
    slot_id = experts[None, :] * expert_slots + source * CAP + earlier
    slot_id = jnp.where(token_hot > 0, slot_id, slot_count)
    slots = jnp.arange(slot_count, dtype=jnp.int32)
    match = slot_id[:, :, None] == slots[None, None, :]
    dispatch = jnp.any(match, axis=1).T.astype(jnp.bfloat16)
    combine = jnp.sum(jnp.where(match, gate_of[:, :, None], 0.0), axis=1)

    outgoing = jnp.dot(dispatch, all_tokens, preferred_element_type=jnp.float32).astype(
        jnp.bfloat16
    )
    doubled = jnp.repeat(outgoing.reshape(pair_count, expert_slots, feature), 2, axis=0)
    arriving = lax.all_to_all(doubled, "ep", split_axis=0, concat_axis=0, tiled=True)
    partials = expert_partial(
        arriving.reshape(peer_count * expert_slots, feature), w_gate, w_up, w_down
    ).astype(jnp.bfloat16)
    returned = lax.all_to_all(
        partials.reshape(peer_count, expert_slots, feature),
        "ep",
        split_axis=0,
        concat_axis=0,
        tiled=True,
    )
    expert_out = (
        returned.reshape(pair_count, 2, expert_slots, feature)
        .astype(jnp.float32)
        .sum(axis=1)
        .astype(jnp.bfloat16)
        .reshape(slot_count, feature)
    )
    weight_high = combine.astype(jnp.bfloat16)
    weight_low = (combine - weight_high.astype(jnp.float32)).astype(jnp.bfloat16)
    column_mixed = jnp.dot(weight_high, expert_out, preferred_element_type=jnp.float32) + jnp.dot(
        weight_low, expert_out, preferred_element_type=jnp.float32
    )
    mixed = ring_scatter(
        column_mixed.astype(jnp.bfloat16).reshape(group_count, row_count, feature), group_count
    )
    return (context, mixed)


def solution(mesh):
    in_specs = (
        P(("grp", "ep"), None, None),
        P(("grp", "ep"), None, None),
        P(("grp", "ep")),
        P(("grp", "ep")),
        P(("grp", "ep"), None),
        P(("grp", "ep"), None),
        P(("grp", "ep"), None),
        P(("grp", "ep"), None, None),
        P(("grp", "ep"), None, None),
        P(("grp", "ep"), None, None),
    )
    out_specs = (P(("grp", "ep"), None, None), P(("grp", "ep"), None))
    return jax.shard_map(
        per_device, mesh=mesh, in_specs=in_specs, out_specs=out_specs, check_vma=False
    )
```

```python
import functools

import jax
import jax.numpy as jnp
from jax import lax
from jax.experimental import pallas as pl
from jax.experimental.pallas import tpu as pltpu
from jax.sharding import PartitionSpec as P

MESH = pl.DeviceIdType.MESH
CHUNKS = 4
TOPK = 8
LAT = 512
CAP = 2


score_scale = 192.0 ** (-0.5)
neg_large = -1e30


def attend(queries, cache, lengths, live_count):
    scores = (
        jnp.einsum("rhc,rlc->rhl", queries, cache, preferred_element_type=jnp.float32) * score_scale
    )
    positions = lax.broadcasted_iota(jnp.int32, scores.shape, 2)
    inside = positions < lengths[:, None, None]
    masked = jnp.where(inside, scores, neg_large)
    highest = jnp.max(masked, axis=2, keepdims=True)
    powers = jnp.where(inside, jnp.exp(masked - highest), 0.0)
    totals = jnp.sum(powers, axis=2, keepdims=True)
    weights = (powers / totals).astype(jnp.bfloat16)
    context = jnp.einsum(
        "rhl,rlc->rhc", weights, cache[:, :, :LAT], preferred_element_type=jnp.float32
    ).astype(jnp.bfloat16)
    request_slot = lax.broadcasted_iota(jnp.int32, context.shape, 0)
    return jnp.where(request_slot < live_count, context, jnp.zeros_like(context))


def gather_kernel(chips, widths, x_ref, out_ref, send_sem, recv_sem):
    group = lax.axis_index("grp")
    peer_col = lax.axis_index("ep")
    z = group // 2
    core = group % 2
    right = lax.rem(z + 1, chips) * 2 + core
    left = lax.rem(z + chips - 1, chips) * 2 + core
    partner = z * 2 + (1 - core)
    starts = [sum(widths[:piece]) for piece in range(len(widths))]

    barrier = pltpu.get_barrier_semaphore()
    for peer in (left, right, partner):
        pl.semaphore_signal(barrier, inc=1, device_id=(peer, peer_col), device_id_type=MESH)
    pl.semaphore_wait(barrier, 3)

    started = []

    def window(ref, origin, piece):
        columns = pl.ds(starts[piece], widths[piece])
        if origin is None:
            return ref.at[:, columns]
        return ref.at[origin, :, columns]

    def send(origin, piece, peer, from_input):
        copy = pltpu.make_async_remote_copy(
            src_ref=window(x_ref, None, piece) if from_input else window(out_ref, origin, piece),
            dst_ref=window(out_ref, origin, piece),
            send_sem=send_sem.at[len(started)],
            recv_sem=recv_sem.at[origin, piece],
            device_id=(peer, peer_col),
            device_id_type=MESH,
        )
        copy.start()
        started.append(copy)

    def arrive(origin, piece, peer):
        pltpu.make_async_remote_copy(
            src_ref=window(out_ref, origin, piece),
            dst_ref=window(out_ref, origin, piece),
            send_sem=send_sem.at[0],
            recv_sem=recv_sem.at[origin, piece],
            device_id=(peer, peer_col),
            device_id_type=MESH,
        ).wait_recv()

    for piece in range(len(widths)):
        send(group, piece, right, True)
        send(group, piece, left, True)
        send(group, piece, partner, True)
    out_ref[group] = x_ref[...]
    forward_hops = chips // 2
    backward_hops = (chips - 1) // 2
    for step in range(1, forward_hops + 1):
        origin = lax.rem(z + chips - step, chips) * 2 + core
        for piece in range(len(widths)):
            arrive(origin, piece, left)
            if step < forward_hops:
                send(origin, piece, right, False)
            send(origin, piece, partner, False)
        if step <= backward_hops:
            origin = lax.rem(z + step, chips) * 2 + core
            for piece in range(len(widths)):
                arrive(origin, piece, right)
                if step < backward_hops:
                    send(origin, piece, left, False)
                send(origin, piece, partner, False)
    for other in range(chips):
        for piece in range(len(widths)):
            arrive(other * 2 + (1 - core), piece, partner)
    for copy in started:
        copy.wait_send()


def send_count(chips):
    forward_hops = chips // 2
    backward_hops = (chips - 1) // 2
    return 3 + 2 * forward_hops - 1 + 2 * backward_hops - 1


def ring_gather(block, group_count):
    chips = group_count // 2
    lanes = block.shape[1] // 128
    widths = tuple(
        (lanes * (piece + 1) // CHUNKS - lanes * piece // CHUNKS) * 128 for piece in range(CHUNKS)
    )
    return pl.pallas_call(
        functools.partial(gather_kernel, chips, widths),
        out_shape=jax.ShapeDtypeStruct((group_count,) + block.shape, block.dtype),
        in_specs=[pl.BlockSpec(memory_space=pltpu.VMEM)],
        out_specs=pl.BlockSpec(memory_space=pltpu.VMEM),
        scratch_shapes=[
            pltpu.SemaphoreType.DMA((send_count(chips) * len(widths),)),
            pltpu.SemaphoreType.DMA((group_count, len(widths))),
        ],
        compiler_params=pltpu.CompilerParams(collective_id=0, has_side_effects=True),
    )(block)


def scatter_kernel(
    chips, widths, parts_ref, out_ref, early, forward_in, backward_in, forward_out, backward_out,
    send_sem, recv_sem,
):
    group = lax.axis_index("grp")
    peer_col = lax.axis_index("ep")
    z = group // 2
    core = group % 2
    right = lax.rem(z + 1, chips) * 2 + core
    left = lax.rem(z + chips - 1, chips) * 2 + core
    partner = z * 2 + (1 - core)
    forward_hops = chips // 2
    backward_hops = (chips - 1) // 2
    starts = [sum(widths[:piece]) for piece in range(len(widths))]
    pieces = range(len(widths))

    def cols(piece):
        return pl.ds(starts[piece], widths[piece])

    barrier = pltpu.get_barrier_semaphore()
    for peer in (left, right, partner):
        pl.semaphore_signal(barrier, inc=1, device_id=(peer, peer_col), device_id_type=MESH)
    pl.semaphore_wait(barrier, 3)

    started = []

    def copy_of(src, dst, peer, slot, piece, number):
        return pltpu.make_async_remote_copy(
            src_ref=src,
            dst_ref=dst,
            send_sem=send_sem.at[number],
            recv_sem=recv_sem.at[slot, piece],
            device_id=(peer, peer_col),
            device_id_type=MESH,
        )

    def send(src, dst, peer, slot, piece):
        copy = copy_of(src, dst, peer, slot, piece, len(started))
        copy.start()
        started.append(copy)

    def arrive(dst, peer, slot, piece):
        copy_of(dst, dst, peer, slot, piece, 0).wait_recv()

    for other in range(chips):
        for piece in pieces:
            send(
                parts_ref.at[other * 2 + (1 - core), :, cols(piece)],
                early.at[other, :, cols(piece)],
                partner,
                other,
                piece,
            )
    for other in range(chips):
        for piece in pieces:
            arrive(early.at[other, :, cols(piece)], partner, other, piece)

    def chip_part(chip, piece):
        return parts_ref[chip * 2 + core, :, cols(piece)].astype(jnp.float32) + early[
            chip, :, cols(piece)
        ].astype(jnp.float32)

    def hop(step, chip, inbox, outbox, source, dest, first_slot, piece):
        value = chip_part(chip, piece)
        if step > 0:
            arrive(inbox.at[step - 1, :, cols(piece)], source, first_slot + step - 1, piece)
            value = value + inbox[step - 1, :, cols(piece)].astype(jnp.float32)
        outbox[step, :, cols(piece)] = value.astype(outbox.dtype)
        send(outbox.at[step, :, cols(piece)], inbox.at[step, :, cols(piece)], dest, first_slot + step, piece)

    for step in range(forward_hops):
        chip = lax.rem(z + forward_hops - step, chips)
        for piece in pieces:
            hop(step, chip, forward_in, forward_out, left, right, chips, piece)
        if step < backward_hops:
            chip = lax.rem(z + chips - backward_hops + step, chips)
            for piece in pieces:
                hop(step, chip, backward_in, backward_out, right, left, chips + forward_hops, piece)
    for piece in pieces:
        arrive(forward_in.at[forward_hops - 1, :, cols(piece)], left, chips + forward_hops - 1, piece)
        total = chip_part(z, piece) + forward_in[forward_hops - 1, :, cols(piece)].astype(
            jnp.float32
        )
        if backward_hops > 0:
            last = chips + forward_hops + backward_hops - 1
            arrive(backward_in.at[backward_hops - 1, :, cols(piece)], right, last, piece)
            total = total + backward_in[backward_hops - 1, :, cols(piece)].astype(jnp.float32)
        out_ref[:, cols(piece)] = total.astype(out_ref.dtype)
    for copy in started:
        copy.wait_send()


def ring_scatter(parts, group_count):
    chips = group_count // 2
    forward_hops = chips // 2
    backward_hops = (chips - 1) // 2
    block = parts.shape[1:]
    lanes = block[1] // 128
    widths = tuple(
        (lanes * (piece + 1) // CHUNKS - lanes * piece // CHUNKS) * 128 for piece in range(CHUNKS)
    )
    slots = chips + forward_hops + backward_hops
    sends = (chips + forward_hops + backward_hops) * len(widths)
    return pl.pallas_call(
        functools.partial(scatter_kernel, chips, widths),
        out_shape=jax.ShapeDtypeStruct(block, parts.dtype),
        in_specs=[pl.BlockSpec(memory_space=pltpu.VMEM)],
        out_specs=pl.BlockSpec(memory_space=pltpu.VMEM),
        scratch_shapes=[
            pltpu.VMEM((chips,) + block, parts.dtype),
            pltpu.VMEM((forward_hops,) + block, parts.dtype),
            pltpu.VMEM((max(backward_hops, 1),) + block, parts.dtype),
            pltpu.VMEM((forward_hops,) + block, parts.dtype),
            pltpu.VMEM((max(backward_hops, 1),) + block, parts.dtype),
            pltpu.SemaphoreType.DMA((sends,)),
            pltpu.SemaphoreType.DMA((slots, len(widths))),
        ],
        compiler_params=pltpu.CompilerParams(collective_id=1, has_side_effects=True),
    )(parts)


def expert_partial(flat_rows, w_gate, w_up, w_down):
    gate_part = jnp.dot(flat_rows, w_gate[0], preferred_element_type=jnp.float32)
    up_part = jnp.dot(flat_rows, w_up[0], preferred_element_type=jnp.float32)
    hidden = lax.optimization_barrier((jax.nn.silu(gate_part) * up_part).astype(jnp.bfloat16))
    return jnp.dot(hidden, w_down[0], preferred_element_type=jnp.float32)


def per_device(queries, cache, lengths, live_rows, tokens, ids, gates, w_gate, w_up, w_down):
    context = attend(queries, cache, lengths, live_rows[0])
    group_count = lax.axis_size("grp")
    peer_count = lax.axis_size("ep")
    pair_count = peer_count // 2
    row_count = tokens.shape[0]
    feature = tokens.shape[1]
    expert_slots = group_count * CAP
    slot_count = pair_count * expert_slots
    column_rows = group_count * row_count

    gate_high = gates.astype(jnp.bfloat16)
    gate_low = (gates - gate_high.astype(jnp.float32)).astype(jnp.bfloat16)
    meta = jnp.concatenate([ids.astype(jnp.bfloat16), gate_high, gate_low], axis=1)
    meta = jnp.pad(meta, ((0, 0), (0, 128 - meta.shape[1])))
    packed = ring_gather(jnp.concatenate([tokens, meta], axis=1), group_count).reshape(
        column_rows, feature + meta.shape[1]
    )
    all_tokens = packed[:, :feature]
    all_ids = packed[:, feature : feature + TOPK].astype(jnp.int32)
    all_gates = packed[:, feature + TOPK : feature + 2 * TOPK].astype(jnp.float32) + packed[
        :, feature + 2 * TOPK : feature + 3 * TOPK
    ].astype(jnp.float32)

    my_group = lax.axis_index("grp")
    local = all_ids - pair_count * my_group
    experts = jnp.arange(pair_count, dtype=jnp.int32)
    pick_hot = (local[:, :, None] == experts[None, None, :]).astype(jnp.int32)
    token_hot = jnp.sum(pick_hot, axis=1)
    gate_of = jnp.sum(all_gates[:, :, None] * pick_hot.astype(jnp.float32), axis=1)
    blocks = token_hot.reshape(group_count, row_count, pair_count)
    earlier = (jnp.cumsum(blocks, axis=1) - blocks).reshape(column_rows, pair_count)
    source = jnp.arange(column_rows, dtype=jnp.int32)[:, None] // row_count
    slot_id = experts[None, :] * expert_slots + source * CAP + earlier
    slot_id = jnp.where(token_hot > 0, slot_id, slot_count)
    slots = jnp.arange(slot_count, dtype=jnp.int32)
    match = slot_id[:, :, None] == slots[None, None, :]
    dispatch = jnp.any(match, axis=1).T.astype(jnp.bfloat16)
    combine = jnp.sum(jnp.where(match, gate_of[:, :, None], 0.0), axis=1)

    outgoing = jnp.dot(dispatch, all_tokens, preferred_element_type=jnp.float32).astype(
        jnp.bfloat16
    )
    doubled = jnp.repeat(outgoing.reshape(pair_count, expert_slots, feature), 2, axis=0)
    arriving = lax.all_to_all(doubled, "ep", split_axis=0, concat_axis=0, tiled=True)
    partials = expert_partial(
        arriving.reshape(peer_count * expert_slots, feature), w_gate, w_up, w_down
    ).astype(jnp.bfloat16)
    returned = lax.all_to_all(
        partials.reshape(peer_count, expert_slots, feature),
        "ep",
        split_axis=0,
        concat_axis=0,
        tiled=True,
    )
    expert_out = (
        returned.reshape(pair_count, 2, expert_slots, feature)
        .astype(jnp.float32)
        .sum(axis=1)
        .astype(jnp.bfloat16)
        .reshape(slot_count, feature)
    )
    weight_high = combine.astype(jnp.bfloat16)
    weight_low = (combine - weight_high.astype(jnp.float32)).astype(jnp.bfloat16)
    column_mixed = jnp.dot(weight_high, expert_out, preferred_element_type=jnp.float32) + jnp.dot(
        weight_low, expert_out, preferred_element_type=jnp.float32
    )
    mixed = ring_scatter(
        column_mixed.astype(jnp.bfloat16).reshape(group_count, row_count, feature), group_count
    )
    return (context, mixed)


def solution(mesh):
    in_specs = (
        P(("grp", "ep"), None, None),
        P(("grp", "ep"), None, None),
        P(("grp", "ep")),
        P(("grp", "ep")),
        P(("grp", "ep"), None),
        P(("grp", "ep"), None),
        P(("grp", "ep"), None),
        P(("grp", "ep"), None, None),
        P(("grp", "ep"), None, None),
        P(("grp", "ep"), None, None),
    )
    out_specs = (P(("grp", "ep"), None, None), P(("grp", "ep"), None))
    return jax.shard_map(
        per_device, mesh=mesh, in_specs=in_specs, out_specs=out_specs, check_vma=False
    )
```

```python
import functools

import jax
import jax.numpy as jnp
from jax import lax
from jax.experimental import pallas as pl
from jax.experimental.pallas import tpu as pltpu
from jax.sharding import PartitionSpec as P

MESH = pl.DeviceIdType.MESH
CHUNKS = 4
TOPK = 8
LAT = 512
CAP = 2


score_scale = 192.0 ** (-0.5)
neg_large = -1e30


def attend(queries, cache, lengths, live_count):
    scores = (
        jnp.einsum("rhc,rlc->rhl", queries, cache, preferred_element_type=jnp.float32) * score_scale
    )
    positions = lax.broadcasted_iota(jnp.int32, scores.shape, 2)
    inside = positions < lengths[:, None, None]
    masked = jnp.where(inside, scores, neg_large)
    highest = jnp.max(masked, axis=2, keepdims=True)
    powers = jnp.where(inside, jnp.exp(masked - highest), 0.0)
    totals = jnp.sum(powers, axis=2, keepdims=True)
    weights = (powers / totals).astype(jnp.bfloat16)
    context = jnp.einsum(
        "rhl,rlc->rhc", weights, cache[:, :, :LAT], preferred_element_type=jnp.float32
    ).astype(jnp.bfloat16)
    request_slot = lax.broadcasted_iota(jnp.int32, context.shape, 0)
    return jnp.where(request_slot < live_count, context, jnp.zeros_like(context))


def gather_kernel(chips, widths, x_ref, out_ref, send_sem, recv_sem):
    group = lax.axis_index("grp")
    peer_col = lax.axis_index("ep")
    z = group // 2
    core = group % 2
    right = lax.rem(z + 1, chips) * 2 + core
    left = lax.rem(z + chips - 1, chips) * 2 + core
    partner = z * 2 + (1 - core)
    starts = [sum(widths[:piece]) for piece in range(len(widths))]

    barrier = pltpu.get_barrier_semaphore()
    for peer in (left, right, partner):
        pl.semaphore_signal(barrier, inc=1, device_id=(peer, peer_col), device_id_type=MESH)
    pl.semaphore_wait(barrier, 3)

    started = []

    def window(ref, origin, piece):
        columns = pl.ds(starts[piece], widths[piece])
        if origin is None:
            return ref.at[:, columns]
        return ref.at[origin, :, columns]

    def send(origin, piece, peer, from_input):
        copy = pltpu.make_async_remote_copy(
            src_ref=window(x_ref, None, piece) if from_input else window(out_ref, origin, piece),
            dst_ref=window(out_ref, origin, piece),
            send_sem=send_sem.at[len(started)],
            recv_sem=recv_sem.at[origin, piece],
            device_id=(peer, peer_col),
            device_id_type=MESH,
        )
        copy.start()
        started.append(copy)

    def arrive(origin, piece, peer):
        pltpu.make_async_remote_copy(
            src_ref=window(out_ref, origin, piece),
            dst_ref=window(out_ref, origin, piece),
            send_sem=send_sem.at[0],
            recv_sem=recv_sem.at[origin, piece],
            device_id=(peer, peer_col),
            device_id_type=MESH,
        ).wait_recv()

    for piece in range(len(widths)):
        send(group, piece, right, True)
        send(group, piece, left, True)
        send(group, piece, partner, True)
    out_ref[group] = x_ref[...]
    forward_hops = chips // 2
    backward_hops = (chips - 1) // 2
    for step in range(1, forward_hops + 1):
        origin = lax.rem(z + chips - step, chips) * 2 + core
        for piece in range(len(widths)):
            arrive(origin, piece, left)
            if step < forward_hops:
                send(origin, piece, right, False)
            send(origin, piece, partner, False)
        if step <= backward_hops:
            origin = lax.rem(z + step, chips) * 2 + core
            for piece in range(len(widths)):
                arrive(origin, piece, right)
                if step < backward_hops:
                    send(origin, piece, left, False)
                send(origin, piece, partner, False)
    for other in range(chips):
        for piece in range(len(widths)):
            arrive(other * 2 + (1 - core), piece, partner)
    for copy in started:
        copy.wait_send()


def send_count(chips):
    forward_hops = chips // 2
    backward_hops = (chips - 1) // 2
    return 3 + 2 * forward_hops - 1 + 2 * backward_hops - 1


def ring_gather(block, group_count):
    chips = group_count // 2
    lanes = block.shape[1] // 128
    widths = tuple(
        (lanes * (piece + 1) // CHUNKS - lanes * piece // CHUNKS) * 128 for piece in range(CHUNKS)
    )
    return pl.pallas_call(
        functools.partial(gather_kernel, chips, widths),
        out_shape=jax.ShapeDtypeStruct((group_count,) + block.shape, block.dtype),
        in_specs=[pl.BlockSpec(memory_space=pltpu.VMEM)],
        out_specs=pl.BlockSpec(memory_space=pltpu.VMEM),
        scratch_shapes=[
            pltpu.SemaphoreType.DMA((send_count(chips) * len(widths),)),
            pltpu.SemaphoreType.DMA((group_count, len(widths))),
        ],
        compiler_params=pltpu.CompilerParams(collective_id=0, has_side_effects=True),
    )(block)


def scatter_kernel(
    chips, widths, parts_ref, out_ref, early, forward_in, backward_in, forward_out, backward_out,
    send_sem, recv_sem,
):
    group = lax.axis_index("grp")
    peer_col = lax.axis_index("ep")
    z = group // 2
    core = group % 2
    right = lax.rem(z + 1, chips) * 2 + core
    left = lax.rem(z + chips - 1, chips) * 2 + core
    partner = z * 2 + (1 - core)
    forward_hops = chips // 2
    backward_hops = (chips - 1) // 2
    starts = [sum(widths[:piece]) for piece in range(len(widths))]
    pieces = range(len(widths))

    def cols(piece):
        return pl.ds(starts[piece], widths[piece])

    barrier = pltpu.get_barrier_semaphore()
    for peer in (left, right, partner):
        pl.semaphore_signal(barrier, inc=1, device_id=(peer, peer_col), device_id_type=MESH)
    pl.semaphore_wait(barrier, 3)

    started = []

    def copy_of(src, dst, peer, slot, piece, number):
        return pltpu.make_async_remote_copy(
            src_ref=src,
            dst_ref=dst,
            send_sem=send_sem.at[number],
            recv_sem=recv_sem.at[slot, piece],
            device_id=(peer, peer_col),
            device_id_type=MESH,
        )

    def send(src, dst, peer, slot, piece):
        copy = copy_of(src, dst, peer, slot, piece, len(started))
        copy.start()
        started.append(copy)

    def arrive(dst, peer, slot, piece):
        copy_of(dst, dst, peer, slot, piece, 0).wait_recv()

    for other in range(chips):
        for piece in pieces:
            send(
                parts_ref.at[other * 2 + (1 - core), :, cols(piece)],
                early.at[other, :, cols(piece)],
                partner,
                other,
                piece,
            )
    for other in range(chips):
        for piece in pieces:
            arrive(early.at[other, :, cols(piece)], partner, other, piece)

    def chip_part(chip, piece):
        return parts_ref[chip * 2 + core, :, cols(piece)].astype(jnp.float32) + early[
            chip, :, cols(piece)
        ].astype(jnp.float32)

    def hop(step, chip, inbox, outbox, source, dest, first_slot, piece):
        value = chip_part(chip, piece)
        if step > 0:
            arrive(inbox.at[step - 1, :, cols(piece)], source, first_slot + step - 1, piece)
            value = value + inbox[step - 1, :, cols(piece)].astype(jnp.float32)
        outbox[step, :, cols(piece)] = value.astype(outbox.dtype)
        send(outbox.at[step, :, cols(piece)], inbox.at[step, :, cols(piece)], dest, first_slot + step, piece)

    for step in range(forward_hops):
        chip = lax.rem(z + forward_hops - step, chips)
        for piece in pieces:
            hop(step, chip, forward_in, forward_out, left, right, chips, piece)
        if step < backward_hops:
            chip = lax.rem(z + chips - backward_hops + step, chips)
            for piece in pieces:
                hop(step, chip, backward_in, backward_out, right, left, chips + forward_hops, piece)
    for piece in pieces:
        arrive(forward_in.at[forward_hops - 1, :, cols(piece)], left, chips + forward_hops - 1, piece)
        total = chip_part(z, piece) + forward_in[forward_hops - 1, :, cols(piece)].astype(
            jnp.float32
        )
        if backward_hops > 0:
            last = chips + forward_hops + backward_hops - 1
            arrive(backward_in.at[backward_hops - 1, :, cols(piece)], right, last, piece)
            total = total + backward_in[backward_hops - 1, :, cols(piece)].astype(jnp.float32)
        out_ref[:, cols(piece)] = total.astype(out_ref.dtype)
    for copy in started:
        copy.wait_send()


def ring_scatter(parts, group_count):
    chips = group_count // 2
    forward_hops = chips // 2
    backward_hops = (chips - 1) // 2
    block = parts.shape[1:]
    lanes = block[1] // 128
    widths = tuple(
        (lanes * (piece + 1) // CHUNKS - lanes * piece // CHUNKS) * 128 for piece in range(CHUNKS)
    )
    slots = chips + forward_hops + backward_hops
    sends = (chips + forward_hops + backward_hops) * len(widths)
    return pl.pallas_call(
        functools.partial(scatter_kernel, chips, widths),
        out_shape=jax.ShapeDtypeStruct(block, parts.dtype),
        in_specs=[pl.BlockSpec(memory_space=pltpu.VMEM)],
        out_specs=pl.BlockSpec(memory_space=pltpu.VMEM),
        scratch_shapes=[
            pltpu.VMEM((chips,) + block, parts.dtype),
            pltpu.VMEM((forward_hops,) + block, parts.dtype),
            pltpu.VMEM((max(backward_hops, 1),) + block, parts.dtype),
            pltpu.VMEM((forward_hops,) + block, parts.dtype),
            pltpu.VMEM((max(backward_hops, 1),) + block, parts.dtype),
            pltpu.SemaphoreType.DMA((sends,)),
            pltpu.SemaphoreType.DMA((slots, len(widths))),
        ],
        compiler_params=pltpu.CompilerParams(collective_id=1, has_side_effects=True),
    )(parts)


def expert_partial(flat_rows, w_gate, w_up, w_down):
    gate_part = jnp.dot(flat_rows, w_gate[0], preferred_element_type=jnp.float32)
    up_part = jnp.dot(flat_rows, w_up[0], preferred_element_type=jnp.float32)
    hidden = lax.optimization_barrier((jax.nn.silu(gate_part) * up_part).astype(jnp.bfloat16))
    return jnp.dot(hidden, w_down[0], preferred_element_type=jnp.float32)


def per_device(queries, cache, lengths, live_rows, tokens, ids, gates, w_gate, w_up, w_down):
    context = attend(queries, cache, lengths, live_rows[0])
    group_count = lax.axis_size("grp")
    peer_count = lax.axis_size("ep")
    pair_count = peer_count // 2
    row_count = tokens.shape[0]
    feature = tokens.shape[1]
    expert_slots = group_count * CAP
    slot_count = pair_count * expert_slots
    column_rows = group_count * row_count

    gate_high = gates.astype(jnp.bfloat16)
    gate_low = (gates - gate_high.astype(jnp.float32)).astype(jnp.bfloat16)
    meta = jnp.concatenate([ids.astype(jnp.bfloat16), gate_high, gate_low], axis=1)
    meta = jnp.pad(meta, ((0, 0), (0, 128 - meta.shape[1])))
    packed = ring_gather(jnp.concatenate([tokens, meta], axis=1), group_count).reshape(
        column_rows, feature + meta.shape[1]
    )
    all_tokens = packed[:, :feature]
    all_ids = packed[:, feature : feature + TOPK].astype(jnp.int32)
    all_gates = packed[:, feature + TOPK : feature + 2 * TOPK].astype(jnp.float32) + packed[
        :, feature + 2 * TOPK : feature + 3 * TOPK
    ].astype(jnp.float32)

    my_group = lax.axis_index("grp")
    local = all_ids - pair_count * my_group
    experts = jnp.arange(pair_count, dtype=jnp.int32)
    pick_hot = (local[:, :, None] == experts[None, None, :]).astype(jnp.int32)
    token_hot = jnp.sum(pick_hot, axis=1)
    gate_of = jnp.sum(all_gates[:, :, None] * pick_hot.astype(jnp.float32), axis=1)
    blocks = token_hot.reshape(group_count, row_count, pair_count)
    earlier = (jnp.cumsum(blocks, axis=1) - blocks).reshape(column_rows, pair_count)
    source = jnp.arange(column_rows, dtype=jnp.int32)[:, None] // row_count
    slot_id = experts[None, :] * expert_slots + source * CAP + earlier
    slot_id = jnp.where(token_hot > 0, slot_id, slot_count)
    slots = jnp.arange(slot_count, dtype=jnp.int32)
    match = slot_id[:, :, None] == slots[None, None, :]
    dispatch = jnp.any(match, axis=1).T.astype(jnp.bfloat16)
    combine = jnp.sum(jnp.where(match, gate_of[:, :, None], 0.0), axis=1)

    outgoing = jnp.dot(dispatch, all_tokens, preferred_element_type=jnp.float32).astype(
        jnp.bfloat16
    )
    doubled = jnp.repeat(outgoing.reshape(pair_count, expert_slots, feature), 2, axis=0)
    arriving = lax.all_to_all(doubled, "ep", split_axis=0, concat_axis=0, tiled=True)
    partials = expert_partial(
        arriving.reshape(peer_count * expert_slots, feature), w_gate, w_up, w_down
    ).astype(jnp.bfloat16)
    returned = lax.all_to_all(
        partials.reshape(peer_count, expert_slots, feature),
        "ep",
        split_axis=0,
        concat_axis=0,
        tiled=True,
    )
    half_slots = jnp.arange(2 * slot_count, dtype=jnp.int32)
    half_weight = 0.0
    for half in range(2):
        placed = slot_id + half * expert_slots + experts[None, :] * expert_slots
        placed = jnp.where(token_hot > 0, placed, 2 * slot_count)
        half_weight = half_weight + jnp.sum(
            jnp.where(placed[:, :, None] == half_slots[None, None, :], gate_of[:, :, None], 0.0),
            axis=1,
        )
    weight_high = half_weight.astype(jnp.bfloat16)
    weight_low = (half_weight - weight_high.astype(jnp.float32)).astype(jnp.bfloat16)
    weight_high, weight_low = lax.optimization_barrier((weight_high, weight_low))
    halves = returned.reshape(2 * slot_count, feature)
    column_mixed = jnp.dot(weight_high, halves, preferred_element_type=jnp.float32) + jnp.dot(
        weight_low, halves, preferred_element_type=jnp.float32
    )
    mixed = ring_scatter(
        column_mixed.astype(jnp.bfloat16).reshape(group_count, row_count, feature), group_count
    )
    return (context, mixed)


def solution(mesh):
    in_specs = (
        P(("grp", "ep"), None, None),
        P(("grp", "ep"), None, None),
        P(("grp", "ep")),
        P(("grp", "ep")),
        P(("grp", "ep"), None),
        P(("grp", "ep"), None),
        P(("grp", "ep"), None),
        P(("grp", "ep"), None, None),
        P(("grp", "ep"), None, None),
        P(("grp", "ep"), None, None),
    )
    out_specs = (P(("grp", "ep"), None, None), P(("grp", "ep"), None))
    return jax.shard_map(
        per_device, mesh=mesh, in_specs=in_specs, out_specs=out_specs, check_vma=False
    )
```

```python
import functools

import jax
import jax.numpy as jnp
from jax import lax
from jax.experimental import pallas as pl
from jax.experimental.pallas import tpu as pltpu
from jax.sharding import PartitionSpec as P

MESH = pl.DeviceIdType.MESH
CHUNKS = 4
TOPK = 8
LAT = 512
CAP = 2


score_scale = 192.0 ** (-0.5)
neg_large = -1e30


def attend(queries, cache, lengths, live_count):
    scores = (
        jnp.einsum("rhc,rlc->rhl", queries, cache, preferred_element_type=jnp.float32) * score_scale
    )
    positions = lax.broadcasted_iota(jnp.int32, scores.shape, 2)
    inside = positions < lengths[:, None, None]
    masked = jnp.where(inside, scores, neg_large)
    highest = jnp.max(masked, axis=2, keepdims=True)
    powers = jnp.where(inside, jnp.exp(masked - highest), 0.0)
    totals = jnp.sum(powers, axis=2, keepdims=True)
    weights = (powers / totals).astype(jnp.bfloat16)
    context = jnp.einsum(
        "rhl,rlc->rhc", weights, cache[:, :, :LAT], preferred_element_type=jnp.float32
    ).astype(jnp.bfloat16)
    request_slot = lax.broadcasted_iota(jnp.int32, context.shape, 0)
    return jnp.where(request_slot < live_count, context, jnp.zeros_like(context))


def gather_kernel(chips, windows, x_ref, m_ref, out_ref, mout_ref, send_sem, recv_sem):
    group = lax.axis_index("grp")
    peer_col = lax.axis_index("ep")
    z = group // 2
    core = group % 2
    right = lax.rem(z + 1, chips) * 2 + core
    left = lax.rem(z + chips - 1, chips) * 2 + core
    partner = z * 2 + (1 - core)
    sources = (x_ref, m_ref)
    targets = (out_ref, mout_ref)

    barrier = pltpu.get_barrier_semaphore()
    for peer in (left, right, partner):
        pl.semaphore_signal(barrier, inc=1, device_id=(peer, peer_col), device_id_type=MESH)
    pl.semaphore_wait(barrier, 3)

    started = []

    def window(refs, origin, piece):
        which, start, width = windows[piece]
        columns = pl.ds(start, width)
        if origin is None:
            return refs[which].at[:, columns]
        return refs[which].at[origin, :, columns]

    def send(origin, piece, peer, from_input):
        copy = pltpu.make_async_remote_copy(
            src_ref=window(sources, None, piece) if from_input else window(targets, origin, piece),
            dst_ref=window(targets, origin, piece),
            send_sem=send_sem.at[len(started)],
            recv_sem=recv_sem.at[origin, piece],
            device_id=(peer, peer_col),
            device_id_type=MESH,
        )
        copy.start()
        started.append(copy)

    def arrive(origin, piece, peer):
        pltpu.make_async_remote_copy(
            src_ref=window(targets, origin, piece),
            dst_ref=window(targets, origin, piece),
            send_sem=send_sem.at[0],
            recv_sem=recv_sem.at[origin, piece],
            device_id=(peer, peer_col),
            device_id_type=MESH,
        ).wait_recv()

    for piece in range(len(windows)):
        send(group, piece, right, True)
        send(group, piece, left, True)
        send(group, piece, partner, True)
    out_ref[group] = x_ref[...]
    mout_ref[group] = m_ref[...]
    forward_hops = chips // 2
    backward_hops = (chips - 1) // 2
    for step in range(1, forward_hops + 1):
        origin = lax.rem(z + chips - step, chips) * 2 + core
        for piece in range(len(windows)):
            arrive(origin, piece, left)
            if step < forward_hops:
                send(origin, piece, right, False)
            send(origin, piece, partner, False)
        if step <= backward_hops:
            origin = lax.rem(z + step, chips) * 2 + core
            for piece in range(len(windows)):
                arrive(origin, piece, right)
                if step < backward_hops:
                    send(origin, piece, left, False)
                send(origin, piece, partner, False)
    for other in range(chips):
        for piece in range(len(windows)):
            arrive(other * 2 + (1 - core), piece, partner)
    for copy in started:
        copy.wait_send()


def send_count(chips):
    forward_hops = chips // 2
    backward_hops = (chips - 1) // 2
    return 3 + 2 * forward_hops - 1 + 2 * backward_hops - 1


def ring_gather(block, meta, group_count):
    chips = group_count // 2
    lanes = block.shape[1] // 128
    windows = tuple(
        (0, lanes * piece // CHUNKS * 128, (lanes * (piece + 1) // CHUNKS - lanes * piece // CHUNKS) * 128)
        for piece in range(CHUNKS)
    ) + ((1, 0, meta.shape[1]),)
    return pl.pallas_call(
        functools.partial(gather_kernel, chips, windows),
        out_shape=(
            jax.ShapeDtypeStruct((group_count,) + block.shape, block.dtype),
            jax.ShapeDtypeStruct((group_count,) + meta.shape, meta.dtype),
        ),
        in_specs=[pl.BlockSpec(memory_space=pltpu.VMEM)] * 2,
        out_specs=(pl.BlockSpec(memory_space=pltpu.VMEM),) * 2,
        scratch_shapes=[
            pltpu.SemaphoreType.DMA((send_count(chips) * len(windows),)),
            pltpu.SemaphoreType.DMA((group_count, len(windows))),
        ],
        compiler_params=pltpu.CompilerParams(collective_id=0, has_side_effects=True),
    )(block, meta)


def scatter_kernel(
    chips, widths, parts_ref, out_ref, early, forward_in, backward_in, forward_out, backward_out,
    send_sem, recv_sem,
):
    group = lax.axis_index("grp")
    peer_col = lax.axis_index("ep")
    z = group // 2
    core = group % 2
    right = lax.rem(z + 1, chips) * 2 + core
    left = lax.rem(z + chips - 1, chips) * 2 + core
    partner = z * 2 + (1 - core)
    forward_hops = chips // 2
    backward_hops = (chips - 1) // 2
    starts = [sum(widths[:piece]) for piece in range(len(widths))]
    pieces = range(len(widths))

    def cols(piece):
        return pl.ds(starts[piece], widths[piece])

    barrier = pltpu.get_barrier_semaphore()
    for peer in (left, right, partner):
        pl.semaphore_signal(barrier, inc=1, device_id=(peer, peer_col), device_id_type=MESH)
    pl.semaphore_wait(barrier, 3)

    started = []

    def copy_of(src, dst, peer, slot, piece, number):
        return pltpu.make_async_remote_copy(
            src_ref=src,
            dst_ref=dst,
            send_sem=send_sem.at[number],
            recv_sem=recv_sem.at[slot, piece],
            device_id=(peer, peer_col),
            device_id_type=MESH,
        )

    def send(src, dst, peer, slot, piece):
        copy = copy_of(src, dst, peer, slot, piece, len(started))
        copy.start()
        started.append(copy)

    def arrive(dst, peer, slot, piece):
        copy_of(dst, dst, peer, slot, piece, 0).wait_recv()

    for other in range(chips):
        for piece in pieces:
            send(
                parts_ref.at[other * 2 + (1 - core), :, cols(piece)],
                early.at[other, :, cols(piece)],
                partner,
                other,
                piece,
            )
    for other in range(chips):
        for piece in pieces:
            arrive(early.at[other, :, cols(piece)], partner, other, piece)

    def chip_part(chip, piece):
        return parts_ref[chip * 2 + core, :, cols(piece)].astype(jnp.float32) + early[
            chip, :, cols(piece)
        ].astype(jnp.float32)

    def hop(step, chip, inbox, outbox, source, dest, first_slot, piece):
        value = chip_part(chip, piece)
        if step > 0:
            arrive(inbox.at[step - 1, :, cols(piece)], source, first_slot + step - 1, piece)
            value = value + inbox[step - 1, :, cols(piece)].astype(jnp.float32)
        outbox[step, :, cols(piece)] = value.astype(outbox.dtype)
        send(outbox.at[step, :, cols(piece)], inbox.at[step, :, cols(piece)], dest, first_slot + step, piece)

    for step in range(forward_hops):
        chip = lax.rem(z + forward_hops - step, chips)
        for piece in pieces:
            hop(step, chip, forward_in, forward_out, left, right, chips, piece)
        if step < backward_hops:
            chip = lax.rem(z + chips - backward_hops + step, chips)
            for piece in pieces:
                hop(step, chip, backward_in, backward_out, right, left, chips + forward_hops, piece)
    for piece in pieces:
        arrive(forward_in.at[forward_hops - 1, :, cols(piece)], left, chips + forward_hops - 1, piece)
        total = chip_part(z, piece) + forward_in[forward_hops - 1, :, cols(piece)].astype(
            jnp.float32
        )
        if backward_hops > 0:
            last = chips + forward_hops + backward_hops - 1
            arrive(backward_in.at[backward_hops - 1, :, cols(piece)], right, last, piece)
            total = total + backward_in[backward_hops - 1, :, cols(piece)].astype(jnp.float32)
        out_ref[:, cols(piece)] = total.astype(out_ref.dtype)
    for copy in started:
        copy.wait_send()


def ring_scatter(parts, group_count):
    chips = group_count // 2
    forward_hops = chips // 2
    backward_hops = (chips - 1) // 2
    block = parts.shape[1:]
    lanes = block[1] // 128
    widths = tuple(
        (lanes * (piece + 1) // CHUNKS - lanes * piece // CHUNKS) * 128 for piece in range(CHUNKS)
    )
    slots = chips + forward_hops + backward_hops
    sends = (chips + forward_hops + backward_hops) * len(widths)
    return pl.pallas_call(
        functools.partial(scatter_kernel, chips, widths),
        out_shape=jax.ShapeDtypeStruct(block, parts.dtype),
        in_specs=[pl.BlockSpec(memory_space=pltpu.VMEM)],
        out_specs=pl.BlockSpec(memory_space=pltpu.VMEM),
        scratch_shapes=[
            pltpu.VMEM((chips,) + block, parts.dtype),
            pltpu.VMEM((forward_hops,) + block, parts.dtype),
            pltpu.VMEM((max(backward_hops, 1),) + block, parts.dtype),
            pltpu.VMEM((forward_hops,) + block, parts.dtype),
            pltpu.VMEM((max(backward_hops, 1),) + block, parts.dtype),
            pltpu.SemaphoreType.DMA((sends,)),
            pltpu.SemaphoreType.DMA((slots, len(widths))),
        ],
        compiler_params=pltpu.CompilerParams(collective_id=1, has_side_effects=True),
    )(parts)


def expert_partial(flat_rows, w_gate, w_up, w_down):
    gate_part = jnp.dot(flat_rows, w_gate[0], preferred_element_type=jnp.float32)
    up_part = jnp.dot(flat_rows, w_up[0], preferred_element_type=jnp.float32)
    hidden = lax.optimization_barrier((jax.nn.silu(gate_part) * up_part).astype(jnp.bfloat16))
    return jnp.dot(hidden, w_down[0], preferred_element_type=jnp.float32)


def per_device(queries, cache, lengths, live_rows, tokens, ids, gates, w_gate, w_up, w_down):
    context = attend(queries, cache, lengths, live_rows[0])
    group_count = lax.axis_size("grp")
    peer_count = lax.axis_size("ep")
    pair_count = peer_count // 2
    row_count = tokens.shape[0]
    feature = tokens.shape[1]
    expert_slots = group_count * CAP
    slot_count = pair_count * expert_slots
    column_rows = group_count * row_count

    gate_high = gates.astype(jnp.bfloat16)
    gate_low = (gates - gate_high.astype(jnp.float32)).astype(jnp.bfloat16)
    meta = jnp.concatenate([ids.astype(jnp.bfloat16), gate_high, gate_low], axis=1)
    meta = jnp.pad(meta, ((0, 0), (0, 128 - meta.shape[1])))
    gathered, gathered_meta = ring_gather(tokens, meta, group_count)
    all_tokens = gathered.reshape(column_rows, feature)
    packed = gathered_meta.reshape(column_rows, meta.shape[1])
    all_ids = packed[:, :TOPK].astype(jnp.int32)
    all_gates = packed[:, TOPK : 2 * TOPK].astype(jnp.float32) + packed[
        :, 2 * TOPK : 3 * TOPK
    ].astype(jnp.float32)

    my_group = lax.axis_index("grp")
    local = all_ids - pair_count * my_group
    experts = jnp.arange(pair_count, dtype=jnp.int32)
    pick_hot = (local[:, :, None] == experts[None, None, :]).astype(jnp.int32)
    token_hot = jnp.sum(pick_hot, axis=1)
    gate_of = jnp.sum(all_gates[:, :, None] * pick_hot.astype(jnp.float32), axis=1)
    blocks = token_hot.reshape(group_count, row_count, pair_count)
    earlier = (jnp.cumsum(blocks, axis=1) - blocks).reshape(column_rows, pair_count)
    source = jnp.arange(column_rows, dtype=jnp.int32)[:, None] // row_count
    slot_id = experts[None, :] * expert_slots + source * CAP + earlier
    slot_id = jnp.where(token_hot > 0, slot_id, slot_count)
    slots = jnp.arange(slot_count, dtype=jnp.int32)
    match = slot_id[:, :, None] == slots[None, None, :]
    dispatch = jnp.any(match, axis=1).T.astype(jnp.bfloat16)
    combine = jnp.sum(jnp.where(match, gate_of[:, :, None], 0.0), axis=1)

    outgoing = jnp.dot(dispatch, all_tokens, preferred_element_type=jnp.float32).astype(
        jnp.bfloat16
    )
    doubled = jnp.repeat(outgoing.reshape(pair_count, expert_slots, feature), 2, axis=0)
    arriving = lax.all_to_all(doubled, "ep", split_axis=0, concat_axis=0, tiled=True)
    partials = expert_partial(
        arriving.reshape(peer_count * expert_slots, feature), w_gate, w_up, w_down
    ).astype(jnp.bfloat16)
    returned = lax.all_to_all(
        partials.reshape(peer_count, expert_slots, feature),
        "ep",
        split_axis=0,
        concat_axis=0,
        tiled=True,
    )
    expert_out = (
        returned.reshape(pair_count, 2, expert_slots, feature)
        .astype(jnp.float32)
        .sum(axis=1)
        .astype(jnp.bfloat16)
        .reshape(slot_count, feature)
    )
    weight_high = combine.astype(jnp.bfloat16)
    weight_low = (combine - weight_high.astype(jnp.float32)).astype(jnp.bfloat16)
    column_mixed = jnp.dot(weight_high, expert_out, preferred_element_type=jnp.float32) + jnp.dot(
        weight_low, expert_out, preferred_element_type=jnp.float32
    )
    mixed = ring_scatter(
        column_mixed.astype(jnp.bfloat16).reshape(group_count, row_count, feature), group_count
    )
    return (context, mixed)


def solution(mesh):
    in_specs = (
        P(("grp", "ep"), None, None),
        P(("grp", "ep"), None, None),
        P(("grp", "ep")),
        P(("grp", "ep")),
        P(("grp", "ep"), None),
        P(("grp", "ep"), None),
        P(("grp", "ep"), None),
        P(("grp", "ep"), None, None),
        P(("grp", "ep"), None, None),
        P(("grp", "ep"), None, None),
    )
    out_specs = (P(("grp", "ep"), None, None), P(("grp", "ep"), None))
    return jax.shard_map(
        per_device, mesh=mesh, in_specs=in_specs, out_specs=out_specs, check_vma=False
    )
```

```python
import functools

import jax
import jax.numpy as jnp
from jax import lax
from jax.experimental import pallas as pl
from jax.experimental.pallas import tpu as pltpu
from jax.sharding import PartitionSpec as P

MESH = pl.DeviceIdType.MESH
CHUNKS = 4
TOPK = 8
LAT = 512
CAP = 2


score_scale = 192.0 ** (-0.5)
neg_large = -1e30


def attend(queries, cache, lengths, live_count):
    scores = (
        jnp.einsum("rhc,rlc->rhl", queries, cache, preferred_element_type=jnp.float32) * score_scale
    )
    positions = lax.broadcasted_iota(jnp.int32, scores.shape, 2)
    inside = positions < lengths[:, None, None]
    masked = jnp.where(inside, scores, neg_large)
    highest = jnp.max(masked, axis=2, keepdims=True)
    powers = jnp.where(inside, jnp.exp(masked - highest), 0.0)
    totals = jnp.sum(powers, axis=2, keepdims=True)
    weights = (powers / totals).astype(jnp.bfloat16)
    context = jnp.einsum(
        "rhl,rlc->rhc", weights, cache[:, :, :LAT], preferred_element_type=jnp.float32
    ).astype(jnp.bfloat16)
    request_slot = lax.broadcasted_iota(jnp.int32, context.shape, 0)
    return jnp.where(request_slot < live_count, context, jnp.zeros_like(context))


def gather_kernel(chips, windows, x_ref, m_ref, out_ref, mout_ref, send_sem, recv_sem):
    group = lax.axis_index("grp")
    peer_col = lax.axis_index("ep")
    z = group // 2
    core = group % 2
    right = lax.rem(z + 1, chips) * 2 + core
    left = lax.rem(z + chips - 1, chips) * 2 + core
    partner = z * 2 + (1 - core)
    sources = (x_ref, m_ref)
    targets = (out_ref, mout_ref)

    barrier = pltpu.get_barrier_semaphore()
    for peer in (left, right, partner):
        pl.semaphore_signal(barrier, inc=1, device_id=(peer, peer_col), device_id_type=MESH)
    pl.semaphore_wait(barrier, 3)

    started = []

    def window(refs, origin, piece):
        which, start, width = windows[piece]
        columns = pl.ds(start, width)
        if origin is None:
            return refs[which].at[:, columns]
        return refs[which].at[origin, :, columns]

    def send(origin, piece, peer, from_input):
        copy = pltpu.make_async_remote_copy(
            src_ref=window(sources, None, piece) if from_input else window(targets, origin, piece),
            dst_ref=window(targets, origin, piece),
            send_sem=send_sem.at[len(started)],
            recv_sem=recv_sem.at[origin, piece],
            device_id=(peer, peer_col),
            device_id_type=MESH,
        )
        copy.start()
        started.append(copy)

    def arrive(origin, piece, peer):
        pltpu.make_async_remote_copy(
            src_ref=window(targets, origin, piece),
            dst_ref=window(targets, origin, piece),
            send_sem=send_sem.at[0],
            recv_sem=recv_sem.at[origin, piece],
            device_id=(peer, peer_col),
            device_id_type=MESH,
        ).wait_recv()

    for piece in range(len(windows)):
        send(group, piece, right, True)
        send(group, piece, left, True)
        send(group, piece, partner, True)
    out_ref[group] = x_ref[...]
    mout_ref[group] = m_ref[...]
    forward_hops = chips // 2
    backward_hops = (chips - 1) // 2
    for step in range(1, forward_hops + 1):
        origin = lax.rem(z + chips - step, chips) * 2 + core
        for piece in range(len(windows)):
            arrive(origin, piece, left)
            if step < forward_hops:
                send(origin, piece, right, False)
            send(origin, piece, partner, False)
        if step <= backward_hops:
            origin = lax.rem(z + step, chips) * 2 + core
            for piece in range(len(windows)):
                arrive(origin, piece, right)
                if step < backward_hops:
                    send(origin, piece, left, False)
                send(origin, piece, partner, False)
    for other in range(chips):
        for piece in range(len(windows)):
            arrive(other * 2 + (1 - core), piece, partner)
    for copy in started:
        copy.wait_send()


def send_count(chips):
    forward_hops = chips // 2
    backward_hops = (chips - 1) // 2
    return 3 + 2 * forward_hops - 1 + 2 * backward_hops - 1


def ring_gather(block, meta, group_count):
    chips = group_count // 2
    lanes = block.shape[1] // 128
    windows = tuple(
        (0, lanes * piece // CHUNKS * 128, (lanes * (piece + 1) // CHUNKS - lanes * piece // CHUNKS) * 128)
        for piece in range(CHUNKS)
    ) + ((1, 0, meta.shape[1]),)
    return pl.pallas_call(
        functools.partial(gather_kernel, chips, windows),
        out_shape=(
            jax.ShapeDtypeStruct((group_count,) + block.shape, block.dtype),
            jax.ShapeDtypeStruct((group_count,) + meta.shape, meta.dtype),
        ),
        in_specs=[pl.BlockSpec(memory_space=pltpu.VMEM)] * 2,
        out_specs=(pl.BlockSpec(memory_space=pltpu.VMEM),) * 2,
        scratch_shapes=[
            pltpu.SemaphoreType.DMA((send_count(chips) * len(windows),)),
            pltpu.SemaphoreType.DMA((group_count, len(windows))),
        ],
        compiler_params=pltpu.CompilerParams(collective_id=0, has_side_effects=True),
    )(block, meta)


def scatter_kernel(
    chips, widths, parts_ref, out_ref, early, forward_in, backward_in, forward_out, backward_out,
    send_sem, recv_sem,
):
    group = lax.axis_index("grp")
    peer_col = lax.axis_index("ep")
    z = group // 2
    core = group % 2
    right = lax.rem(z + 1, chips) * 2 + core
    left = lax.rem(z + chips - 1, chips) * 2 + core
    partner = z * 2 + (1 - core)
    forward_hops = chips // 2
    backward_hops = (chips - 1) // 2
    starts = [sum(widths[:piece]) for piece in range(len(widths))]
    pieces = range(len(widths))

    def cols(piece):
        return pl.ds(starts[piece], widths[piece])

    barrier = pltpu.get_barrier_semaphore()
    for peer in (left, right, partner):
        pl.semaphore_signal(barrier, inc=1, device_id=(peer, peer_col), device_id_type=MESH)
    pl.semaphore_wait(barrier, 3)

    started = []

    def copy_of(src, dst, peer, slot, piece, number):
        return pltpu.make_async_remote_copy(
            src_ref=src,
            dst_ref=dst,
            send_sem=send_sem.at[number],
            recv_sem=recv_sem.at[slot, piece],
            device_id=(peer, peer_col),
            device_id_type=MESH,
        )

    def send(src, dst, peer, slot, piece):
        copy = copy_of(src, dst, peer, slot, piece, len(started))
        copy.start()
        started.append(copy)

    def arrive(dst, peer, slot, piece):
        copy_of(dst, dst, peer, slot, piece, 0).wait_recv()

    for other in range(chips):
        for piece in pieces:
            send(
                parts_ref.at[other * 2 + (1 - core), :, cols(piece)],
                early.at[other, :, cols(piece)],
                partner,
                other,
                piece,
            )
    for other in range(chips):
        for piece in pieces:
            arrive(early.at[other, :, cols(piece)], partner, other, piece)

    def chip_part(chip, piece):
        return parts_ref[chip * 2 + core, :, cols(piece)].astype(jnp.float32) + early[
            chip, :, cols(piece)
        ].astype(jnp.float32)

    def hop(step, chip, inbox, outbox, source, dest, first_slot, piece):
        value = chip_part(chip, piece)
        if step > 0:
            arrive(inbox.at[step - 1, :, cols(piece)], source, first_slot + step - 1, piece)
            value = value + inbox[step - 1, :, cols(piece)].astype(jnp.float32)
        outbox[step, :, cols(piece)] = value.astype(outbox.dtype)
        send(outbox.at[step, :, cols(piece)], inbox.at[step, :, cols(piece)], dest, first_slot + step, piece)

    for step in range(forward_hops):
        chip = lax.rem(z + forward_hops - step, chips)
        for piece in pieces:
            hop(step, chip, forward_in, forward_out, left, right, chips, piece)
        if step < backward_hops:
            chip = lax.rem(z + chips - backward_hops + step, chips)
            for piece in pieces:
                hop(step, chip, backward_in, backward_out, right, left, chips + forward_hops, piece)
    for piece in pieces:
        arrive(forward_in.at[forward_hops - 1, :, cols(piece)], left, chips + forward_hops - 1, piece)
        total = chip_part(z, piece) + forward_in[forward_hops - 1, :, cols(piece)].astype(
            jnp.float32
        )
        if backward_hops > 0:
            last = chips + forward_hops + backward_hops - 1
            arrive(backward_in.at[backward_hops - 1, :, cols(piece)], right, last, piece)
            total = total + backward_in[backward_hops - 1, :, cols(piece)].astype(jnp.float32)
        out_ref[:, cols(piece)] = total.astype(out_ref.dtype)
    for copy in started:
        copy.wait_send()


def ring_scatter(parts, group_count):
    chips = group_count // 2
    forward_hops = chips // 2
    backward_hops = (chips - 1) // 2
    block = parts.shape[1:]
    lanes = block[1] // 128
    widths = tuple(
        (lanes * (piece + 1) // CHUNKS - lanes * piece // CHUNKS) * 128 for piece in range(CHUNKS)
    )
    slots = chips + forward_hops + backward_hops
    sends = (chips + forward_hops + backward_hops) * len(widths)
    return pl.pallas_call(
        functools.partial(scatter_kernel, chips, widths),
        out_shape=jax.ShapeDtypeStruct(block, parts.dtype),
        in_specs=[pl.BlockSpec(memory_space=pltpu.VMEM)],
        out_specs=pl.BlockSpec(memory_space=pltpu.VMEM),
        scratch_shapes=[
            pltpu.VMEM((chips,) + block, parts.dtype),
            pltpu.VMEM((forward_hops,) + block, parts.dtype),
            pltpu.VMEM((max(backward_hops, 1),) + block, parts.dtype),
            pltpu.VMEM((forward_hops,) + block, parts.dtype),
            pltpu.VMEM((max(backward_hops, 1),) + block, parts.dtype),
            pltpu.SemaphoreType.DMA((sends,)),
            pltpu.SemaphoreType.DMA((slots, len(widths))),
        ],
        compiler_params=pltpu.CompilerParams(collective_id=1, has_side_effects=True),
    )(parts)


def expert_partial(flat_rows, w_gate, w_up, w_down):
    gate_part = jnp.dot(flat_rows, w_gate[0], preferred_element_type=jnp.float32)
    up_part = jnp.dot(flat_rows, w_up[0], preferred_element_type=jnp.float32)
    hidden = lax.optimization_barrier((jax.nn.silu(gate_part) * up_part).astype(jnp.bfloat16))
    return jnp.dot(hidden, w_down[0], preferred_element_type=jnp.float32)


def per_device(queries, cache, lengths, live_rows, tokens, ids, gates, w_gate, w_up, w_down):
    context = attend(queries, cache, lengths, live_rows[0])
    group_count = lax.axis_size("grp")
    peer_count = lax.axis_size("ep")
    pair_count = peer_count // 2
    row_count = tokens.shape[0]
    feature = tokens.shape[1]
    expert_slots = group_count * CAP
    slot_count = pair_count * expert_slots
    column_rows = group_count * row_count

    meta = jnp.concatenate([ids.astype(jnp.float32), gates], axis=1)
    meta = jnp.pad(meta, ((0, 0), (0, 128 - meta.shape[1])))
    gathered, gathered_meta = ring_gather(tokens, meta, group_count)
    all_tokens = gathered.reshape(column_rows, feature)
    packed = gathered_meta.reshape(column_rows, meta.shape[1])
    all_ids = packed[:, :TOPK].astype(jnp.int32)
    all_gates = packed[:, TOPK : 2 * TOPK]

    my_group = lax.axis_index("grp")
    local = all_ids - pair_count * my_group
    experts = jnp.arange(pair_count, dtype=jnp.int32)
    pick_hot = (local[:, :, None] == experts[None, None, :]).astype(jnp.int32)
    token_hot = jnp.sum(pick_hot, axis=1)
    gate_of = jnp.sum(all_gates[:, :, None] * pick_hot.astype(jnp.float32), axis=1)
    blocks = token_hot.reshape(group_count, row_count, pair_count)
    earlier = (jnp.cumsum(blocks, axis=1) - blocks).reshape(column_rows, pair_count)
    source = jnp.arange(column_rows, dtype=jnp.int32)[:, None] // row_count
    slot_id = experts[None, :] * expert_slots + source * CAP + earlier
    slot_id = jnp.where(token_hot > 0, slot_id, slot_count)
    slots = jnp.arange(slot_count, dtype=jnp.int32)
    match = slot_id[:, :, None] == slots[None, None, :]
    dispatch = jnp.any(match, axis=1).T.astype(jnp.bfloat16)
    combine = jnp.sum(jnp.where(match, gate_of[:, :, None], 0.0), axis=1)

    outgoing = jnp.dot(dispatch, all_tokens, preferred_element_type=jnp.float32).astype(
        jnp.bfloat16
    )
    doubled = jnp.repeat(outgoing.reshape(pair_count, expert_slots, feature), 2, axis=0)
    arriving = lax.all_to_all(doubled, "ep", split_axis=0, concat_axis=0, tiled=True)
    partials = expert_partial(
        arriving.reshape(peer_count * expert_slots, feature), w_gate, w_up, w_down
    ).astype(jnp.bfloat16)
    returned = lax.all_to_all(
        partials.reshape(peer_count, expert_slots, feature),
        "ep",
        split_axis=0,
        concat_axis=0,
        tiled=True,
    )
    expert_out = (
        returned.reshape(pair_count, 2, expert_slots, feature)
        .astype(jnp.float32)
        .sum(axis=1)
        .astype(jnp.bfloat16)
        .reshape(slot_count, feature)
    )
    weight_high = combine.astype(jnp.bfloat16)
    weight_low = (combine - weight_high.astype(jnp.float32)).astype(jnp.bfloat16)
    column_mixed = jnp.dot(weight_high, expert_out, preferred_element_type=jnp.float32) + jnp.dot(
        weight_low, expert_out, preferred_element_type=jnp.float32
    )
    mixed = ring_scatter(
        column_mixed.astype(jnp.bfloat16).reshape(group_count, row_count, feature), group_count
    )
    return (context, mixed)


def solution(mesh):
    in_specs = (
        P(("grp", "ep"), None, None),
        P(("grp", "ep"), None, None),
        P(("grp", "ep")),
        P(("grp", "ep")),
        P(("grp", "ep"), None),
        P(("grp", "ep"), None),
        P(("grp", "ep"), None),
        P(("grp", "ep"), None, None),
        P(("grp", "ep"), None, None),
        P(("grp", "ep"), None, None),
    )
    out_specs = (P(("grp", "ep"), None, None), P(("grp", "ep"), None))
    return jax.shard_map(
        per_device, mesh=mesh, in_specs=in_specs, out_specs=out_specs, check_vma=False
    )
```

```python
import functools

import jax
import jax.numpy as jnp
from jax import lax
from jax.experimental import pallas as pl
from jax.experimental.pallas import tpu as pltpu
from jax.sharding import PartitionSpec as P

MESH = pl.DeviceIdType.MESH
CHUNKS = 4
TOPK = 8
LAT = 512
CAP = 2


score_scale = 192.0 ** (-0.5)
neg_large = -1e30


def attend(queries, cache, lengths, live_count):
    scores = (
        jnp.einsum("rhc,rlc->rhl", queries, cache, preferred_element_type=jnp.float32) * score_scale
    )
    positions = lax.broadcasted_iota(jnp.int32, scores.shape, 2)
    inside = positions < lengths[:, None, None]
    masked = jnp.where(inside, scores, neg_large)
    highest = jnp.max(masked, axis=2, keepdims=True)
    powers = jnp.where(inside, jnp.exp(masked - highest), 0.0)
    totals = jnp.sum(powers, axis=2, keepdims=True)
    weights = (powers / totals).astype(jnp.bfloat16)
    context = jnp.einsum(
        "rhl,rlc->rhc", weights, cache[:, :, :LAT], preferred_element_type=jnp.float32
    ).astype(jnp.bfloat16)
    request_slot = lax.broadcasted_iota(jnp.int32, context.shape, 0)
    return jnp.where(request_slot < live_count, context, jnp.zeros_like(context))


def gather_kernel(
    chips, windows, x_ref, i_ref, g_ref, out_ref, iout_ref, gout_ref, send_sem, recv_sem
):
    group = lax.axis_index("grp")
    peer_col = lax.axis_index("ep")
    z = group // 2
    core = group % 2
    right = lax.rem(z + 1, chips) * 2 + core
    left = lax.rem(z + chips - 1, chips) * 2 + core
    partner = z * 2 + (1 - core)
    sources = (x_ref, i_ref, g_ref)
    targets = (out_ref, iout_ref, gout_ref)

    barrier = pltpu.get_barrier_semaphore()
    for peer in (left, right, partner):
        pl.semaphore_signal(barrier, inc=1, device_id=(peer, peer_col), device_id_type=MESH)
    pl.semaphore_wait(barrier, 3)

    started = []

    def window(refs, origin, piece):
        which, start, width = windows[piece]
        columns = pl.ds(start, width)
        if origin is None:
            return refs[which].at[:, columns]
        return refs[which].at[origin, :, columns]

    def send(origin, piece, peer, from_input):
        copy = pltpu.make_async_remote_copy(
            src_ref=window(sources, None, piece) if from_input else window(targets, origin, piece),
            dst_ref=window(targets, origin, piece),
            send_sem=send_sem.at[len(started)],
            recv_sem=recv_sem.at[origin, piece],
            device_id=(peer, peer_col),
            device_id_type=MESH,
        )
        copy.start()
        started.append(copy)

    def arrive(origin, piece, peer):
        pltpu.make_async_remote_copy(
            src_ref=window(targets, origin, piece),
            dst_ref=window(targets, origin, piece),
            send_sem=send_sem.at[0],
            recv_sem=recv_sem.at[origin, piece],
            device_id=(peer, peer_col),
            device_id_type=MESH,
        ).wait_recv()

    for piece in range(len(windows)):
        send(group, piece, right, True)
        send(group, piece, left, True)
        send(group, piece, partner, True)
    for source, target in zip(sources, targets):
        target[group] = source[...]
    forward_hops = chips // 2
    backward_hops = (chips - 1) // 2
    for step in range(1, forward_hops + 1):
        origin = lax.rem(z + chips - step, chips) * 2 + core
        for piece in range(len(windows)):
            arrive(origin, piece, left)
            if step < forward_hops:
                send(origin, piece, right, False)
            send(origin, piece, partner, False)
        if step <= backward_hops:
            origin = lax.rem(z + step, chips) * 2 + core
            for piece in range(len(windows)):
                arrive(origin, piece, right)
                if step < backward_hops:
                    send(origin, piece, left, False)
                send(origin, piece, partner, False)
    for other in range(chips):
        for piece in range(len(windows)):
            arrive(other * 2 + (1 - core), piece, partner)
    for copy in started:
        copy.wait_send()


def send_count(chips):
    forward_hops = chips // 2
    backward_hops = (chips - 1) // 2
    return 3 + 2 * forward_hops - 1 + 2 * backward_hops - 1


def ring_gather(block, ids, gates, group_count):
    chips = group_count // 2
    lanes = block.shape[1] // 128
    windows = tuple(
        (0, lanes * piece // CHUNKS * 128, (lanes * (piece + 1) // CHUNKS - lanes * piece // CHUNKS) * 128)
        for piece in range(CHUNKS)
    ) + ((1, 0, ids.shape[1]), (2, 0, gates.shape[1]))
    return pl.pallas_call(
        functools.partial(gather_kernel, chips, windows),
        out_shape=tuple(
            jax.ShapeDtypeStruct((group_count,) + part.shape, part.dtype)
            for part in (block, ids, gates)
        ),
        in_specs=[pl.BlockSpec(memory_space=pltpu.VMEM)] * 3,
        out_specs=(pl.BlockSpec(memory_space=pltpu.VMEM),) * 3,
        scratch_shapes=[
            pltpu.SemaphoreType.DMA((send_count(chips) * len(windows),)),
            pltpu.SemaphoreType.DMA((group_count, len(windows))),
        ],
        compiler_params=pltpu.CompilerParams(collective_id=0, has_side_effects=True),
    )(block, ids, gates)


def scatter_kernel(
    chips, widths, parts_ref, out_ref, early, forward_in, backward_in, forward_out, backward_out,
    send_sem, recv_sem,
):
    group = lax.axis_index("grp")
    peer_col = lax.axis_index("ep")
    z = group // 2
    core = group % 2
    right = lax.rem(z + 1, chips) * 2 + core
    left = lax.rem(z + chips - 1, chips) * 2 + core
    partner = z * 2 + (1 - core)
    forward_hops = chips // 2
    backward_hops = (chips - 1) // 2
    starts = [sum(widths[:piece]) for piece in range(len(widths))]
    pieces = range(len(widths))

    def cols(piece):
        return pl.ds(starts[piece], widths[piece])

    barrier = pltpu.get_barrier_semaphore()
    for peer in (left, right, partner):
        pl.semaphore_signal(barrier, inc=1, device_id=(peer, peer_col), device_id_type=MESH)
    pl.semaphore_wait(barrier, 3)

    started = []

    def copy_of(src, dst, peer, slot, piece, number):
        return pltpu.make_async_remote_copy(
            src_ref=src,
            dst_ref=dst,
            send_sem=send_sem.at[number],
            recv_sem=recv_sem.at[slot, piece],
            device_id=(peer, peer_col),
            device_id_type=MESH,
        )

    def send(src, dst, peer, slot, piece):
        copy = copy_of(src, dst, peer, slot, piece, len(started))
        copy.start()
        started.append(copy)

    def arrive(dst, peer, slot, piece):
        copy_of(dst, dst, peer, slot, piece, 0).wait_recv()

    for other in range(chips):
        for piece in pieces:
            send(
                parts_ref.at[other * 2 + (1 - core), :, cols(piece)],
                early.at[other, :, cols(piece)],
                partner,
                other,
                piece,
            )
    for other in range(chips):
        for piece in pieces:
            arrive(early.at[other, :, cols(piece)], partner, other, piece)

    def chip_part(chip, piece):
        return parts_ref[chip * 2 + core, :, cols(piece)].astype(jnp.float32) + early[
            chip, :, cols(piece)
        ].astype(jnp.float32)

    def hop(step, chip, inbox, outbox, source, dest, first_slot, piece):
        value = chip_part(chip, piece)
        if step > 0:
            arrive(inbox.at[step - 1, :, cols(piece)], source, first_slot + step - 1, piece)
            value = value + inbox[step - 1, :, cols(piece)].astype(jnp.float32)
        outbox[step, :, cols(piece)] = value.astype(outbox.dtype)
        send(outbox.at[step, :, cols(piece)], inbox.at[step, :, cols(piece)], dest, first_slot + step, piece)

    for step in range(forward_hops):
        chip = lax.rem(z + forward_hops - step, chips)
        for piece in pieces:
            hop(step, chip, forward_in, forward_out, left, right, chips, piece)
        if step < backward_hops:
            chip = lax.rem(z + chips - backward_hops + step, chips)
            for piece in pieces:
                hop(step, chip, backward_in, backward_out, right, left, chips + forward_hops, piece)
    for piece in pieces:
        arrive(forward_in.at[forward_hops - 1, :, cols(piece)], left, chips + forward_hops - 1, piece)
        total = chip_part(z, piece) + forward_in[forward_hops - 1, :, cols(piece)].astype(
            jnp.float32
        )
        if backward_hops > 0:
            last = chips + forward_hops + backward_hops - 1
            arrive(backward_in.at[backward_hops - 1, :, cols(piece)], right, last, piece)
            total = total + backward_in[backward_hops - 1, :, cols(piece)].astype(jnp.float32)
        out_ref[:, cols(piece)] = total.astype(out_ref.dtype)
    for copy in started:
        copy.wait_send()


def ring_scatter(parts, group_count):
    chips = group_count // 2
    forward_hops = chips // 2
    backward_hops = (chips - 1) // 2
    block = parts.shape[1:]
    lanes = block[1] // 128
    widths = tuple(
        (lanes * (piece + 1) // CHUNKS - lanes * piece // CHUNKS) * 128 for piece in range(CHUNKS)
    )
    slots = chips + forward_hops + backward_hops
    sends = (chips + forward_hops + backward_hops) * len(widths)
    return pl.pallas_call(
        functools.partial(scatter_kernel, chips, widths),
        out_shape=jax.ShapeDtypeStruct(block, parts.dtype),
        in_specs=[pl.BlockSpec(memory_space=pltpu.VMEM)],
        out_specs=pl.BlockSpec(memory_space=pltpu.VMEM),
        scratch_shapes=[
            pltpu.VMEM((chips,) + block, parts.dtype),
            pltpu.VMEM((forward_hops,) + block, parts.dtype),
            pltpu.VMEM((max(backward_hops, 1),) + block, parts.dtype),
            pltpu.VMEM((forward_hops,) + block, parts.dtype),
            pltpu.VMEM((max(backward_hops, 1),) + block, parts.dtype),
            pltpu.SemaphoreType.DMA((sends,)),
            pltpu.SemaphoreType.DMA((slots, len(widths))),
        ],
        compiler_params=pltpu.CompilerParams(collective_id=1, has_side_effects=True),
    )(parts)


def expert_partial(flat_rows, w_gate, w_up, w_down):
    gate_part = jnp.dot(flat_rows, w_gate[0], preferred_element_type=jnp.float32)
    up_part = jnp.dot(flat_rows, w_up[0], preferred_element_type=jnp.float32)
    hidden = lax.optimization_barrier((jax.nn.silu(gate_part) * up_part).astype(jnp.bfloat16))
    return jnp.dot(hidden, w_down[0], preferred_element_type=jnp.float32)


def per_device(queries, cache, lengths, live_rows, tokens, ids, gates, w_gate, w_up, w_down):
    context = attend(queries, cache, lengths, live_rows[0])
    group_count = lax.axis_size("grp")
    peer_count = lax.axis_size("ep")
    pair_count = peer_count // 2
    row_count = tokens.shape[0]
    feature = tokens.shape[1]
    expert_slots = group_count * CAP
    slot_count = pair_count * expert_slots
    column_rows = group_count * row_count

    gathered, gathered_ids, gathered_gates = ring_gather(tokens, ids, gates, group_count)
    all_tokens = gathered.reshape(column_rows, feature)
    all_ids = gathered_ids.reshape(column_rows, TOPK)
    all_gates = gathered_gates.reshape(column_rows, TOPK)

    my_group = lax.axis_index("grp")
    local = all_ids - pair_count * my_group
    experts = jnp.arange(pair_count, dtype=jnp.int32)
    pick_hot = (local[:, :, None] == experts[None, None, :]).astype(jnp.int32)
    token_hot = jnp.sum(pick_hot, axis=1)
    gate_of = jnp.sum(all_gates[:, :, None] * pick_hot.astype(jnp.float32), axis=1)
    blocks = token_hot.reshape(group_count, row_count, pair_count)
    earlier = (jnp.cumsum(blocks, axis=1) - blocks).reshape(column_rows, pair_count)
    source = jnp.arange(column_rows, dtype=jnp.int32)[:, None] // row_count
    slot_id = experts[None, :] * expert_slots + source * CAP + earlier
    slot_id = jnp.where(token_hot > 0, slot_id, slot_count)
    slots = jnp.arange(slot_count, dtype=jnp.int32)
    match = slot_id[:, :, None] == slots[None, None, :]
    dispatch = jnp.any(match, axis=1).T.astype(jnp.bfloat16)
    combine = jnp.sum(jnp.where(match, gate_of[:, :, None], 0.0), axis=1)

    outgoing = jnp.dot(dispatch, all_tokens, preferred_element_type=jnp.float32).astype(
        jnp.bfloat16
    )
    doubled = jnp.repeat(outgoing.reshape(pair_count, expert_slots, feature), 2, axis=0)
    arriving = lax.all_to_all(doubled, "ep", split_axis=0, concat_axis=0, tiled=True)
    partials = expert_partial(
        arriving.reshape(peer_count * expert_slots, feature), w_gate, w_up, w_down
    ).astype(jnp.bfloat16)
    returned = lax.all_to_all(
        partials.reshape(peer_count, expert_slots, feature),
        "ep",
        split_axis=0,
        concat_axis=0,
        tiled=True,
    )
    expert_out = (
        returned.reshape(pair_count, 2, expert_slots, feature)
        .astype(jnp.float32)
        .sum(axis=1)
        .astype(jnp.bfloat16)
        .reshape(slot_count, feature)
    )
    weight_high = combine.astype(jnp.bfloat16)
    weight_low = (combine - weight_high.astype(jnp.float32)).astype(jnp.bfloat16)
    column_mixed = jnp.dot(weight_high, expert_out, preferred_element_type=jnp.float32) + jnp.dot(
        weight_low, expert_out, preferred_element_type=jnp.float32
    )
    mixed = ring_scatter(
        column_mixed.astype(jnp.bfloat16).reshape(group_count, row_count, feature), group_count
    )
    return (context, mixed)


def solution(mesh):
    in_specs = (
        P(("grp", "ep"), None, None),
        P(("grp", "ep"), None, None),
        P(("grp", "ep")),
        P(("grp", "ep")),
        P(("grp", "ep"), None),
        P(("grp", "ep"), None),
        P(("grp", "ep"), None),
        P(("grp", "ep"), None, None),
        P(("grp", "ep"), None, None),
        P(("grp", "ep"), None, None),
    )
    out_specs = (P(("grp", "ep"), None, None), P(("grp", "ep"), None))
    return jax.shard_map(
        per_device, mesh=mesh, in_specs=in_specs, out_specs=out_specs, check_vma=False
    )
```

```python
import functools

import jax
import jax.numpy as jnp
from jax import lax
from jax.experimental import pallas as pl
from jax.experimental.pallas import tpu as pltpu
from jax.sharding import PartitionSpec as P

MESH = pl.DeviceIdType.MESH
CHUNKS = 4
TOPK = 8
LAT = 512
CAP = 2


score_scale = 192.0 ** (-0.5)
neg_large = -1e30


def attend(queries, cache, lengths, live_count):
    scores = (
        jnp.einsum("rhc,rlc->rhl", queries, cache, preferred_element_type=jnp.float32) * score_scale
    )
    positions = lax.broadcasted_iota(jnp.int32, scores.shape, 2)
    inside = positions < lengths[:, None, None]
    masked = jnp.where(inside, scores, neg_large)
    highest = jnp.max(masked, axis=2, keepdims=True)
    powers = jnp.where(inside, jnp.exp(masked - highest), 0.0)
    totals = jnp.sum(powers, axis=2, keepdims=True)
    weights = (powers / totals).astype(jnp.bfloat16)
    context = jnp.einsum(
        "rhl,rlc->rhc", weights, cache[:, :, :LAT], preferred_element_type=jnp.float32
    ).astype(jnp.bfloat16)
    request_slot = lax.broadcasted_iota(jnp.int32, context.shape, 0)
    return jnp.where(request_slot < live_count, context, jnp.zeros_like(context))


def gather_kernel(chips, windows, x_ref, m_ref, out_ref, mout_ref, send_sem, recv_sem):
    group = lax.axis_index("grp")
    peer_col = lax.axis_index("ep")
    z = group // 2
    core = group % 2
    right = lax.rem(z + 1, chips) * 2 + core
    left = lax.rem(z + chips - 1, chips) * 2 + core
    partner = z * 2 + (1 - core)
    sources = (x_ref, m_ref)
    targets = (out_ref, mout_ref)

    barrier = pltpu.get_barrier_semaphore()
    for peer in (left, right, partner):
        pl.semaphore_signal(barrier, inc=1, device_id=(peer, peer_col), device_id_type=MESH)
    pl.semaphore_wait(barrier, 3)

    started = []

    def window(refs, origin, piece):
        which, start, width = windows[piece]
        columns = pl.ds(start, width)
        if origin is None:
            return refs[which].at[:, columns]
        return refs[which].at[origin, :, columns]

    def send(origin, piece, peer, from_input):
        copy = pltpu.make_async_remote_copy(
            src_ref=window(sources, None, piece) if from_input else window(targets, origin, piece),
            dst_ref=window(targets, origin, piece),
            send_sem=send_sem.at[len(started)],
            recv_sem=recv_sem.at[origin, piece],
            device_id=(peer, peer_col),
            device_id_type=MESH,
        )
        copy.start()
        started.append(copy)

    def arrive(origin, piece, peer):
        pltpu.make_async_remote_copy(
            src_ref=window(targets, origin, piece),
            dst_ref=window(targets, origin, piece),
            send_sem=send_sem.at[0],
            recv_sem=recv_sem.at[origin, piece],
            device_id=(peer, peer_col),
            device_id_type=MESH,
        ).wait_recv()

    for piece in range(len(windows)):
        send(group, piece, right, True)
        send(group, piece, left, True)
        send(group, piece, partner, True)
    out_ref[group] = x_ref[...]
    mout_ref[group] = m_ref[...]
    forward_hops = chips // 2
    backward_hops = (chips - 1) // 2
    for step in range(1, forward_hops + 1):
        origin = lax.rem(z + chips - step, chips) * 2 + core
        for piece in range(len(windows)):
            arrive(origin, piece, left)
            if step < forward_hops:
                send(origin, piece, right, False)
            send(origin, piece, partner, False)
        if step <= backward_hops:
            origin = lax.rem(z + step, chips) * 2 + core
            for piece in range(len(windows)):
                arrive(origin, piece, right)
                if step < backward_hops:
                    send(origin, piece, left, False)
                send(origin, piece, partner, False)
    for other in range(chips):
        for piece in range(len(windows)):
            arrive(other * 2 + (1 - core), piece, partner)
    for copy in started:
        copy.wait_send()


def send_count(chips):
    forward_hops = chips // 2
    backward_hops = (chips - 1) // 2
    return 3 + 2 * forward_hops - 1 + 2 * backward_hops - 1


def ring_gather(block, meta, group_count):
    chips = group_count // 2
    lanes = block.shape[1] // 128
    windows = tuple(
        (0, lanes * piece // CHUNKS * 128, (lanes * (piece + 1) // CHUNKS - lanes * piece // CHUNKS) * 128)
        for piece in range(CHUNKS)
    ) + ((1, 0, meta.shape[1]),)
    return pl.pallas_call(
        functools.partial(gather_kernel, chips, windows),
        out_shape=(
            jax.ShapeDtypeStruct((group_count,) + block.shape, block.dtype),
            jax.ShapeDtypeStruct((group_count,) + meta.shape, meta.dtype),
        ),
        in_specs=[pl.BlockSpec(memory_space=pltpu.VMEM)] * 2,
        out_specs=(pl.BlockSpec(memory_space=pltpu.VMEM),) * 2,
        scratch_shapes=[
            pltpu.SemaphoreType.DMA((send_count(chips) * len(windows),)),
            pltpu.SemaphoreType.DMA((group_count, len(windows))),
        ],
        compiler_params=pltpu.CompilerParams(collective_id=0, has_side_effects=True),
    )(block, meta)


def scatter_kernel(
    chips, widths, parts_ref, out_ref, early, forward_in, backward_in, forward_out, backward_out,
    send_sem, recv_sem,
):
    group = lax.axis_index("grp")
    peer_col = lax.axis_index("ep")
    z = group // 2
    core = group % 2
    right = lax.rem(z + 1, chips) * 2 + core
    left = lax.rem(z + chips - 1, chips) * 2 + core
    partner = z * 2 + (1 - core)
    forward_hops = chips // 2
    backward_hops = (chips - 1) // 2
    starts = [sum(widths[:piece]) for piece in range(len(widths))]
    pieces = range(len(widths))

    def cols(piece):
        return pl.ds(starts[piece], widths[piece])

    barrier = pltpu.get_barrier_semaphore()
    for peer in (left, right, partner):
        pl.semaphore_signal(barrier, inc=1, device_id=(peer, peer_col), device_id_type=MESH)
    pl.semaphore_wait(barrier, 3)

    started = []

    def copy_of(src, dst, peer, slot, piece, number):
        return pltpu.make_async_remote_copy(
            src_ref=src,
            dst_ref=dst,
            send_sem=send_sem.at[number],
            recv_sem=recv_sem.at[slot, piece],
            device_id=(peer, peer_col),
            device_id_type=MESH,
        )

    def send(src, dst, peer, slot, piece):
        copy = copy_of(src, dst, peer, slot, piece, len(started))
        copy.start()
        started.append(copy)

    def arrive(dst, peer, slot, piece):
        copy_of(dst, dst, peer, slot, piece, 0).wait_recv()

    for other in range(chips):
        for piece in pieces:
            send(
                parts_ref.at[other * 2 + (1 - core), :, cols(piece)],
                early.at[other, :, cols(piece)],
                partner,
                other,
                piece,
            )
    for other in range(chips):
        for piece in pieces:
            arrive(early.at[other, :, cols(piece)], partner, other, piece)

    def chip_part(chip, piece):
        return parts_ref[chip * 2 + core, :, cols(piece)].astype(jnp.float32) + early[
            chip, :, cols(piece)
        ].astype(jnp.float32)

    def hop(step, chip, inbox, outbox, source, dest, first_slot, piece):
        value = chip_part(chip, piece)
        if step > 0:
            arrive(inbox.at[step - 1, :, cols(piece)], source, first_slot + step - 1, piece)
            value = value + inbox[step - 1, :, cols(piece)].astype(jnp.float32)
        outbox[step, :, cols(piece)] = value.astype(outbox.dtype)
        send(outbox.at[step, :, cols(piece)], inbox.at[step, :, cols(piece)], dest, first_slot + step, piece)

    for step in range(forward_hops):
        chip = lax.rem(z + forward_hops - step, chips)
        for piece in pieces:
            hop(step, chip, forward_in, forward_out, left, right, chips, piece)
        if step < backward_hops:
            chip = lax.rem(z + chips - backward_hops + step, chips)
            for piece in pieces:
                hop(step, chip, backward_in, backward_out, right, left, chips + forward_hops, piece)
    for piece in pieces:
        arrive(forward_in.at[forward_hops - 1, :, cols(piece)], left, chips + forward_hops - 1, piece)
        total = chip_part(z, piece) + forward_in[forward_hops - 1, :, cols(piece)].astype(
            jnp.float32
        )
        if backward_hops > 0:
            last = chips + forward_hops + backward_hops - 1
            arrive(backward_in.at[backward_hops - 1, :, cols(piece)], right, last, piece)
            total = total + backward_in[backward_hops - 1, :, cols(piece)].astype(jnp.float32)
        out_ref[:, cols(piece)] = total.astype(out_ref.dtype)
    for copy in started:
        copy.wait_send()


def ring_scatter(parts, group_count):
    chips = group_count // 2
    forward_hops = chips // 2
    backward_hops = (chips - 1) // 2
    block = parts.shape[1:]
    lanes = block[1] // 128
    widths = tuple(
        (lanes * (piece + 1) // CHUNKS - lanes * piece // CHUNKS) * 128 for piece in range(CHUNKS)
    )
    slots = chips + forward_hops + backward_hops
    sends = (chips + forward_hops + backward_hops) * len(widths)
    return pl.pallas_call(
        functools.partial(scatter_kernel, chips, widths),
        out_shape=jax.ShapeDtypeStruct(block, jnp.float32),
        in_specs=[pl.BlockSpec(memory_space=pltpu.VMEM)],
        out_specs=pl.BlockSpec(memory_space=pltpu.VMEM),
        scratch_shapes=[
            pltpu.VMEM((chips,) + block, parts.dtype),
            pltpu.VMEM((forward_hops,) + block, parts.dtype),
            pltpu.VMEM((max(backward_hops, 1),) + block, parts.dtype),
            pltpu.VMEM((forward_hops,) + block, parts.dtype),
            pltpu.VMEM((max(backward_hops, 1),) + block, parts.dtype),
            pltpu.SemaphoreType.DMA((sends,)),
            pltpu.SemaphoreType.DMA((slots, len(widths))),
        ],
        compiler_params=pltpu.CompilerParams(collective_id=1, has_side_effects=True),
    )(parts)


def expert_partial(flat_rows, w_gate, w_up, w_down):
    gate_part = jnp.dot(flat_rows, w_gate[0], preferred_element_type=jnp.float32)
    up_part = jnp.dot(flat_rows, w_up[0], preferred_element_type=jnp.float32)
    hidden = lax.optimization_barrier((jax.nn.silu(gate_part) * up_part).astype(jnp.bfloat16))
    return jnp.dot(hidden, w_down[0], preferred_element_type=jnp.float32)


def per_device(queries, cache, lengths, live_rows, tokens, ids, gates, w_gate, w_up, w_down):
    context = attend(queries, cache, lengths, live_rows[0])
    group_count = lax.axis_size("grp")
    peer_count = lax.axis_size("ep")
    pair_count = peer_count // 2
    row_count = tokens.shape[0]
    feature = tokens.shape[1]
    expert_slots = group_count * CAP
    slot_count = pair_count * expert_slots
    column_rows = group_count * row_count

    meta = jnp.concatenate([ids.astype(jnp.float32), gates], axis=1)
    meta = jnp.pad(meta, ((0, 0), (0, 128 - meta.shape[1])))
    gathered, gathered_meta = ring_gather(tokens, meta, group_count)
    all_tokens = gathered.reshape(column_rows, feature)
    packed = gathered_meta.reshape(column_rows, meta.shape[1])
    all_ids = packed[:, :TOPK].astype(jnp.int32)
    all_gates = packed[:, TOPK : 2 * TOPK]

    my_group = lax.axis_index("grp")
    local = all_ids - pair_count * my_group
    experts = jnp.arange(pair_count, dtype=jnp.int32)
    pick_hot = (local[:, :, None] == experts[None, None, :]).astype(jnp.int32)
    token_hot = jnp.sum(pick_hot, axis=1)
    gate_of = jnp.sum(all_gates[:, :, None] * pick_hot.astype(jnp.float32), axis=1)
    blocks = token_hot.reshape(group_count, row_count, pair_count)
    earlier = (jnp.cumsum(blocks, axis=1) - blocks).reshape(column_rows, pair_count)
    source = jnp.arange(column_rows, dtype=jnp.int32)[:, None] // row_count
    slot_id = experts[None, :] * expert_slots + source * CAP + earlier
    slot_id = jnp.where(token_hot > 0, slot_id, slot_count)
    slots = jnp.arange(slot_count, dtype=jnp.int32)
    match = slot_id[:, :, None] == slots[None, None, :]
    dispatch = jnp.any(match, axis=1).T.astype(jnp.bfloat16)
    combine = jnp.sum(jnp.where(match, gate_of[:, :, None], 0.0), axis=1)

    outgoing = jnp.dot(dispatch, all_tokens, preferred_element_type=jnp.float32).astype(
        jnp.bfloat16
    )
    doubled = jnp.repeat(outgoing.reshape(pair_count, expert_slots, feature), 2, axis=0)
    arriving = lax.all_to_all(doubled, "ep", split_axis=0, concat_axis=0, tiled=True)
    partials = expert_partial(
        arriving.reshape(peer_count * expert_slots, feature), w_gate, w_up, w_down
    ).astype(jnp.bfloat16)
    returned = lax.all_to_all(
        partials.reshape(peer_count, expert_slots, feature),
        "ep",
        split_axis=0,
        concat_axis=0,
        tiled=True,
    )
    expert_out = (
        returned.reshape(pair_count, 2, expert_slots, feature)
        .astype(jnp.float32)
        .sum(axis=1)
        .astype(jnp.bfloat16)
        .reshape(slot_count, feature)
    )
    weight_high = combine.astype(jnp.bfloat16)
    weight_low = (combine - weight_high.astype(jnp.float32)).astype(jnp.bfloat16)
    column_mixed = jnp.dot(weight_high, expert_out, preferred_element_type=jnp.float32) + jnp.dot(
        weight_low, expert_out, preferred_element_type=jnp.float32
    )
    mixed = ring_scatter(
        column_mixed.astype(jnp.bfloat16).reshape(group_count, row_count, feature), group_count
    ).astype(jnp.bfloat16)
    return (context, mixed)


def solution(mesh):
    in_specs = (
        P(("grp", "ep"), None, None),
        P(("grp", "ep"), None, None),
        P(("grp", "ep")),
        P(("grp", "ep")),
        P(("grp", "ep"), None),
        P(("grp", "ep"), None),
        P(("grp", "ep"), None),
        P(("grp", "ep"), None, None),
        P(("grp", "ep"), None, None),
        P(("grp", "ep"), None, None),
    )
    out_specs = (P(("grp", "ep"), None, None), P(("grp", "ep"), None))
    return jax.shard_map(
        per_device, mesh=mesh, in_specs=in_specs, out_specs=out_specs, check_vma=False
    )
```

```python
import functools

import jax
import jax.numpy as jnp
from jax import lax
from jax.experimental import pallas as pl
from jax.experimental.pallas import tpu as pltpu
from jax.sharding import PartitionSpec as P

MESH = pl.DeviceIdType.MESH
CHUNKS = 4
TOPK = 8
LAT = 512
CAP = 2


score_scale = 192.0 ** (-0.5)
neg_large = -1e30


def attend(queries, cache, lengths, live_count):
    scores = (
        jnp.einsum("rhc,rlc->rhl", queries, cache, preferred_element_type=jnp.float32) * score_scale
    )
    positions = lax.broadcasted_iota(jnp.int32, scores.shape, 2)
    inside = positions < lengths[:, None, None]
    masked = jnp.where(inside, scores, neg_large)
    highest = jnp.max(masked, axis=2, keepdims=True)
    powers = jnp.where(inside, jnp.exp(masked - highest), 0.0)
    totals = jnp.sum(powers, axis=2, keepdims=True)
    weights = (powers / totals).astype(jnp.bfloat16)
    context = jnp.einsum(
        "rhl,rlc->rhc", weights, cache[:, :, :LAT], preferred_element_type=jnp.float32
    ).astype(jnp.bfloat16)
    request_slot = lax.broadcasted_iota(jnp.int32, context.shape, 0)
    return jnp.where(request_slot < live_count, context, jnp.zeros_like(context))


def gather_kernel(chips, windows, x_ref, m_ref, out_ref, mout_ref, send_sem, recv_sem):
    group = lax.axis_index("grp")
    peer_col = lax.axis_index("ep")
    z = group // 2
    core = group % 2
    right = lax.rem(z + 1, chips) * 2 + core
    left = lax.rem(z + chips - 1, chips) * 2 + core
    partner = z * 2 + (1 - core)
    sources = (x_ref, m_ref)
    targets = (out_ref, mout_ref)

    barrier = pltpu.get_barrier_semaphore()
    for peer in (left, right, partner):
        pl.semaphore_signal(barrier, inc=1, device_id=(peer, peer_col), device_id_type=MESH)
    pl.semaphore_wait(barrier, 3)

    started = []

    def window(refs, origin, piece):
        which, start, width = windows[piece]
        columns = pl.ds(start, width)
        if origin is None:
            return refs[which].at[:, columns]
        return refs[which].at[origin, :, columns]

    def send(origin, piece, peer, from_input):
        copy = pltpu.make_async_remote_copy(
            src_ref=window(sources, None, piece) if from_input else window(targets, origin, piece),
            dst_ref=window(targets, origin, piece),
            send_sem=send_sem.at[len(started)],
            recv_sem=recv_sem.at[origin, piece],
            device_id=(peer, peer_col),
            device_id_type=MESH,
        )
        copy.start()
        started.append(copy)

    def arrive(origin, piece, peer):
        pltpu.make_async_remote_copy(
            src_ref=window(targets, origin, piece),
            dst_ref=window(targets, origin, piece),
            send_sem=send_sem.at[0],
            recv_sem=recv_sem.at[origin, piece],
            device_id=(peer, peer_col),
            device_id_type=MESH,
        ).wait_recv()

    for piece in range(len(windows)):
        send(group, piece, right, True)
        send(group, piece, left, True)
        send(group, piece, partner, True)
    out_ref[group] = x_ref[...]
    mout_ref[group] = m_ref[...]
    forward_hops = chips // 2
    backward_hops = (chips - 1) // 2
    for step in range(1, forward_hops + 1):
        origin = lax.rem(z + chips - step, chips) * 2 + core
        for piece in range(len(windows)):
            arrive(origin, piece, left)
            if step < forward_hops:
                send(origin, piece, right, False)
            send(origin, piece, partner, False)
        if step <= backward_hops:
            origin = lax.rem(z + step, chips) * 2 + core
            for piece in range(len(windows)):
                arrive(origin, piece, right)
                if step < backward_hops:
                    send(origin, piece, left, False)
                send(origin, piece, partner, False)
    for other in range(chips):
        for piece in range(len(windows)):
            arrive(other * 2 + (1 - core), piece, partner)
    for copy in started:
        copy.wait_send()


def send_count(chips):
    forward_hops = chips // 2
    backward_hops = (chips - 1) // 2
    return 3 + 2 * forward_hops - 1 + 2 * backward_hops - 1


def ring_gather(block, meta, group_count):
    chips = group_count // 2
    lanes = block.shape[1] // 128
    windows = tuple(
        (0, lanes * piece // CHUNKS * 128, (lanes * (piece + 1) // CHUNKS - lanes * piece // CHUNKS) * 128)
        for piece in range(CHUNKS)
    ) + ((1, 0, meta.shape[1]),)
    return pl.pallas_call(
        functools.partial(gather_kernel, chips, windows),
        out_shape=(
            jax.ShapeDtypeStruct((group_count,) + block.shape, block.dtype),
            jax.ShapeDtypeStruct((group_count,) + meta.shape, meta.dtype),
        ),
        in_specs=[pl.BlockSpec(memory_space=pltpu.VMEM)] * 2,
        out_specs=(pl.BlockSpec(memory_space=pltpu.VMEM),) * 2,
        scratch_shapes=[
            pltpu.SemaphoreType.DMA((send_count(chips) * len(windows),)),
            pltpu.SemaphoreType.DMA((group_count, len(windows))),
        ],
        compiler_params=pltpu.CompilerParams(collective_id=0, has_side_effects=True),
    )(block, meta)


def scatter_kernel(
    chips, widths, parts_ref, out_ref, early, forward_in, backward_in, forward_out, backward_out,
    send_sem, recv_sem,
):
    group = lax.axis_index("grp")
    peer_col = lax.axis_index("ep")
    z = group // 2
    core = group % 2
    right = lax.rem(z + 1, chips) * 2 + core
    left = lax.rem(z + chips - 1, chips) * 2 + core
    partner = z * 2 + (1 - core)
    forward_hops = chips // 2
    backward_hops = (chips - 1) // 2
    starts = [sum(widths[:piece]) for piece in range(len(widths))]
    pieces = range(len(widths))

    def cols(piece):
        return pl.ds(starts[piece], widths[piece])

    barrier = pltpu.get_barrier_semaphore()
    for peer in (left, right, partner):
        pl.semaphore_signal(barrier, inc=1, device_id=(peer, peer_col), device_id_type=MESH)
    pl.semaphore_wait(barrier, 3)

    started = []

    def copy_of(src, dst, peer, slot, piece, number):
        return pltpu.make_async_remote_copy(
            src_ref=src,
            dst_ref=dst,
            send_sem=send_sem.at[number],
            recv_sem=recv_sem.at[slot, piece],
            device_id=(peer, peer_col),
            device_id_type=MESH,
        )

    def send(src, dst, peer, slot, piece):
        copy = copy_of(src, dst, peer, slot, piece, len(started))
        copy.start()
        started.append(copy)

    def arrive(dst, peer, slot, piece):
        copy_of(dst, dst, peer, slot, piece, 0).wait_recv()

    for other in range(chips):
        for piece in pieces:
            send(
                parts_ref.at[other * 2 + (1 - core), :, cols(piece)],
                early.at[other, :, cols(piece)],
                partner,
                other,
                piece,
            )
    for other in range(chips):
        for piece in pieces:
            arrive(early.at[other, :, cols(piece)], partner, other, piece)

    def chip_part(chip, piece):
        return parts_ref[chip * 2 + core, :, cols(piece)].astype(jnp.float32) + early[
            chip, :, cols(piece)
        ].astype(jnp.float32)

    def hop(step, chip, inbox, outbox, source, dest, first_slot, piece):
        value = chip_part(chip, piece)
        if step > 0:
            arrive(inbox.at[step - 1, :, cols(piece)], source, first_slot + step - 1, piece)
            value = value + inbox[step - 1, :, cols(piece)].astype(jnp.float32)
        outbox[step, :, cols(piece)] = value.astype(outbox.dtype)
        send(outbox.at[step, :, cols(piece)], inbox.at[step, :, cols(piece)], dest, first_slot + step, piece)

    for step in range(forward_hops):
        chip = lax.rem(z + forward_hops - step, chips)
        for piece in pieces:
            hop(step, chip, forward_in, forward_out, left, right, chips, piece)
        if step < backward_hops:
            chip = lax.rem(z + chips - backward_hops + step, chips)
            for piece in pieces:
                hop(step, chip, backward_in, backward_out, right, left, chips + forward_hops, piece)
    for piece in pieces:
        arrive(forward_in.at[forward_hops - 1, :, cols(piece)], left, chips + forward_hops - 1, piece)
        total = chip_part(z, piece) + forward_in[forward_hops - 1, :, cols(piece)].astype(
            jnp.float32
        )
        if backward_hops > 0:
            last = chips + forward_hops + backward_hops - 1
            arrive(backward_in.at[backward_hops - 1, :, cols(piece)], right, last, piece)
            total = total + backward_in[backward_hops - 1, :, cols(piece)].astype(jnp.float32)
        out_ref[:, cols(piece)] = total.astype(out_ref.dtype)
    for copy in started:
        copy.wait_send()


def ring_scatter(parts, group_count):
    chips = group_count // 2
    forward_hops = chips // 2
    backward_hops = (chips - 1) // 2
    block = parts.shape[1:]
    lanes = block[1] // 128
    widths = tuple(
        (lanes * (piece + 1) // CHUNKS - lanes * piece // CHUNKS) * 128 for piece in range(CHUNKS)
    )
    slots = chips + forward_hops + backward_hops
    sends = (chips + forward_hops + backward_hops) * len(widths)
    return pl.pallas_call(
        functools.partial(scatter_kernel, chips, widths),
        out_shape=jax.ShapeDtypeStruct(block, parts.dtype),
        in_specs=[pl.BlockSpec(memory_space=pltpu.VMEM)],
        out_specs=pl.BlockSpec(memory_space=pltpu.VMEM),
        scratch_shapes=[
            pltpu.VMEM((chips,) + block, parts.dtype),
            pltpu.VMEM((forward_hops,) + block, parts.dtype),
            pltpu.VMEM((max(backward_hops, 1),) + block, parts.dtype),
            pltpu.VMEM((forward_hops,) + block, parts.dtype),
            pltpu.VMEM((max(backward_hops, 1),) + block, parts.dtype),
            pltpu.SemaphoreType.DMA((sends,)),
            pltpu.SemaphoreType.DMA((slots, len(widths))),
        ],
        compiler_params=pltpu.CompilerParams(collective_id=1, has_side_effects=True),
    )(parts)


def expert_partial(flat_rows, w_gate, w_up, w_down):
    gate_part = jnp.dot(flat_rows, w_gate[0], preferred_element_type=jnp.float32)
    up_part = jnp.dot(flat_rows, w_up[0], preferred_element_type=jnp.float32)
    hidden = lax.optimization_barrier((jax.nn.silu(gate_part) * up_part).astype(jnp.bfloat16))
    return jnp.dot(hidden, w_down[0], preferred_element_type=jnp.float32)


def per_device(queries, cache, lengths, live_rows, tokens, ids, gates, w_gate, w_up, w_down):
    context = attend(queries, cache, lengths, live_rows[0])
    group_count = lax.axis_size("grp")
    peer_count = lax.axis_size("ep")
    pair_count = peer_count // 2
    row_count = tokens.shape[0]
    feature = tokens.shape[1]
    expert_slots = group_count * CAP
    slot_count = pair_count * expert_slots
    column_rows = group_count * row_count

    meta = jnp.concatenate([ids.astype(jnp.float32), gates], axis=1)
    meta = jnp.pad(meta, ((0, 0), (0, 128 - meta.shape[1])))
    gathered, gathered_meta = ring_gather(tokens, meta, group_count)
    all_tokens = gathered.reshape(column_rows, feature)
    packed = gathered_meta.reshape(column_rows, meta.shape[1])
    all_ids = packed[:, :TOPK].astype(jnp.int32)
    all_gates = packed[:, TOPK : 2 * TOPK]

    my_group = lax.axis_index("grp")
    local = all_ids - pair_count * my_group
    experts = jnp.arange(pair_count, dtype=jnp.int32)
    pick_hot = (local[:, :, None] == experts[None, None, :]).astype(jnp.int32)
    token_hot = jnp.sum(pick_hot, axis=1)
    gate_of = jnp.sum(all_gates[:, :, None] * pick_hot.astype(jnp.float32), axis=1)
    blocks = token_hot.reshape(group_count, row_count, pair_count)
    earlier = (jnp.cumsum(blocks, axis=1) - blocks).reshape(column_rows, pair_count)
    source = jnp.arange(column_rows, dtype=jnp.int32)[:, None] // row_count
    slot_id = experts[None, :] * expert_slots + source * CAP + earlier
    slot_id = jnp.where(token_hot > 0, slot_id, slot_count)
    slots = jnp.arange(slot_count, dtype=jnp.int32)
    match = slot_id[:, :, None] == slots[None, None, :]
    dispatch = jnp.any(match, axis=1).T.astype(jnp.bfloat16)
    combine = jnp.sum(jnp.where(match, gate_of[:, :, None], 0.0), axis=1)

    outgoing = jnp.dot(dispatch, all_tokens, preferred_element_type=jnp.float32).astype(
        jnp.bfloat16
    )
    doubled = jnp.repeat(outgoing.reshape(pair_count, expert_slots, feature), 2, axis=0)
    arriving = lax.all_to_all(doubled, "ep", split_axis=0, concat_axis=0, tiled=True)
    partials = expert_partial(
        arriving.reshape(peer_count * expert_slots, feature), w_gate, w_up, w_down
    ).astype(jnp.bfloat16)
    returned = lax.all_to_all(
        partials.reshape(peer_count, expert_slots, feature),
        "ep",
        split_axis=0,
        concat_axis=0,
        tiled=True,
    )
    expert_out = (
        returned.reshape(pair_count, 2, expert_slots, feature)
        .astype(jnp.float32)
        .sum(axis=1)
        .astype(jnp.bfloat16)
        .reshape(slot_count, feature)
    )
    weight_high = combine.astype(jnp.bfloat16)
    weight_low = (combine - weight_high.astype(jnp.float32)).astype(jnp.bfloat16)
    column_mixed = jnp.dot(
        jnp.concatenate([weight_high, weight_low], axis=1),
        jnp.concatenate([expert_out, expert_out], axis=0),
        preferred_element_type=jnp.float32,
    )
    mixed = ring_scatter(
        column_mixed.astype(jnp.bfloat16).reshape(group_count, row_count, feature), group_count
    )
    return (context, mixed)


def solution(mesh):
    in_specs = (
        P(("grp", "ep"), None, None),
        P(("grp", "ep"), None, None),
        P(("grp", "ep")),
        P(("grp", "ep")),
        P(("grp", "ep"), None),
        P(("grp", "ep"), None),
        P(("grp", "ep"), None),
        P(("grp", "ep"), None, None),
        P(("grp", "ep"), None, None),
        P(("grp", "ep"), None, None),
    )
    out_specs = (P(("grp", "ep"), None, None), P(("grp", "ep"), None))
    return jax.shard_map(
        per_device, mesh=mesh, in_specs=in_specs, out_specs=out_specs, check_vma=False
    )
```
